32 devices in a mesh: dp: 8 (over z, y), seq: 4 (over x, core).
Axes of the slice: x: 2, y: 2, z: 4, core: 2. Of those that a mesh axis runs over, the one named last changes fastest.
Arguments:
- byte_ids: int32 [24, 2048], P('dp', 'seq'), may hold values from 0 to 258
- lengths: int32 [24], P('dp'), may hold values from 128 to 2048, as said below
- teacher: float32 [24, 1024, 768], P('dp', 'seq'), may hold values from -6 to 6
- embed_table: bfloat16 [259, 768], P(None, ('dp', 'seq')), may hold values from -6 to 6
- conv_weight: bfloat16 [4, 768], P(None, ('dp', 'seq')), may hold values from -3 to 3
- score_weight: bfloat16 [768], P(('dp', 'seq')), may hold values from -0.625 to 0.625
- attn_gain: bfloat16 [768], P(('dp', 'seq')), may hold values from 0.5 to 1.5
- rel_bias: bfloat16 [32, 12], replicated, may hold values from -6 to 6
- query_weight: bfloat16 [768, 768], P(('dp', 'seq')), may hold values from -0.0546875 to 0.0546875
- key_weight: bfloat16 [768, 768], P(('dp', 'seq')), may hold values from -0.21875 to 0.21875
- value_weight: bfloat16 [768, 768], P(('dp', 'seq')), may hold values from -0.21875 to 0.21875
- output_weight: bfloat16 [768, 768], P(('dp', 'seq')), may hold values from -0.875 to 0.875
- ffn_gain: bfloat16 [768], P(('dp', 'seq')), may hold values from 0.5 to 1.5
- gate_weight: bfloat16 [768, 2048], P(('dp', 'seq')), may hold values from -0.21875 to 0.21875
- up_weight: bfloat16 [768, 2048], P(('dp', 'seq')), may hold values from -0.21875 to 0.21875
- down_weight: bfloat16 [2048, 768], P(('dp', 'seq')), may hold values from -0.125 to 0.125
Outputs:
- layer_out: float32 [24, 1024, 768], P('dp', 'seq')
- loss_value: float32 [], replicated
- embed_grad: float32 [259, 768], P(None, ('dp', 'seq'))
- conv_grad: float32 [4, 768], P(None, ('dp', 'seq'))
- score_grad: float32 [768], P(('dp', 'seq'))
- attn_gain_grad: float32 [768], P(('dp', 'seq'))
- bias_grad: float32 [32, 12], replicated
- query_grad: float32 [768, 768], P(('dp', 'seq'))
- key_grad: float32 [768, 768], P(('dp', 'seq'))
- value_grad: float32 [768, 768], P(('dp', 'seq'))
- output_grad: float32 [768, 768], P(('dp', 'seq'))
- ffn_gain_grad: float32 [768], P(('dp', 'seq'))
- gate_grad: float32 [768, 2048], P(('dp', 'seq'))
- up_grad: float32 [768, 2048], P(('dp', 'seq'))
- down_grad: float32 [2048, 768], P(('dp', 'seq'))
The draws below stay inside these ranges and needn't reach their ends.
Inputs may be any that keep to these rules, and one draw needn't show every extreme that they name: `lengths`: valid bytes of each sequence; in every draw some sequence has all 2048 bytes valid.
All inputs are finite; a program needn't handle non-finite values.
Results may differ from the reference program's by a relative error of at most 0.038.
Values may be sent and summed in bfloat16 or wider, within the bound.
No kernel may reach another device: no remote copies, remote signals or barrier semaphores. Data moves between devices by JAX's collectives and lax.ppermute only.
A program may use at most 256 MiB of HBM per device.

```python
import jax
import jax.numpy as jnp
from jax import lax

D = 768
HEADS = 12
HEAD_DIM = 64
FF = 2048
VOCAB = 259
KERNEL = 4
BLOCKS = 4
BUCKETS = 32
SEQ_DEV = 3
LENGTH = 2048
SEQ_TOKENS = 1024
BATCH = 24


def draw_lengths(key, part):
    position = jnp.arange(BATCH, dtype=jnp.int32)
    lowest = LENGTH // 8
    target = lowest + position * (LENGTH - lowest) // max(BATCH - 1, 1)
    jitter = jax.random.randint(jax.random.fold_in(key, 11), (BATCH,), -(LENGTH // 16), LENGTH // 16 + 1)
    drawn_len = jnp.clip(target + jitter, LENGTH // 16, LENGTH)
    return jnp.where(position == BATCH - 1, LENGTH, drawn_len).astype(jnp.int32)


def place_ends(values, rng, smallest, high):
    place = [jax.random.randint(jax.random.fold_in(rng, axis), (), 0, length) for axis, length in enumerate(values.shape)]
    widest = values.shape.index(max(values.shape))
    neighbour = place[:widest] + [(place[widest] + 1) % values.shape[widest]] + place[widest + 1:]
    return values.at[tuple(place)].set(smallest).at[tuple(neighbour)].set(high)


def steps_of(own_key, extent, pieces, low, largest):
    loudness, own = 1.0, jax.random.fold_in(own_key, 6)
    for axis_at, shards_of in pieces:
        draws = jnp.exp(jax.random.uniform(jax.random.fold_in(own, axis_at), (shards_of,), jnp.float32, low / len(pieces), largest / len(pieces)))
        loudness = loudness * jnp.repeat(draws, extent[axis_at] // shards_of).reshape([-1 if axis == axis_at else 1 for axis in range(len(extent))])
    return loudness


def gaussian(rng, dims, spread, most, shards=(), kind=jnp.bfloat16):
    result = spread * jax.random.normal(rng, dims, jnp.float32)
    if shards:
        result = result * steps_of(rng, dims, shards, -0.22, 0.18)
    return jnp.clip(result, -most, most).astype(kind)


def setup_inputs(seed: int = 0) -> dict:
    seeds = jax.random.split(jax.random.key(seed), 17)
    byte_ids = place_ends(jax.random.randint(seeds[0], (BATCH, LENGTH), 0, VOCAB), jax.random.fold_in(seeds[0], 1), 0, VOCAB - 1).astype(jnp.int32)
    lengths = draw_lengths(jax.random.fold_in(seeds[16], 71), 0)
    teacher = gaussian(seeds[2], (BATCH, SEQ_TOKENS, D), 1.0, 6.0, ((0, 8), (1, 4)), jnp.float32)
    embed_table = gaussian(seeds[3], (VOCAB, D), 1.0, 6.0, ((1, 32),))
    conv_weight = gaussian(seeds[4], (KERNEL, D), KERNEL ** -0.5, 3.0, ((1, 32),))
    score_weight = gaussian(seeds[5], (D,), (D // 9) ** -0.5, 0.625, ((0, 32),))
    attn_gain = jnp.clip(1.0 + 0.1 * jax.random.normal(seeds[6], (D,), jnp.float32), 0.5, 1.5).astype(jnp.bfloat16)
    rel_bias = gaussian(seeds[7], (BUCKETS, HEADS), 1.0, 6.0)
    query_weight = gaussian(seeds[8], (D, D), (D * 16) ** -0.5, 0.0546875, ((0, 32),))
    key_weight = gaussian(seeds[9], (D, D), D ** -0.5, 0.21875, ((0, 32),))
    value_weight = gaussian(seeds[10], (D, D), D ** -0.5, 0.21875, ((0, 32),))
    output_weight = gaussian(seeds[11], (D, D), (D // 16) ** -0.5, 0.875, ((0, 32),))
    ffn_gain = jnp.clip(1.0 + 0.1 * jax.random.normal(seeds[12], (D,), jnp.float32), 0.5, 1.5).astype(jnp.bfloat16)
    gate_weight = gaussian(seeds[13], (D, FF), D ** -0.5, 0.21875, ((0, 32),))
    up_weight = gaussian(seeds[14], (D, FF), D ** -0.5, 0.21875, ((0, 32),))
    down_weight = gaussian(seeds[15], (FF, D), FF ** -0.5, 0.125, ((0, 32),))
    return {"byte_ids": byte_ids, "lengths": lengths, "teacher": teacher, "embed_table": embed_table, "conv_weight": conv_weight, "score_weight": score_weight, "attn_gain": attn_gain, "rel_bias": rel_bias, "query_weight": query_weight, "key_weight": key_weight, "value_weight": value_weight, "output_weight": output_weight, "ffn_gain": ffn_gain, "gate_weight": gate_weight, "up_weight": up_weight, "down_weight": down_weight}


@jax.custom_vjp
def low(v):
    return lax.optimization_barrier(v.astype(jnp.bfloat16)).astype(jnp.float32)

@jax.custom_vjp
def low_back(v):
    return v

def low_keep(v):
    return (low(v), None)

def low_pass(kept, grad):
    return (grad,)

def back_keep(v):
    return (v, None)

def back_low(kept, grad):
    return (low(grad),)
low.defvjp(low_keep, low_pass)
low_back.defvjp(back_keep, back_low)
epsilon = 1e-06
thresholds = (12, 16, 23, 32, 46, 64, 91)
masked_score = -1000000000.0

def bucket_of(relative):
    distance = jnp.abs(relative)
    far_bucket = 8 + sum(((distance >= border).astype(jnp.int32) for border in thresholds))
    return jnp.where(relative > 0, 16, 0).astype(jnp.int32) + jnp.where(distance < 8, distance, far_bucket).astype(jnp.int32)

def rms_norm(values, gain_vec):
    return values * lax.rsqrt(lax.optimization_barrier(jnp.mean(values * values, axis=-1, keepdims=True)) + epsilon) * gain_vec

def matmul(first_op, second_op):
    return jnp.matmul(first_op, second_op, precision=lax.Precision.HIGHEST)

def encode_group(params, bias_heads, ids_group, lens_group, teacher_group):
    embed_table, conv_weight, score_weight, attn_gain, query_weight, key_weight, value_weight, output_weight, ffn_gain, gate_weight, up_weight, down_weight = params
    group_size = ids_group.shape[0]
    embedded = embed_table[ids_group]
    padded = jnp.pad(embedded, ((0, 0), (1, 2), (0, 0)))
    conv_out = sum((conv_weight[kernel_tap] * padded[:, kernel_tap:kernel_tap + LENGTH] for kernel_tap in range(KERNEL)))
    candidates = []
    for block_size in range(1, BLOCKS + 1):
        rounded = block_size * -(-LENGTH // block_size)
        extended = jnp.pad(conv_out, ((0, 0), (0, rounded - LENGTH), (0, 0)))
        pooled_mean = lax.optimization_barrier(jnp.mean(extended.reshape(group_size, rounded // block_size, block_size, D), axis=2))
        candidates.append(jnp.repeat(pooled_mean, block_size, axis=1)[:, :LENGTH])
    stacked = jnp.stack(candidates, axis=2)
    block_scores = jnp.einsum('glbd,d->glb', stacked, score_weight, precision=lax.Precision.HIGHEST)
    block_probs = jax.nn.softmax(block_scores, axis=-1)
    mixture = jnp.einsum('glb,glbd->gld', block_probs, stacked, precision=lax.Precision.HIGHEST)
    residual_in = lax.optimization_barrier(jnp.mean(mixture.reshape(group_size, SEQ_TOKENS, 2, D), axis=2))
    normed = low(rms_norm(residual_in, attn_gain))
    queries = low_back(low(matmul(normed, query_weight))).reshape(group_size, SEQ_TOKENS, HEADS, HEAD_DIM)
    key_rows = low_back(low(matmul(normed, key_weight))).reshape(group_size, SEQ_TOKENS, HEADS, HEAD_DIM)
    value_rows = low_back(low(matmul(normed, value_weight))).reshape(group_size, SEQ_TOKENS, HEADS, HEAD_DIM)
    key_live = 2 * jnp.arange(SEQ_TOKENS, dtype=jnp.int32)[None, :] < lens_group[:, None]
    products = low_back(jnp.einsum('gqhd,gkhd->ghqk', queries, key_rows, precision=lax.Precision.HIGHEST))
    scores = jnp.where(key_live[:, None, None, :], products + bias_heads[None], masked_score)
    reduced_weights = low(jax.nn.softmax(scores, axis=-1))
    attended = jnp.einsum('ghqk,gkhd->gqhd', reduced_weights, value_rows, precision=lax.Precision.HIGHEST)
    attended = low_back(low(attended)).reshape(group_size, SEQ_TOKENS, D)
    attn_branch = low_back(matmul(attended, output_weight))
    after_attn = residual_in + attn_branch
    ffn_in = low(rms_norm(after_attn, ffn_gain))
    gate_pre = low_back(matmul(ffn_in, gate_weight))
    up_pre = low_back(matmul(ffn_in, up_weight))
    hidden = low(jax.nn.gelu(gate_pre, approximate=True) * up_pre)
    ffn_branch = low_back(matmul(hidden, down_weight))
    block_out = after_attn + ffn_branch
    token_live = key_live.astype(jnp.float32)
    error_sum = jnp.sum(token_live[:, :, None] * (block_out - teacher_group) ** 2)
    return (block_out, error_sum)

def reference(byte_ids, lengths, teacher, embed_table, conv_weight, score_weight, attn_gain, rel_bias, query_weight, key_weight, value_weight, output_weight, ffn_gain, gate_weight, up_weight, down_weight):
    params = tuple((weight_arr.astype(jnp.float32) for weight_arr in (embed_table, conv_weight, score_weight, attn_gain, query_weight, key_weight, value_weight, output_weight, ffn_gain, gate_weight, up_weight, down_weight)))
    table_f = rel_bias.astype(jnp.float32)
    positions = jnp.arange(SEQ_TOKENS, dtype=jnp.int32)
    buckets = bucket_of(positions[None, :] - positions[:, None])
    live_count = jnp.sum((2 * positions[None, :] < lengths[:, None]).astype(jnp.float32))
    groups = BATCH // SEQ_DEV
    ids_grouped = byte_ids.reshape(groups, SEQ_DEV, LENGTH)
    lens_grouped = lengths.reshape(groups, SEQ_DEV)
    teacher_grouped = teacher.reshape(groups, SEQ_DEV, SEQ_TOKENS, D)
    group_fn = jax.checkpoint(encode_group)

    def total_loss(weights_all, bias_table):
        bias_heads = jnp.transpose(bias_table[buckets], (2, 0, 1))

        def scan_step(carried, batch_slice):
            outputs, errors = group_fn(weights_all, bias_heads, *batch_slice)
            return (carried + errors, outputs)
        error_total, outputs = lax.scan(scan_step, jnp.zeros((), jnp.float32), (ids_grouped, lens_grouped, teacher_grouped))
        return (error_total / live_count, outputs.reshape(BATCH, SEQ_TOKENS, D))
    loss_value, pullback, layer_out = jax.vjp(total_loss, params, table_f, has_aux=True)
    weight_grads, bias_grad = pullback(jnp.ones((), jnp.float32))
    return (layer_out, loss_value, weight_grads[0], weight_grads[1], weight_grads[2], weight_grads[3], bias_grad, weight_grads[4], weight_grads[5], weight_grads[6], weight_grads[7], weight_grads[8], weight_grads[9], weight_grads[10], weight_grads[11])
```

```python
from functools import partial

import jax
import jax.numpy as jnp
from jax import lax
from jax.experimental import pallas as pl
from jax.experimental.pallas import tpu as pltpu
from jax.sharding import PartitionSpec as P

D = 768
HEADS = 12
HEAD_DIM = 64
VOCAB = 259
BUCKETS = 32
TABLE = 384
PAIRS = HEADS // 2
SIDE = 128
ONES = 16
LEFT = 20
RIGHT = 21
HALF = 128

epsilon = 1e-06
thresholds = (12, 16, 23, 32, 46, 64, 91)
masked_score = -1000000000.0
highest = lax.Precision.HIGHEST
bf16 = jnp.bfloat16
f32 = jnp.float32
both = ("dp", "seq")


def nt(a, b):
    return lax.dot_general(a, b, (((1,), (1,)), ((), ())), preferred_element_type=f32)


def nn(a, b):
    return lax.dot_general(a, b, (((1,), (0,)), ((), ())), preferred_element_type=f32)


def bucket_of(relative):
    distance = jnp.abs(relative)
    far_bucket = 8 + sum(((distance >= border).astype(jnp.int32) for border in thresholds))
    return jnp.where(relative > 0, 16, 0).astype(jnp.int32) + jnp.where(
        distance < 8, distance, far_bucket
    )


def hot_buckets(relative):
    return (bucket_of(relative)[..., None] == jnp.arange(BUCKETS, dtype=jnp.int32)).astype(f32)


def swap(value, axis, bit):
    peers = lax.axis_size(axis)
    return lax.ppermute(value, axis, [(i, i ^ bit) for i in range(peers)])


def axis_bits(axis):
    bits, bit = [], lax.axis_size(axis) // 2
    while bit:
        bits.append((axis, bit))
        bit //= 2
    return bits


def my_bit(axis, bit):
    return (lax.axis_index(axis) // bit) % 2


def gather_stage(value, axis, bit, position):
    other = swap(value, axis, bit)
    upper = my_bit(axis, bit) == 1
    return jnp.stack(
        [jnp.where(upper, other, value), jnp.where(upper, value, other)], axis=position
    )


def gather_rows(value):
    rows, cols = value.shape
    for position, (axis, bit) in enumerate(axis_bits("dp") + axis_bits("seq")):
        value = gather_stage(value, axis, bit, position)
    return value.reshape(-1, cols)


def scatter_rows(total, order=None):
    rows, cols = total.shape
    stages = axis_bits("dp") + axis_bits("seq")
    total = total.reshape([2] * len(stages) + [rows >> len(stages), cols])
    left = list(stages)
    for axis, bit in order or stages[::-1]:
        position = left.index((axis, bit))
        mine = my_bit(axis, bit)
        keep = lax.dynamic_index_in_dim(total, mine, position, keepdims=False)
        send = lax.dynamic_index_in_dim(total, 1 - mine, position, keepdims=False)
        total = keep.astype(f32) + swap(send.astype(bf16), axis, bit).astype(f32)
        left.remove((axis, bit))
    return total


def up(x):
    return pltpu.roll(x, x.shape[0] - 1, 0)


def down(x):
    return pltpu.roll(x, 1, 0)


def pool_chunk(e, taps, live, m0, m1):
    w0, w1, w2, w3 = taps
    e0, e1, e2, e3 = e
    e3d, e0u, e1u = down(e3), up(e0), up(e1)
    c0 = (w0 * e3d + w1 * e0 + w2 * e1 + w3 * e2) * live[0]
    c1 = (w0 * e0 + w1 * e1 + w2 * e2 + w3 * e3) * live[1]
    c2 = (w0 * e1 + w1 * e2 + w2 * e3 + w3 * e0u) * live[2]
    c3 = (w0 * e2 + w1 * e3 + w2 * e0u + w3 * e1u) * live[3]
    return (c0, c1, c2, c3), triples((c0, c1, c2, c3), m0, m1)


def triples(c, m0, m1):
    c0, c1, c2, c3 = c
    p01, p23 = c0 + c1, c2 + c3
    t0, t1, t2, t3 = down(c3) + p01, p01 + c2, c1 + p23, p23 + up(c0)
    before, after = (down(t3), t0, t1, t2), (t1, t2, t3, up(t0))
    here = (t0, t1, t2, t3)
    return tuple(
        jnp.where(m0[k], after[k], jnp.where(m1[k], here[k], before[k])) for k in range(4)
    )


def position_marks(first, rows, total_bytes):
    row = lax.broadcasted_iota(jnp.int32, (rows, 128), 0)
    live, m0, m1 = [], [], []
    for k in range(4):
        pos = first + 4 * (row - 8) + k
        live.append(((pos >= 0) & (pos < total_bytes)).astype(f32))
        shifted = (pos + 48).astype(f32)
        third = jnp.floor((shifted + 0.5) * (1.0 / 3.0))
        rest = shifted - 3.0 * third
        m0.append(rest < 0.5)
        m1.append((rest > 0.5) & (rest < 1.5))
    return live, m0, m1


def lane_chunk(i):
    return pl.ds(pl.multiple_of(i * 128, 128), 128)


def embed_bytes(ids, table, emb):
    lane = lax.broadcasted_iota(jnp.int32, (ids.shape[0], TABLE), 1)
    emb[...] = nt((ids == lane).astype(bf16), table)


def small_rows(table, small):
    lane = lax.broadcasted_iota(jnp.int32, (8, TABLE), 1)
    row = lax.broadcasted_iota(jnp.int32, (8, TABLE), 0)
    small[...] = nt((lane == row + VOCAB).astype(bf16), table)


def block_probs(emb, small, cands, accs, live, m0, m1, rows):
    accs[...] = jnp.zeros_like(accs)

    def step(i, _):
        chunk = lane_chunk(i)
        taps = [small[k : k + 1, chunk] for k in range(4)]
        scorer = small[4:5, chunk]
        e = [emb[k * rows : (k + 1) * rows, chunk] for k in range(4)]
        c, h = pool_chunk(e, taps, live, m0, m1)
        p01, p23 = c[0] + c[1], c[2] + c[3]
        for k in range(4):
            cands[k, :, chunk] = c[k]
            cands[4 + k, :, chunk] = h[k]
            accs[k] += c[k] * scorer
            accs[4 + k] += h[k] * scorer
        accs[8] += p01 * scorer
        accs[9] += p23 * scorer
        return 0

    lax.fori_loop(0, D // 128, step, 0)
    total = [jnp.sum(accs[k], axis=-1, keepdims=True) for k in range(10)]
    quad = 0.25 * (total[8] + total[9])
    probs = []
    for k in range(4):
        scores = (total[k], 0.5 * total[8 + k // 2], total[4 + k] * (1.0 / 3.0), quad)
        top = jnp.maximum(jnp.maximum(scores[0], scores[1]), jnp.maximum(scores[2], scores[3]))
        powers = [jnp.exp(score - top) for score in scores]
        norm = 1.0 / (powers[0] + powers[1] + powers[2] + powers[3])
        probs.append([power * norm for power in powers])
    return probs


def pool_kernel(first_ref, ids, table, resid, normed, emb, small, cands, accs, tokens, *, rows, total_bytes):
    first = first_ref[pl.program_id(0) % 2]
    embed_bytes(ids[...], table[...], emb)
    small_rows(table[...], small)
    live, m0, m1 = position_marks(first, rows, total_bytes)
    probs = block_probs(emb, small, cands, accs, live, m0, m1, rows)
    own = rows - 16

    def step(i, square):
        chunk = lane_chunk(i)
        c = [cands[k, :, chunk] for k in range(4)]
        h = [cands[4 + k, :, chunk] for k in range(4)]
        p01, p23 = c[0] + c[1], c[2] + c[3]
        quad = p01 + p23
        for half, pair in ((0, p01), (1, p23)):
            a, b = probs[2 * half], probs[2 * half + 1]
            token = 0.5 * (
                a[0] * c[2 * half]
                + b[0] * c[2 * half + 1]
                + ((a[1] + b[1]) * 0.5) * pair
                + (a[2] * h[2 * half] + b[2] * h[2 * half + 1]) * (1.0 / 3.0)
                + ((a[3] + b[3]) * 0.25) * quad
            )
            tokens[i, pl.ds(half, own, stride=2), :] = token[8 : 8 + own]
        values = tokens[i]
        resid[:, chunk] = values
        return square + values * values

    square = lax.fori_loop(0, D // 128, step, jnp.zeros((2 * own, 128), f32))
    scale = lax.rsqrt(jnp.sum(square, axis=-1, keepdims=True) * (1.0 / D) + epsilon)
    normed[...] = (resid[...] * scale * small[5:6, :]).astype(bf16)


def pool(first, ids, table, total_bytes):
    count, wide, _ = ids.shape
    rows = wide // 4
    tokens = 2 * (rows - 16)
    return pl.pallas_call(
        partial(pool_kernel, rows=rows, total_bytes=total_bytes),
        grid=(count,),
        in_specs=[
            pl.BlockSpec(memory_space=pltpu.SMEM),
            pl.BlockSpec((None, wide, 1), lambda i: (i, 0, 0)),
            pl.BlockSpec((D, TABLE), lambda i: (0, 0)),
        ],
        out_specs=[
            pl.BlockSpec((None, tokens, D), lambda i: (i, 0, 0)),
            pl.BlockSpec((None, tokens, D), lambda i: (i, 0, 0)),
        ],
        out_shape=[
            jax.ShapeDtypeStruct((count, tokens, D), f32),
            jax.ShapeDtypeStruct((count, tokens, D), bf16),
        ],
        scratch_shapes=[
            pltpu.VMEM((wide, D), f32),
            pltpu.VMEM((8, D), f32),
            pltpu.VMEM((8, rows, D), f32),
            pltpu.VMEM((10, rows, 128), f32),
            pltpu.VMEM((D // 128, tokens, 128), f32),
        ],
        cost_estimate=pl.CostEstimate(flops=count * 8_000_000_000, bytes_accessed=4_000_000, transcendentals=0),
        name="pool",
    )(first, ids, table)


def pool_back_kernel(
    first_ref, ids, ids_row, table, grad_normed, resid, after, embed_grad, small_grad,
    emb, small, cands, accs, tokens, pulls, emb_grad, *, rows, total_bytes,
):
    first = first_ref[0]
    own = rows - 16
    chunks = D // 128

    @pl.when(pl.program_id(0) == 0)
    def _():
        embed_grad[...] = jnp.zeros_like(embed_grad)
        small_grad[...] = jnp.zeros_like(small_grad)

    embed_bytes(ids[...], table[...], emb)
    small_rows(table[...], small)
    live, m0, m1 = position_marks(first, rows, total_bytes)

    x, gn = resid[...], grad_normed[...]
    scale = lax.rsqrt(jnp.mean(x * x, axis=-1, keepdims=True) + epsilon)
    gain = small[5:6, :]
    small_grad[5:6, :] += jnp.sum(gn * x * scale, axis=0, keepdims=True)
    gg = gain * gn
    inner = jnp.mean(gg * x, axis=-1, keepdims=True)
    total = after[...] + scale * gg - x * (scale * scale * scale * inner)
    for i in range(chunks):
        tokens[i] = total[:, i * 128 : (i + 1) * 128]

    probs = block_probs(emb, small, cands, accs, live, m0, m1, rows)
    accs[...] = jnp.zeros_like(accs)
    pulls[:, 0:8, :] = jnp.zeros((2, 8, D), f32)
    pulls[:, rows - 8 : rows, :] = jnp.zeros((2, 8, D), f32)

    def dots(i, _):
        chunk = lane_chunk(i)
        for half in range(2):
            pulls[half, 8 : 8 + own, chunk] = 0.5 * tokens[i, pl.ds(half, own, stride=2), :]
        g = [pulls[half, :, chunk] for half in range(2)]
        c = [cands[k, :, chunk] for k in range(4)]
        h = [cands[4 + k, :, chunk] for k in range(4)]
        p01, p23 = c[0] + c[1], c[2] + c[3]
        quad = p01 + p23
        for k in range(4):
            accs[k] += g[k // 2] * c[k]
            accs[4 + k] += g[k // 2] * h[k]
        accs[8] += g[0] * p01
        accs[9] += g[1] * p23
        accs[10] += g[0] * quad
        accs[11] += g[1] * quad
        return 0

    lax.fori_loop(0, chunks, dots, 0)
    total = [jnp.sum(accs[k], axis=-1, keepdims=True) for k in range(12)]
    pulled = []
    for k in range(4):
        gd = (
            total[k],
            0.5 * total[8 + k // 2],
            total[4 + k] * (1.0 / 3.0),
            0.25 * total[10 + k // 2],
        )
        p = probs[k]
        mean = p[0] * gd[0] + p[1] * gd[1] + p[2] * gd[2] + p[3] * gd[3]
        pulled.append([p[b] * (gd[b] - mean) for b in range(4)])
    pair_p = [0.5 * (probs[0][1] + probs[1][1]), 0.5 * (probs[2][1] + probs[3][1])]
    pair_s = [0.5 * (pulled[0][1] + pulled[1][1]), 0.5 * (pulled[2][1] + pulled[3][1])]
    quad_p = [0.25 * (probs[0][3] + probs[1][3]), 0.25 * (probs[2][3] + probs[3][3])]
    quad_s = 0.25 * (pulled[0][3] + pulled[1][3] + pulled[2][3] + pulled[3][3])
    third_s = [pulled[k][2] * (1.0 / 3.0) for k in range(4)]

    def back(i, _):
        chunk = lane_chunk(i)
        w0, w1, w2, w3 = [small[k : k + 1, chunk] for k in range(4)]
        scorer = small[4:5, chunk]
        g = [pulls[half, :, chunk] for half in range(2)]
        c = [cands[k, :, chunk] for k in range(4)]
        h = [cands[4 + k, :, chunk] for k in range(4)]
        e0, e1, e2, e3 = [emb[k * rows : (k + 1) * rows, chunk] for k in range(4)]
        p01, p23 = c[0] + c[1], c[2] + c[3]
        quad = p01 + p23
        score = pair_s[0] * p01 + pair_s[1] * p23 + quad_s * quad
        for k in range(4):
            score += pulled[k][0] * c[k] + third_s[k] * h[k]
        small_grad[4:5, chunk] += jnp.sum(score, axis=0, keepdims=True)
        spread = triples(
            [probs[k][2] * g[k // 2] + pulled[k][2] * scorer for k in range(4)], m0, m1
        )
        wide_quad = quad_p[0] * g[0] + quad_p[1] * g[1] + quad_s * scorer
        wide_pair = [pair_p[half] * g[half] + pair_s[half] * scorer + wide_quad for half in range(2)]
        gc0, gc1, gc2, gc3 = [
            (
                probs[k][0] * g[k // 2]
                + pulled[k][0] * scorer
                + wide_pair[k // 2]
                + spread[k] * (1.0 / 3.0)
            )
            * live[k]
            for k in range(4)
        ]
        e3d, e0u, e1u = down(e3), up(e0), up(e1)
        taps = (
            gc0 * e3d + gc1 * e0 + gc2 * e1 + gc3 * e2,
            gc0 * e0 + gc1 * e1 + gc2 * e2 + gc3 * e3,
            gc0 * e1 + gc1 * e2 + gc2 * e3 + gc3 * e0u,
            gc0 * e2 + gc1 * e3 + gc2 * e0u + gc3 * e1u,
        )
        for k in range(4):
            small_grad[k : k + 1, chunk] += jnp.sum(taps[k], axis=0, keepdims=True)
        gc3d, gc2d, gc0u = down(gc3), down(gc2), up(gc0)
        grads = (
            w0 * gc1 + w1 * gc0 + w2 * gc3d + w3 * gc2d,
            w0 * gc2 + w1 * gc1 + w2 * gc0 + w3 * gc3d,
            w0 * gc3 + w1 * gc2 + w2 * gc1 + w3 * gc0,
            w0 * gc0u + w1 * gc3 + w2 * gc2 + w3 * gc1,
        )
        for k in range(4):
            emb_grad[k * rows : (k + 1) * rows, chunk] = grads[k].astype(bf16)
        return 0

    lax.fori_loop(0, chunks, back, 0)
    row = lax.broadcasted_iota(jnp.int32, (TABLE, 4 * rows), 0)
    embed_grad[...] += nn((ids_row[...] == row).astype(bf16), emb_grad[...])


def pool_back(first, ids, ids_row, table, grad_normed, resid, after, total_bytes):
    count, wide, _ = ids.shape
    rows = wide // 4
    tokens = 2 * (rows - 16)
    token_spec = pl.BlockSpec((None, tokens, D), lambda i: (i, 0, 0))
    return pl.pallas_call(
        partial(pool_back_kernel, rows=rows, total_bytes=total_bytes),
        grid=(count,),
        in_specs=[
            pl.BlockSpec(memory_space=pltpu.SMEM),
            pl.BlockSpec((None, wide, 1), lambda i: (i, 0, 0)),
            pl.BlockSpec((None, 1, wide), lambda i: (i, 0, 0)),
            pl.BlockSpec((D, TABLE), lambda i: (0, 0)),
            token_spec,
            token_spec,
            token_spec,
        ],
        out_specs=[
            pl.BlockSpec((TABLE, D), lambda i: (0, 0)),
            pl.BlockSpec((8, D), lambda i: (0, 0)),
        ],
        out_shape=[
            jax.ShapeDtypeStruct((TABLE, D), f32),
            jax.ShapeDtypeStruct((8, D), f32),
        ],
        scratch_shapes=[
            pltpu.VMEM((wide, D), f32),
            pltpu.VMEM((8, D), f32),
            pltpu.VMEM((8, rows, D), f32),
            pltpu.VMEM((12, rows, 128), f32),
            pltpu.VMEM((D // 128, tokens, 128), f32),
            pltpu.VMEM((2, rows, D), f32),
            pltpu.VMEM((wide, D), bf16),
        ],
        cost_estimate=pl.CostEstimate(flops=count * 20_000_000_000, bytes_accessed=8_000_000, transcendentals=0),
        name="pool_back",
    )(first, ids, ids_row, table, grad_normed, resid, after)


def bias_kernel(rank_ref, far_ref, diag, tile, turned, *, queries, near, parts):
    head = pl.program_id(0)
    rank = rank_ref[0]
    full = jnp.broadcast_to(diag[...], (queries, diag.shape[-1]))
    rolled = pltpu.roll(full, 0, 1, stride=1, stride_axis=0)[:, :near]
    lane = lax.broadcasted_iota(jnp.int32, (queries, near), 1)
    rolled = jnp.where((lane < HALF) & (rank == 0), far_ref[head, 1], rolled)
    rolled = jnp.where((lane >= near - HALF) & (rank == parts - 1), far_ref[head, 0], rolled)
    tile[...] = rolled.astype(bf16)
    turned[...] = rolled.T.astype(bf16)


def near_bias(rank, far, diag, queries, near, parts):
    return pl.pallas_call(
        partial(bias_kernel, queries=queries, near=near, parts=parts),
        grid=(HEADS,),
        in_specs=[
            pl.BlockSpec(memory_space=pltpu.SMEM),
            pl.BlockSpec(memory_space=pltpu.SMEM),
            pl.BlockSpec((None, 1, diag.shape[-1]), lambda i: (i, 0, 0)),
        ],
        out_specs=[
            pl.BlockSpec((None, queries, near), lambda i: (i, 0, 0)),
            pl.BlockSpec((None, near, queries), lambda i: (i, 0, 0)),
        ],
        out_shape=[
            jax.ShapeDtypeStruct((HEADS, queries, near), bf16),
            jax.ShapeDtypeStruct((HEADS, near, queries), bf16),
        ],
        cost_estimate=pl.CostEstimate(flops=4_000_000_000, bytes_accessed=6_300_000, transcendentals=0),
        name="near_bias",
    )(rank, far, diag)


def row_offset(rank, step, blocks):
    half = lax.rem(2 * rank - 1 + step + 2 * blocks, 2 * blocks)
    apart = jnp.bitwise_xor(rank, half // 2)
    slot = (apart % 2) * 2 + apart // 2
    return pl.multiple_of(slot * (2 * HALF) + (half % 2) * HALF, HALF)


def side_lanes(rows, picks):
    lane = lax.broadcasted_iota(jnp.int32, (rows, SIDE), 1)
    value = jnp.zeros((rows, SIDE), f32)
    for index, entry in picks:
        value = jnp.where(lane == index, entry, value)
    return value.astype(bf16)


def three_parts(value):
    high = value.astype(bf16).astype(f32)
    rest = value - high
    middle = rest.astype(bf16).astype(f32)
    return high, middle, rest - middle


def one_head(values, head):
    lane = lax.broadcasted_iota(jnp.int32, values.shape, 1)
    return jnp.where((lane // HEAD_DIM) == head, values, jnp.zeros_like(values))


def attend_kernel(rank_ref, q, k, v, side, bias, out, norm, kcat, vcat, *, near, blocks):
    rank = rank_ref[0]
    pair = pl.program_id(0)
    queries = q.shape[0]

    @pl.when(pair == 0)
    def _():
        kcat[:, SIDE:] = side[...]
        vcat[:, SIDE:] = side[...]
        norm[...] = jnp.zeros_like(norm)

    for step in range(2 * blocks):
        source = pl.ds(row_offset(rank, step, blocks), HALF)
        kcat[step * HALF : (step + 1) * HALF, :SIDE] = k[source, :]
        vcat[step * HALF : (step + 1) * HALF, :SIDE] = v[source, :]

    lane = lax.broadcasted_iota(jnp.int32, (queries, SIDE), 1)
    halves = []
    for head in range(2):
        index = 2 * pair + head
        extra = side_lanes(queries, [(0, 1.0), (1 + index, 1.0)])
        wide = jnp.concatenate([one_head(q[...], head), extra], axis=1)
        logits = nt(wide, kcat[...])
        close = logits[:, :near] + bias[head].astype(f32)
        away = logits[:, near:]
        top = jnp.maximum(
            jnp.max(close, axis=-1, keepdims=True), jnp.max(away, axis=-1, keepdims=True)
        )
        close = jnp.exp(close - top).astype(bf16)
        away = jnp.exp(away - top).astype(bf16)
        mixed = nn(close, vcat[:near, :]) + nn(away, vcat[near:, :])
        total = mixed[:, SIDE + ONES : SIDE + ONES + 1]
        halves.append(mixed[:, :SIDE] * (1.0 / total))
        norm[...] = jnp.where(lane == index, top + jnp.log(total), norm[...])
    out[...] = jnp.where(lane < HEAD_DIM, halves[0], halves[1]).astype(bf16)


def attend(rank, q, kv, side, bias):
    queries, keys = q.shape[0], kv.shape[0]
    near = bias.shape[-1]
    blocks = keys // queries
    return pl.pallas_call(
        partial(attend_kernel, near=near, blocks=blocks),
        grid=(PAIRS,),
        in_specs=[
            pl.BlockSpec(memory_space=pltpu.SMEM),
            pl.BlockSpec((queries, SIDE), lambda i: (0, i)),
            pl.BlockSpec((keys, SIDE), lambda i: (0, i)),
            pl.BlockSpec((keys, SIDE), lambda i: (0, i + PAIRS)),
            pl.BlockSpec((keys, SIDE), lambda i: (0, 0)),
            pl.BlockSpec((2, queries, near), lambda i: (i, 0, 0)),
        ],
        out_specs=[
            pl.BlockSpec((queries, SIDE), lambda i: (0, i)),
            pl.BlockSpec((queries, SIDE), lambda i: (0, 0)),
        ],
        out_shape=[
            jax.ShapeDtypeStruct((queries, D), bf16),
            jax.ShapeDtypeStruct((queries, SIDE), f32),
        ],
        scratch_shapes=[pltpu.VMEM((keys, 2 * SIDE), bf16)] * 2,
        cost_estimate=pl.CostEstimate(flops=5_000_000_000, bytes_accessed=8_000_000, transcendentals=0),
        name="attend",
    )(rank, q, kv, kv, side, bias)


def attend_back_kernel(
    rank_ref, q, k, v, side, bias, norm, mixed, grad, dq, dk, dv, dnear, dfar,
    kcat, vcat, kturn, *, near, blocks, part,
):
    rank = rank_ref[0]
    pair = pl.program_id(0)
    queries = q.shape[0]
    keys = k.shape[0]

    @pl.when(pair == 0)
    def _():
        kcat[:, SIDE:] = side[...]
        vcat[:, SIDE:] = side[...]
        kturn[SIDE:, :] = side[...].astype(f32).T[ONES : 2 * ONES, :].astype(bf16)

    for step in range(2 * blocks):
        source = pl.ds(row_offset(rank, step, blocks), HALF)
        kcat[step * HALF : (step + 1) * HALF, :SIDE] = k[source, :]
        vcat[step * HALF : (step + 1) * HALF, :SIDE] = v[source, :]
    kturn[:SIDE, :] = kcat[:, :SIDE].astype(f32).T.astype(bf16)

    lane = lax.broadcasted_iota(jnp.int32, (queries, SIDE), 1)
    queries_of, grads_of, wide_q, wide_g = [], [], [], []
    products = grad[...].astype(f32) * mixed[...].astype(f32)
    for head in range(2):
        index = 2 * pair + head
        level = jnp.sum(jnp.where(lane == index, norm[...], 0.0), axis=-1, keepdims=True)
        delta = jnp.sum(
            jnp.where((lane // HEAD_DIM) == head, products, 0.0), axis=-1, keepdims=True
        )
        la, lb, lc = three_parts(-level)
        da, db, dc = three_parts(-delta)
        queries_of.append(one_head(q[...], head))
        grads_of.append(one_head(grad[...], head))
        extra = [(0, 1.0), (1 + index, 1.0), (ONES, la), (ONES + 1, lb), (ONES + 2, lc)]
        wide_q.append(jnp.concatenate([queries_of[head], side_lanes(queries, extra)], axis=1))
        extra = [(ONES, da), (ONES + 1, db), (ONES + 2, dc)]
        wide_g.append(jnp.concatenate([grads_of[head], side_lanes(queries, extra)], axis=1))

    sums = [jnp.zeros((kturn.shape[0], queries), f32) for _ in range(2)]
    for base in range(0, keys, part):
        span = slice(base, base + part)
        value_part = jnp.zeros((part, SIDE), f32)
        key_part = jnp.zeros((part, SIDE), f32)
        for head in range(2):
            logits = nt(kcat[span, :], wide_q[head])
            if base < near:
                logits = logits + bias[head, span, :].astype(f32)
            probs = jnp.exp(logits)
            pull = nt(vcat[span, :], wide_g[head])
            low = (probs * pull).astype(bf16)
            value_part += nn(probs.astype(bf16), grads_of[head])
            key_part += nn(low, queries_of[head])
            sums[head] += nn(kturn[:, span], low)
            if base < near:
                dnear[head, span, :] = low
        for step in range(base // HALF, (base + part) // HALF):
            target = pl.ds(row_offset(rank, step, blocks), HALF)
            inner = slice(step * HALF - base, (step + 1) * HALF - base)
            dk[target, :] = key_part[inner].astype(bf16)
            dv[target, :] = value_part[inner].astype(bf16)
    turned = jnp.concatenate([sums[0][:HEAD_DIM], sums[1][HEAD_DIM:SIDE]], axis=0)
    dq[...] = turned.T.astype(bf16)
    for head in range(2):
        dfar[head] = sums[head][SIDE:, :]


def attend_back(rank, q, kv, side, bias, norm, mixed, grad):
    queries, keys = q.shape[0], kv.shape[0]
    near = bias.shape[1]
    blocks = keys // queries
    own = pl.BlockSpec((queries, SIDE), lambda i: (0, i))
    every = pl.BlockSpec((keys, SIDE), lambda i: (0, i))
    return pl.pallas_call(
        partial(attend_back_kernel, near=near, blocks=blocks, part=2 * HALF),
        grid=(PAIRS,),
        in_specs=[
            pl.BlockSpec(memory_space=pltpu.SMEM),
            own,
            every,
            pl.BlockSpec((keys, SIDE), lambda i: (0, i + PAIRS)),
            pl.BlockSpec((keys, SIDE), lambda i: (0, 0)),
            pl.BlockSpec((2, near, queries), lambda i: (i, 0, 0)),
            pl.BlockSpec((queries, SIDE), lambda i: (0, 0)),
            own,
            own,
        ],
        out_specs=[
            own,
            every,
            every,
            pl.BlockSpec((2, near, queries), lambda i: (i, 0, 0)),
            pl.BlockSpec((2, ONES, queries), lambda i: (i, 0, 0)),
        ],
        out_shape=[
            jax.ShapeDtypeStruct((queries, D), bf16),
            jax.ShapeDtypeStruct((keys, D), bf16),
            jax.ShapeDtypeStruct((keys, D), bf16),
            jax.ShapeDtypeStruct((HEADS, near, queries), bf16),
            jax.ShapeDtypeStruct((HEADS, ONES, queries), f32),
        ],
        scratch_shapes=[
            pltpu.VMEM((keys, 2 * SIDE), bf16),
            pltpu.VMEM((keys, 2 * SIDE), bf16),
            pltpu.VMEM((SIDE + ONES, keys), bf16),
        ],
        cost_estimate=pl.CostEstimate(flops=12_000_000_000, bytes_accessed=12_000_000, transcendentals=0),
        name="attend_back",
    )(rank, q, kv, kv, side, bias, norm, mixed, grad)


def diagonal_kernel(a, b, c, out, *, queries):
    row = lax.broadcasted_iota(jnp.int32, (HALF, HALF), 0)
    lane = lax.broadcasted_iota(jnp.int32, (HALF, HALF), 1)
    flip = (row + lane == HALF - 1).astype(bf16)
    for step in range(a.shape[0] // HALF):
        span = slice(step * HALF, (step + 1) * HALF)
        total = nn(flip, a[span, :]) + nn(flip, b[span, :]) + nn(flip, c[span, :])
        wide = jnp.concatenate([total, jnp.zeros((HALF, HALF), f32)], axis=1)
        rolled = pltpu.roll(wide, 0, 1, stride=1, stride_axis=0)
        out[step : step + 1, :] = jnp.sum(rolled, axis=0, keepdims=True)


def diagonal_sums(parts):
    heads, near, queries = parts[0].shape
    steps = near // HALF
    spec = pl.BlockSpec((None, near, queries), lambda i: (i, 0, 0))
    return pl.pallas_call(
        partial(diagonal_kernel, queries=queries),
        grid=(heads,),
        in_specs=[spec] * 3,
        out_specs=pl.BlockSpec((None, steps, queries + HALF), lambda i: (i, 0, 0)),
        out_shape=jax.ShapeDtypeStruct((heads, steps, queries + HALF), f32),
        cost_estimate=pl.CostEstimate(flops=4_000_000_000, bytes_accessed=9_000_000, transcendentals=0),
        name="diagonal_sums",
    )(*parts)


def gelu_tanh(values):
    return jax.nn.gelu(values, approximate=True)


def dot(a, b):
    return jnp.dot(a, b, preferred_element_type=f32)


def per_device(
    byte_ids,
    lengths,
    teacher,
    embed_table,
    conv_weight,
    score_weight,
    attn_gain,
    rel_bias,
    query_weight,
    key_weight,
    value_weight,
    output_weight,
    ffn_gain,
    gate_weight,
    up_weight,
    down_weight,
):
    seqs, own_bytes = byte_ids.shape
    own = own_bytes // 2
    parts = lax.axis_size("seq")
    dp_size = lax.axis_size("dp")
    rank = lax.axis_index("seq")
    total_tokens, total_bytes = own * parts, own_bytes * parts
    shard = score_weight.shape[0]
    rank_ref = rank.reshape(1).astype(jnp.int32)

    live_here = jnp.sum(jnp.minimum((lengths + 1) // 2, total_tokens))
    count_bits = jnp.stack([live_here // 64, live_here % 64]).astype(bf16)
    count_cols = jnp.zeros((shard, 2), bf16).at[0].set(jnp.where(rank == 0, count_bits, 0))
    columns = jnp.concatenate(
        [
            embed_table.T,
            conv_weight.T,
            score_weight[:, None],
            attn_gain[:, None],
            ffn_gain[:, None],
            count_cols,
            jnp.zeros((shard, TABLE - VOCAB - 9), bf16),
        ],
        axis=1,
    )
    ids_low = jnp.stack([byte_ids // 16, byte_ids % 16]).astype(bf16)
    id_rows = ids_low.reshape(-1, TABLE)
    value = columns
    stages = axis_bits("dp")
    for position, (axis, bit) in enumerate(stages):
        value = gather_stage(value, axis, bit, position)
    value = value.reshape(dp_size, shard, TABLE)
    mine = jnp.concatenate([value.reshape(-1, TABLE), id_rows], axis=0)
    x_other = swap(mine, "seq", 2)
    pair = jnp.concatenate([mine, x_other], axis=0)
    c_other = swap(pair, "seq", 1)
    wide_rows = mine.shape[0]
    quarters = jnp.concatenate([pair, c_other], axis=0).reshape(parts, wide_rows, TABLE)
    apart = jnp.bitwise_xor(rank, jnp.arange(parts))
    slots = (apart % 2) * 2 + apart // 2
    ordered = jnp.take(quarters, slots, axis=0)
    table = (
        ordered[:, : dp_size * shard]
        .reshape(parts, dp_size, shard, TABLE)
        .transpose(1, 0, 2, 3)
        .reshape(D, TABLE)
    )
    all_ids = ordered[:, dp_size * shard :].reshape(parts, 2, seqs, own_bytes).astype(jnp.int32)
    all_ids = (all_ids[:, 0] * 16 + all_ids[:, 1]).transpose(1, 0, 2).reshape(seqs, total_bytes)
    counts = jnp.sum(table[:, VOCAB + 7 : VOCAB + 9].astype(f32), axis=0)
    live_count = counts[0] * 64.0 + counts[1]
    ffn_gain_full = table[:, VOCAB + 6].astype(f32)

    padded_ids = jnp.pad(all_ids, ((0, 0), (32, 32)), constant_values=-1)
    first_byte = (rank * own_bytes).astype(jnp.int32)
    first_other = (jnp.bitwise_xor(rank, 2) * own_bytes).astype(jnp.int32)
    firsts = jnp.stack([first_byte, first_other])

    def phases(start):
        window = lax.dynamic_slice_in_dim(padded_ids, start, own_bytes + 64, 1)
        return window.reshape(seqs, -1, 4).transpose(0, 2, 1).reshape(seqs, -1)

    phase_ids = phases(first_byte)
    two_phases = jnp.stack([phase_ids, phases(first_other)], axis=1)

    far = rel_bias.astype(f32)
    far_two = jnp.stack([far[15], far[31]], axis=1)
    near = own + 2 * HALF
    steps = jnp.arange(near + own, dtype=jnp.int32)
    relative = jnp.where(steps < near, steps, steps - near - own) - HALF
    diag = jnp.einsum("jb,bh->hj", hot_buckets(relative), far, precision=highest)
    tile, turned_tile = near_bias(rank_ref, far_two, diag[:, None, :], own, near, parts)
    key_at = jnp.arange(total_tokens, dtype=jnp.int32)
    raw_at = rank * own - HALF + key_at
    true_at = jnp.mod(raw_at, total_tokens)
    is_near = key_at < near
    to_right = true_at > rank * own
    masked = jnp.where(2 * true_at[None, :] < lengths[:, None], 0.0, masked_score)
    lanes = jnp.arange(SIDE, dtype=jnp.int32)
    far_rows = jnp.where(
        is_near[:, None], 0.0, jnp.where(to_right[:, None], far[31][None], far[15][None])
    )
    fixed = jnp.concatenate(
        [
            jnp.zeros((total_tokens, 1), f32),
            far_rows,
            jnp.zeros((total_tokens, ONES - 1 - HEADS), f32),
            jnp.ones((total_tokens, 3), f32),
            jnp.zeros((total_tokens, 1), f32),
            (~is_near & ~to_right)[:, None].astype(f32),
            (~is_near & to_right)[:, None].astype(f32),
            jnp.zeros((total_tokens, SIDE - RIGHT - 1), f32),
        ],
        axis=1,
    )
    side = jnp.where(lanes == 0, masked[:, :, None], fixed[None]).astype(bf16)

    qkv_full = gather_rows(jnp.concatenate([query_weight, key_weight, value_weight], axis=1))
    query_full, kv_full = qkv_full[:, :D], qkv_full[:, D:]
    key_full, value_full = qkv_full[:, D : 2 * D], qkv_full[:, 2 * D :]
    gate_up = jnp.concatenate([gate_weight, up_weight], axis=1)
    ffn_dim = gate_weight.shape[1]
    wide_full = lax.all_gather(
        jnp.concatenate([gate_up, output_weight], axis=1), both, axis=0, tiled=True
    )
    down_full = lax.all_gather(down_weight, both, axis=0, tiled=True)
    gate_full, up_full = wide_full[:, :ffn_dim], wide_full[:, ffn_dim : 2 * ffn_dim]
    output_full = wide_full[:, 2 * ffn_dim :]

    resid_two, normed_two = pool(firsts, two_phases.reshape(2 * seqs, -1, 1), table, total_bytes)
    resid_two = resid_two.reshape(seqs, 2, own, D)
    normed_two = normed_two.reshape(seqs, 2 * own, D)
    residual = resid_two[:, 0]
    normed, queries, pairs_kv, attended, norms = [], [], [], [], []
    for s in range(seqs):
        other = swap(normed_two[s], "seq", 1)
        rows = jnp.concatenate([normed_two[s], other], axis=0)
        normed.append(rows)
        queries.append(dot(rows[:own], query_full).astype(bf16))
        pairs_kv.append(dot(rows, kv_full).astype(bf16))
        mixed, norm = attend(rank_ref, queries[s], pairs_kv[s], side[s], tile)
        attended.append(mixed)
        norms.append(norm)

    token_rows = seqs * own
    flat_in = residual.reshape(token_rows, D)
    att = jnp.concatenate(attended, axis=0)
    after_attn = flat_in + dot(att, output_full)
    mean_square = jnp.mean(after_attn * after_attn, axis=-1, keepdims=True)
    ffn_scale = lax.rsqrt(mean_square + epsilon)
    ffn_in = (after_attn * ffn_scale * ffn_gain_full).astype(bf16)
    gate_pre = dot(ffn_in, gate_full)
    up_pre = dot(ffn_in, up_full)
    gate_act, gelu_back = jax.vjp(gelu_tanh, gate_pre)
    hidden = (gate_act * up_pre).astype(bf16)
    block_out = after_attn + dot(hidden, down_full)
    own_at = rank * own + jnp.arange(own, dtype=jnp.int32)
    live = (2 * own_at[None, :] < lengths[:, None]).astype(f32).reshape(token_rows, 1)
    residual_err = block_out - teacher.reshape(token_rows, D)
    error_local = jnp.sum(live * residual_err * residual_err)
    out_grad = (2.0 / live_count) * live * residual_err
    branch_grad = out_grad.astype(bf16)
    down_grad = jnp.einsum("tf,td->fd", hidden, branch_grad, preferred_element_type=f32)
    hidden_grad = jnp.einsum("td,fd->tf", branch_grad, down_full, preferred_element_type=f32)
    gate_low = gelu_back(hidden_grad * up_pre)[0].astype(bf16)
    up_low = (hidden_grad * gate_act).astype(bf16)
    gate_grad = jnp.einsum("td,tf->df", ffn_in, gate_low, preferred_element_type=f32)
    up_grad = jnp.einsum("td,tf->df", ffn_in, up_low, preferred_element_type=f32)
    ffn_in_grad = jnp.einsum(
        "tf,df->td", gate_low, gate_full, preferred_element_type=f32
    ) + jnp.einsum("tf,df->td", up_low, up_full, preferred_element_type=f32)
    ffn_gain_grad = jnp.sum(ffn_in_grad * after_attn * ffn_scale, axis=0)
    gained = ffn_in_grad * ffn_gain_full
    inner = jnp.mean(gained * after_attn, axis=-1, keepdims=True)
    after_grad = out_grad + ffn_scale * gained - after_attn * (ffn_scale**3 * inner)

    gate_up_sum = lax.psum_scatter(
        jnp.concatenate([gate_grad, up_grad], axis=1).astype(bf16), both, scatter_dimension=0, tiled=True
    )
    down_sum = lax.psum_scatter(down_grad.astype(bf16), both, scatter_dimension=0, tiled=True)

    attn_branch_grad = after_grad.astype(bf16)
    output_grad = jnp.einsum("td,te->de", att, attn_branch_grad, preferred_element_type=f32)
    attended_grad = jnp.einsum(
        "te,de->td", attn_branch_grad, output_full, preferred_element_type=f32
    ).astype(bf16)
    normed_grads, near_parts, far_parts = [], [], []
    query_grad = jnp.zeros((D, D), f32)
    key_grad = jnp.zeros((D, D), f32)
    value_grad = jnp.zeros((D, D), f32)
    for s in range(seqs):
        dq, dk, dv, dnear, dfar = attend_back(
            rank_ref, queries[s], pairs_kv[s], side[s], turned_tile, norms[s],
            attended[s], attended_grad[s * own : (s + 1) * own],
        )
        near_parts.append(dnear)
        far_parts.append(jnp.sum(dfar, axis=-1))
        pulled = jnp.einsum("te,de->td", dk, key_full, preferred_element_type=f32) + jnp.einsum(
            "te,de->td", dv, value_full, preferred_element_type=f32
        )
        pulled = pulled.at[:own].add(
            jnp.einsum("te,de->td", dq, query_full, preferred_element_type=f32)
        )
        chip = pulled[: 2 * own] + swap(pulled[2 * own :].astype(bf16), "seq", 1).astype(f32)
        normed_grads.append(
            chip[:own] + swap(chip[own:].astype(bf16), "seq", 2).astype(f32)
        )
        query_grad += jnp.einsum("td,te->de", normed[s][:own], dq, preferred_element_type=f32)
        key_grad += jnp.einsum("td,te->de", normed[s], dk, preferred_element_type=f32)
        value_grad += jnp.einsum("td,te->de", normed[s], dv, preferred_element_type=f32)

    attn_sum = scatter_rows(
        jnp.concatenate([query_grad, key_grad, value_grad, output_grad], axis=1)
    )
    embed_part, small_part = pool_back(
        first_byte.reshape(1), phase_ids[:, :, None], phase_ids[:, None, :], table,
        jnp.stack(normed_grads), residual, after_grad.reshape(seqs, own, D), total_bytes,
    )
    front = jnp.concatenate(
        [
            embed_part[:VOCAB],
            small_part[:6],
            ffn_gain_grad[None],
            jnp.zeros((TABLE - VOCAB - 7, D), f32),
        ],
        axis=0,
    )
    front_sum = scatter_rows(front.T).T

    diagonals = diagonal_sums(near_parts)
    place = jnp.arange(near // HALF, dtype=jnp.int32)[:, None] * HALF
    relative = place - 1 - jnp.arange(own + HALF, dtype=jnp.int32)[None, :]
    raw_key = place + rank * own - HALF
    relative = relative + jnp.where(
        raw_key < 0, total_tokens, jnp.where(raw_key >= total_tokens, -total_tokens, 0)
    )
    bias_local = jnp.einsum(
        "njb,hnj->bh", hot_buckets(relative), diagonals, precision=highest
    )
    far_total = sum(far_parts)
    bias_local = bias_local.at[15].add(far_total[:, LEFT - ONES])
    bias_local = bias_local.at[31].add(far_total[:, RIGHT - ONES])
    sums = jnp.concatenate([bias_local.reshape(-1), error_local[None]])
    sums = lax.psum(sums, both)
    bias_grad = sums[:-1].reshape(BUCKETS, HEADS)

    return (
        block_out.reshape(seqs, own, D),
        sums[-1] / live_count,
        front_sum[:VOCAB],
        front_sum[VOCAB : VOCAB + 4],
        front_sum[VOCAB + 4],
        front_sum[VOCAB + 5],
        bias_grad,
        attn_sum[:, :D],
        attn_sum[:, D : 2 * D],
        attn_sum[:, 2 * D : 3 * D],
        attn_sum[:, 3 * D :],
        front_sum[VOCAB + 6],
        gate_up_sum[:, :ffn_dim].astype(f32),
        gate_up_sum[:, ffn_dim:].astype(f32),
        down_sum.astype(f32),
    )


def solution(mesh):
    tokens = P("dp", "seq", None)
    features = P(("dp", "seq"))
    columns = P(None, ("dp", "seq"))
    rows = P(("dp", "seq"), None)
    in_specs = (
        P("dp", "seq"), P("dp"), tokens, columns, columns, features, features, P(),
        rows, rows, rows, rows, features, rows, rows, rows,
    )
    out_specs = (
        tokens, P(), columns, columns, features, features, P(), rows, rows, rows, rows,
        features, rows, rows, rows,
    )
    return jax.shard_map(
        per_device, mesh=mesh, in_specs=in_specs, out_specs=out_specs, check_vma=False
    )
```

```python
from functools import partial

import jax
import jax.numpy as jnp
from jax import lax
from jax.experimental import pallas as pl
from jax.experimental.pallas import tpu as pltpu
from jax.sharding import PartitionSpec as P

D = 768
HEADS = 12
HEAD_DIM = 64
VOCAB = 259
BUCKETS = 32
TABLE = 384
PAIRS = HEADS // 2
SIDE = 128
ONES = 16
LEFT = 20
RIGHT = 21
HALF = 128

epsilon = 1e-06
thresholds = (12, 16, 23, 32, 46, 64, 91)
masked_score = -1000000000.0
highest = lax.Precision.HIGHEST
bf16 = jnp.bfloat16
f32 = jnp.float32
both = ("dp", "seq")


def nt(a, b):
    return lax.dot_general(a, b, (((1,), (1,)), ((), ())), preferred_element_type=f32)


def nn(a, b):
    return lax.dot_general(a, b, (((1,), (0,)), ((), ())), preferred_element_type=f32)


def bucket_of(relative):
    distance = jnp.abs(relative)
    far_bucket = 8 + sum(((distance >= border).astype(jnp.int32) for border in thresholds))
    return jnp.where(relative > 0, 16, 0).astype(jnp.int32) + jnp.where(
        distance < 8, distance, far_bucket
    )


def hot_buckets(relative):
    return (bucket_of(relative)[..., None] == jnp.arange(BUCKETS, dtype=jnp.int32)).astype(f32)


def swap(value, axis, bit):
    peers = lax.axis_size(axis)
    return lax.ppermute(value, axis, [(i, i ^ bit) for i in range(peers)])


def axis_bits(axis):
    bits, bit = [], lax.axis_size(axis) // 2
    while bit:
        bits.append((axis, bit))
        bit //= 2
    return bits


def my_bit(axis, bit):
    return (lax.axis_index(axis) // bit) % 2


def gather_stage(value, axis, bit, position):
    other = swap(value, axis, bit)
    upper = my_bit(axis, bit) == 1
    return jnp.stack(
        [jnp.where(upper, other, value), jnp.where(upper, value, other)], axis=position
    )


class RowGather:
    def __init__(self, rows, order):
        self.value = rows
        self.order = list(order)
        self.places = axis_bits("dp") + axis_bits("seq")
        self.done = []
        self.got = None

    def start(self):
        if self.order:
            self.stage = self.order.pop(0)
            self.got = swap(self.value, *self.stage)

    def finish(self, *others):
        if self.got is None:
            return
        got = after(self.got, *others) if others else self.got
        self.got = None
        place = self.places.index(self.stage)
        position = sum(p < place for p in self.done)
        self.done.append(place)
        upper = my_bit(*self.stage) == 1
        self.value = jnp.stack(
            [jnp.where(upper, got, self.value), jnp.where(upper, self.value, got)],
            axis=position,
        )

    def result(self):
        self.finish()
        while self.order:
            self.start()
            self.finish()
        return self.value


def gather_order(first_axis):
    seq, dp = axis_bits("seq"), axis_bits("dp")
    if first_axis == "y":
        return dp + seq
    return dp[:-1] + seq[:-1] + dp[-1:] + seq[-1:]


def after(value, *others):
    return lax.optimization_barrier((value,) + others)[0]


def sum_order(first):
    seq, dp = axis_bits("seq")[::-1], axis_bits("dp")[::-1]
    if first == "x":
        return seq + dp
    if first == "y":
        return seq[:1] + dp[:1] + seq[1:] + dp[1:]
    return seq[:1] + dp[1:] + seq[1:] + dp[:1]


class RowSum:
    def __init__(self, total, order):
        self.parts = [total]
        self.left = axis_bits("dp") + axis_bits("seq")
        self.order = list(order)
        self.sent = self.got = None

    def start(self):
        if not self.order:
            return
        axis, bit = self.order.pop(0)
        position = self.left.index((axis, bit))
        self.left.remove((axis, bit))
        mine = my_bit(axis, bit)

        def half(value, which):
            lead, rows, cols = value.shape
            outer = lead << position
            cut = value.reshape(outer, 2, lead * rows // (2 * outer), cols)
            picked = lax.dynamic_index_in_dim(cut, which, 1, keepdims=False)
            return picked.reshape(lead, rows // 2, cols)

        send = sum(half(value, 1 - mine).astype(f32) for value in self.parts)
        self.sent = send.astype(bf16)
        self.parts = [half(value, mine) for value in self.parts]
        self.got = swap(self.sent, axis, bit)

    def finish(self, *others):
        if self.got is not None:
            self.parts.append(after(self.got, *others) if others else self.got)
            self.got = None

    def result(self):
        self.finish()
        while self.order:
            self.start()
            self.finish()
        return sum(value.astype(f32) for value in self.parts)


def after_sends(value, *sums):
    sends = [each.sent for each in sums if each.sent is not None]
    return after(value, *sends)


class SumEverywhere:
    def __init__(self, value):
        self.value = value
        self.order = axis_bits("seq")[::-1] + axis_bits("dp")[::-1]
        self.got = None

    def start(self):
        if self.order:
            self.got = swap(self.value, *self.order.pop(0))

    def finish(self, *others):
        if self.got is not None:
            self.value = self.value + (after(self.got, *others) if others else self.got)
            self.got = None

    def result(self):
        self.finish()
        while self.order:
            self.start()
            self.finish()
        return self.value


def up(x):
    return pltpu.roll(x, x.shape[0] - 1, 0)


def down(x):
    return pltpu.roll(x, 1, 0)


def triples(c, m0, m1):
    c0, c1, c2, c3 = c
    p01, p23 = c0 + c1, c2 + c3
    t0, t1, t2, t3 = down(c3) + p01, p01 + c2, c1 + p23, p23 + up(c0)
    before, after = (down(t3), t0, t1, t2), (t1, t2, t3, up(t0))
    here = (t0, t1, t2, t3)
    return tuple(
        jnp.where(m0[k], after[k], jnp.where(m1[k], here[k], before[k])) for k in range(4)
    )


def position_marks(first, rows, total_bytes):
    row = lax.broadcasted_iota(jnp.int32, (rows, 128), 0)
    live, m0, m1 = [], [], []
    for k in range(4):
        pos = first + 4 * (row - 8) + k
        live.append(((pos >= 0) & (pos < total_bytes)).astype(f32))
        shifted = (pos + 48).astype(f32)
        third = jnp.floor((shifted + 0.5) * (1.0 / 3.0))
        rest = shifted - 3.0 * third
        m0.append(rest < 0.5)
        m1.append((rest > 0.5) & (rest < 1.5))
    return live, m0, m1


def lane_chunk(i):
    return pl.ds(pl.multiple_of(i * 128, 128), 128)


def embed_bytes(ids, table, emb):
    lane = lax.broadcasted_iota(jnp.int32, (ids.shape[0], TABLE), 1)
    emb[...] = nt((ids == lane).astype(bf16), table)


def small_rows(table, small):
    lane = lax.broadcasted_iota(jnp.int32, (8, TABLE), 1)
    row = lax.broadcasted_iota(jnp.int32, (8, TABLE), 0)
    small[...] = nt((lane == row + VOCAB).astype(bf16), table)


def all_lanes(x):
    return jnp.broadcast_to(jnp.sum(x, axis=-1, keepdims=True), x.shape)


def block_probs(emb, small, conv, accs, live, m0, m1, rows):
    accs[0:4] = jnp.zeros((4, rows, 128), f32)

    def step(i, _):
        chunk = lane_chunk(i)
        w0, w1, w2, w3 = [small[k : k + 1, chunk] for k in range(4)]
        scorer = small[4:5, chunk]
        e0, e1, e2, e3 = [emb[k * rows : (k + 1) * rows, chunk] for k in range(4)]
        e3d, e0u, e1u = down(e3), up(e0), up(e1)
        c = (
            w0 * e3d + w1 * e0 + w2 * e1 + w3 * e2,
            w0 * e0 + w1 * e1 + w2 * e2 + w3 * e3,
            w0 * e1 + w1 * e2 + w2 * e3 + w3 * e0u,
            w0 * e2 + w1 * e3 + w2 * e0u + w3 * e1u,
        )
        for k in range(4):
            value = c[k] * live[k]
            conv[k, :, chunk] = value
            accs[k] += value * scorer
        return 0

    lax.fori_loop(0, D // 128, step, 0)
    score = [all_lanes(accs[k]) for k in range(4)]
    three = triples(score, m0, m1)
    p01, p23 = score[0] + score[1], score[2] + score[3]
    quad = 0.25 * (p01 + p23)
    probs = []
    for k in range(4):
        scores = (score[k], 0.5 * (p01, p01, p23, p23)[k], three[k] * (1.0 / 3.0), quad)
        top = jnp.maximum(jnp.maximum(scores[0], scores[1]), jnp.maximum(scores[2], scores[3]))
        powers = [jnp.exp(value - top) for value in scores]
        norm = 1.0 / (powers[0] + powers[1] + powers[2] + powers[3])
        probs.append([power * norm for power in powers])
    return probs


def reach(m0, m1, k, ahead):
    one = jnp.ones(m0[k].shape, f32)
    zero = jnp.zeros_like(one)
    if ahead == 0:
        return one
    if ahead == 1:
        return jnp.where(m0[k] | m1[k], one, zero)
    if ahead == 2:
        return jnp.where(m0[k], one, zero)
    if ahead == -1:
        return jnp.where(m0[k], zero, one)
    return jnp.where(m0[k] | m1[k], zero, one)


def token_weights(probs, m0, m1):
    weights = []
    for half in range(2):
        first, second = probs[2 * half], probs[2 * half + 1]
        pair = 0.5 * (first[1] + second[1])
        quad = 0.25 * (first[3] + second[3])
        row = []
        for j in range(6):
            place = 2 * half - 2 + j
            value = jnp.zeros_like(pair)
            for k, p in ((2 * half, first), (2 * half + 1, second)):
                ahead = place - k
                if abs(ahead) <= 2:
                    value += p[2] * (1.0 / 3.0) * reach(m0, m1, k, ahead)
                if ahead == 0:
                    value += p[0]
            if 0 <= place < 4:
                value += quad
            if place // 2 == half:
                value += pair
            row.append(value)
        weights.append(row)
    return weights


def places(c):
    c0, c1, c2, c3 = c
    return ((down(c2), down(c3), c0, c1, c2, c3), (c0, c1, c2, c3, up(c0), up(c1)))


def pool_kernel(first_ref, ids, table, resid, normed, emb, small, conv, accs, tokens, *, rows, total_bytes):
    first = first_ref[0]
    embed_bytes(ids[...], table[...], emb)
    small_rows(table[...], small)
    live, m0, m1 = position_marks(first, rows, total_bytes)
    probs = block_probs(emb, small, conv, accs, live, m0, m1, rows)
    weights = token_weights(probs, m0, m1)
    for half in range(2):
        for j in range(6):
            accs[6 * half + j] = 0.5 * weights[half][j]
    own = rows - 16

    def step(i, square):
        chunk = lane_chunk(i)
        around = places([conv[k, :, chunk] for k in range(4)])
        for half in range(2):
            token = accs[6 * half] * around[half][0]
            for j in range(1, 6):
                token += accs[6 * half + j] * around[half][j]
            tokens[i, pl.ds(half, own, stride=2), :] = token[8 : 8 + own]
        values = tokens[i]
        resid[:, chunk] = values
        return square + values * values

    square = lax.fori_loop(0, D // 128, step, jnp.zeros((2 * own, 128), f32))
    scale = lax.rsqrt(jnp.sum(square, axis=-1, keepdims=True) * (1.0 / D) + epsilon)
    normed[...] = (resid[...] * scale * small[5:6, :]).astype(bf16)


def pool(first, ids, table, total_bytes):
    count, wide, _ = ids.shape
    rows = wide // 4
    tokens = 2 * (rows - 16)
    return pl.pallas_call(
        partial(pool_kernel, rows=rows, total_bytes=total_bytes),
        grid=(count,),
        in_specs=[
            pl.BlockSpec(memory_space=pltpu.SMEM),
            pl.BlockSpec((None, wide, 1), lambda i: (i, 0, 0)),
            pl.BlockSpec((D, TABLE), lambda i: (0, 0)),
        ],
        out_specs=[
            pl.BlockSpec((None, tokens, D), lambda i: (i, 0, 0)),
            pl.BlockSpec((None, tokens, D), lambda i: (i, 0, 0)),
        ],
        out_shape=[
            jax.ShapeDtypeStruct((count, tokens, D), f32),
            jax.ShapeDtypeStruct((count, tokens, D), bf16),
        ],
        scratch_shapes=[
            pltpu.VMEM((wide, D), f32),
            pltpu.VMEM((8, D), f32),
            pltpu.VMEM((4, rows, D), f32),
            pltpu.VMEM((12, rows, 128), f32),
            pltpu.VMEM((D // 128, tokens, 128), f32),
        ],
        cost_estimate=pl.CostEstimate(flops=count * 3_000_000_000, bytes_accessed=4_000_000, transcendentals=0),
        name="pool",
    )(first, ids, table)


def pool_back_kernel(
    first_ref, ids, ids_row, table, grad_normed, resid, after, embed_grad, small_grad,
    emb, small, conv, accs, tokens, pulls, emb_grad, *, rows, total_bytes,
):
    first = first_ref[0]
    own = rows - 16
    chunks = D // 128

    @pl.when(pl.program_id(0) == 0)
    def _():
        embed_grad[...] = jnp.zeros_like(embed_grad)
        small_grad[...] = jnp.zeros_like(small_grad)

    embed_bytes(ids[...], table[...], emb)
    small_rows(table[...], small)
    live, m0, m1 = position_marks(first, rows, total_bytes)

    x, gn = resid[...], grad_normed[...]
    scale = lax.rsqrt(jnp.mean(x * x, axis=-1, keepdims=True) + epsilon)
    gain = small[5:6, :]
    small_grad[5:6, :] += jnp.sum(gn * x * scale, axis=0, keepdims=True)
    gg = gain * gn
    inner = jnp.mean(gg * x, axis=-1, keepdims=True)
    total = after[...] + scale * gg - x * (scale * scale * scale * inner)
    for i in range(chunks):
        tokens[i] = total[:, i * 128 : (i + 1) * 128]

    probs = block_probs(emb, small, conv, accs, live, m0, m1, rows)
    accs[0:12] = jnp.zeros((12, rows, 128), f32)
    pulls[:, 0:8, :] = jnp.zeros((2, 8, D), f32)
    pulls[:, rows - 8 : rows, :] = jnp.zeros((2, 8, D), f32)

    def dots(i, _):
        chunk = lane_chunk(i)
        around = places([conv[k, :, chunk] for k in range(4)])
        for half in range(2):
            pulls[half, 8 : 8 + own, chunk] = 0.5 * tokens[i, pl.ds(half, own, stride=2), :]
            g = pulls[half, :, chunk]
            for j in range(6):
                accs[6 * half + j] += g * around[half][j]
        return 0

    lax.fori_loop(0, chunks, dots, 0)
    pulled = []
    for half in range(2):
        at = [all_lanes(accs[6 * half + j]) for j in range(6)]
        pair = 0.5 * (at[2] + at[3])
        quad = 0.25 * (at[2] + at[3] + (at[4] + at[5] if half == 0 else at[0] + at[1]))
        for k in (2 * half, 2 * half + 1):
            middle = k - (2 * half - 2)
            three = sum(
                at[middle + ahead] * reach(m0, m1, k, ahead)
                for ahead in range(-2, 3)
                if 0 <= middle + ahead < 6
            ) * (1.0 / 3.0)
            gd = (at[middle], pair, three, quad)
            p = probs[k]
            mean = p[0] * gd[0] + p[1] * gd[1] + p[2] * gd[2] + p[3] * gd[3]
            pulled.append([p[b] * (gd[b] - mean) for b in range(4)])

    spread = triples([pulled[k][2] for k in range(4)], m0, m1)
    quad = 0.25 * (pulled[0][3] + pulled[1][3] + pulled[2][3] + pulled[3][3])
    weights = token_weights(probs, m0, m1)
    for k in range(4):
        half = k // 2
        pair = 0.5 * (pulled[2 * half][1] + pulled[2 * half + 1][1])
        accs[k] = (pulled[k][0] + pair + spread[k] * (1.0 / 3.0) + quad) * live[k]
    inside = (lax.broadcasted_iota(jnp.int32, (rows, 128), 0) >= 8) & (
        lax.broadcasted_iota(jnp.int32, (rows, 128), 0) < 8 + own
    )
    even = [jnp.where(inside, weight, 0.0) for weight in weights[0]]
    odd = [jnp.where(inside, weight, 0.0) for weight in weights[1]]
    reached = (
        (down(odd[4]), even[2], odd[0]),
        (down(odd[5]), even[3], odd[1]),
        (even[4], odd[2], up(even[0])),
        (even[5], odd[3], up(even[1])),
    )
    for k in range(4):
        for j in range(3):
            accs[4 + 3 * k + j] = reached[k][j] * live[k]

    def back(i, _):
        chunk = lane_chunk(i)
        w0, w1, w2, w3 = [small[k : k + 1, chunk] for k in range(4)]
        scorer = small[4:5, chunk]
        g0, g1 = pulls[0, :, chunk], pulls[1, :, chunk]
        g1d, g0u = down(g1), up(g0)
        e0, e1, e2, e3 = [emb[k * rows : (k + 1) * rows, chunk] for k in range(4)]
        near = ((g1d, g0, g1), (g1d, g0, g1), (g0, g1, g0u), (g0, g1, g0u))
        score = jnp.zeros((rows, 128), f32)
        gc = []
        for k in range(4):
            score += accs[k] * conv[k, :, chunk]
            value = accs[k] * scorer
            for j in range(3):
                value += accs[4 + 3 * k + j] * near[k][j]
            gc.append(value)
        small_grad[4:5, chunk] += jnp.sum(score, axis=0, keepdims=True)
        gc0, gc1, gc2, gc3 = gc
        e3d, e0u, e1u = down(e3), up(e0), up(e1)
        taps = (
            gc0 * e3d + gc1 * e0 + gc2 * e1 + gc3 * e2,
            gc0 * e0 + gc1 * e1 + gc2 * e2 + gc3 * e3,
            gc0 * e1 + gc1 * e2 + gc2 * e3 + gc3 * e0u,
            gc0 * e2 + gc1 * e3 + gc2 * e0u + gc3 * e1u,
        )
        for k in range(4):
            small_grad[k : k + 1, chunk] += jnp.sum(taps[k], axis=0, keepdims=True)
        gc3d, gc2d, gc0u = down(gc3), down(gc2), up(gc0)
        grads = (
            w0 * gc1 + w1 * gc0 + w2 * gc3d + w3 * gc2d,
            w0 * gc2 + w1 * gc1 + w2 * gc0 + w3 * gc3d,
            w0 * gc3 + w1 * gc2 + w2 * gc1 + w3 * gc0,
            w0 * gc0u + w1 * gc3 + w2 * gc2 + w3 * gc1,
        )
        for k in range(4):
            emb_grad[k * rows : (k + 1) * rows, chunk] = grads[k].astype(bf16)
        return 0

    lax.fori_loop(0, chunks, back, 0)
    row = lax.broadcasted_iota(jnp.int32, (TABLE, 4 * rows), 0)
    embed_grad[...] += nn((ids_row[...] == row).astype(bf16), emb_grad[...])


def pool_back(seq, first, ids, ids_row, table, grad_normed, resid, after_grad, total_bytes):
    _, wide, _ = ids.shape
    rows = wide // 4
    tokens = 2 * (rows - 16)
    token_spec = pl.BlockSpec((None, tokens, D), lambda i: (seq, 0, 0))
    return pl.pallas_call(
        partial(pool_back_kernel, rows=rows, total_bytes=total_bytes),
        grid=(1,),
        in_specs=[
            pl.BlockSpec(memory_space=pltpu.SMEM),
            pl.BlockSpec((None, wide, 1), lambda i: (seq, 0, 0)),
            pl.BlockSpec((None, 1, wide), lambda i: (seq, 0, 0)),
            pl.BlockSpec((D, TABLE), lambda i: (0, 0)),
            token_spec,
            token_spec,
            token_spec,
        ],
        out_specs=[
            pl.BlockSpec((TABLE, D), lambda i: (0, 0)),
            pl.BlockSpec((8, D), lambda i: (0, 0)),
        ],
        out_shape=[
            jax.ShapeDtypeStruct((TABLE, D), f32),
            jax.ShapeDtypeStruct((8, D), f32),
        ],
        scratch_shapes=[
            pltpu.VMEM((wide, D), f32),
            pltpu.VMEM((8, D), f32),
            pltpu.VMEM((4, rows, D), f32),
            pltpu.VMEM((16, rows, 128), f32),
            pltpu.VMEM((D // 128, tokens, 128), f32),
            pltpu.VMEM((2, rows, D), f32),
            pltpu.VMEM((wide, D), bf16),
        ],
        cost_estimate=pl.CostEstimate(flops=8_000_000_000, bytes_accessed=8_000_000, transcendentals=0),
        name="pool_back",
    )(first, ids, ids_row, table, grad_normed, resid, after_grad)


def prepare_kernel(
    rank_ref, lengths_ref, bias_ref, lanes_bias, tile, turned, side, diag, *, queries, keys, parts
):
    head = pl.program_id(0)
    rank = rank_ref[0]

    @pl.when(head == 0)
    def _():
        place = lax.broadcasted_iota(jnp.int32, (BUCKETS, 6 * HALF), 1)
        inside = lax.rem(place, 2 * HALF)
        offset = jnp.where(inside < HALF, inside, inside - 2 * HALF)
        relative = (place // (2 * HALF) - 1) * HALF + offset
        bucket = lax.broadcasted_iota(jnp.int32, (BUCKETS, 6 * HALF), 0)
        hot = (bucket_of(relative) == bucket).astype(bf16)
        diag[...] = lax.dot_general(
            lanes_bias[...], hot, (((0,), (0,)), ((), ())), preferred_element_type=f32
        )
        row = lax.broadcasted_iota(jnp.int32, (keys, SIDE), 0)
        lane = lax.broadcasted_iota(jnp.int32, (keys, SIDE), 1)
        at = lax.rem(rank * queries - HALF + row + keys, keys)
        far = row >= queries + 2 * HALF
        right = far & (at > rank * queries)
        left = far & (at <= rank * queries)
        fixed = jnp.where(
            right,
            lanes_bias[31:32, :].astype(f32),
            jnp.where(left, lanes_bias[15:16, :].astype(f32), 0.0),
        )
        fixed = jnp.where((lane >= ONES) & (lane < ONES + 3), 1.0, fixed)
        fixed = jnp.where((lane == LEFT) & left | (lane == RIGHT) & right, 1.0, fixed)
        for s in range(side.shape[0]):
            masked = jnp.where(2 * at < lengths_ref[s], 0.0, masked_score)
            side[s] = jnp.where(lane == 0, masked, fixed).astype(bf16)

    blocks = []
    for index in range(3):
        line = diag[pl.ds(head + 1, 1), index * 2 * HALF : (index + 1) * 2 * HALF]
        full = jnp.broadcast_to(line, (HALF, 2 * HALF))
        blocks.append(pltpu.roll(full, 0, 1, stride=1, stride_axis=0)[:, :HALF])
    turned_blocks = [block.T.astype(bf16) for block in blocks]
    blocks = [block.astype(bf16) for block in blocks]
    behind = jnp.full((HALF, HALF), bias_ref[15, head], f32).astype(bf16)
    ahead = jnp.full((HALF, HALF), bias_ref[31, head], f32).astype(bf16)
    steps = queries // HALF
    for q in range(steps):
        for n in range(steps + 2):
            apart = n - 1 - q
            wrapped = ((n == 0) & (rank == 0), (n == steps + 1) & (rank == parts - 1))
            plain = behind if apart < -1 else ahead if apart > 1 else blocks[apart + 1]
            flipped = behind if apart < -1 else ahead if apart > 1 else turned_blocks[apart + 1]
            if n == 0:
                plain = jnp.where(wrapped[0], ahead, plain)
                flipped = jnp.where(wrapped[0], ahead, flipped)
            if n == steps + 1:
                plain = jnp.where(wrapped[1], behind, plain)
                flipped = jnp.where(wrapped[1], behind, flipped)
            tile[q * HALF : (q + 1) * HALF, n * HALF : (n + 1) * HALF] = plain
            turned[n * HALF : (n + 1) * HALF, q * HALF : (q + 1) * HALF] = flipped


def prepare(rank, lengths, bias, queries, keys, parts):
    near = queries + 2 * HALF
    seqs = lengths.shape[0]
    lanes_bias = jnp.pad(bias, ((0, 0), (1, SIDE - 1 - HEADS)))
    smem = pl.BlockSpec(memory_space=pltpu.SMEM)
    return pl.pallas_call(
        partial(prepare_kernel, queries=queries, keys=keys, parts=parts),
        grid=(HEADS,),
        in_specs=[smem, smem, smem, pl.BlockSpec((BUCKETS, SIDE), lambda i: (0, 0))],
        out_specs=[
            pl.BlockSpec((None, queries, near), lambda i: (i, 0, 0)),
            pl.BlockSpec((None, near, queries), lambda i: (i, 0, 0)),
            pl.BlockSpec((seqs, keys, SIDE), lambda i: (0, 0, 0)),
        ],
        out_shape=[
            jax.ShapeDtypeStruct((HEADS, queries, near), bf16),
            jax.ShapeDtypeStruct((HEADS, near, queries), bf16),
            jax.ShapeDtypeStruct((seqs, keys, SIDE), bf16),
        ],
        scratch_shapes=[pltpu.VMEM((SIDE, 6 * HALF), f32)],
        cost_estimate=pl.CostEstimate(flops=6_000_000_000, bytes_accessed=7_000_000, transcendentals=0),
        name="prepare",
    )(rank, lengths, bias.astype(f32), lanes_bias)


def row_offset(rank, step, blocks):
    half = lax.rem(2 * rank - 1 + step + 2 * blocks, 2 * blocks)
    apart = jnp.bitwise_xor(rank, half // 2)
    slot = (apart % 2) * 2 + apart // 2
    return pl.multiple_of(slot * (2 * HALF) + (half % 2) * HALF, HALF)


def side_lanes(rows, picks):
    lane = lax.broadcasted_iota(jnp.int32, (rows, SIDE), 1)
    value = jnp.zeros((rows, SIDE), f32)
    for index, entry in picks:
        value = jnp.where(lane == index, entry, value)
    return value.astype(bf16)


def three_parts(value):
    high = value.astype(bf16).astype(f32)
    rest = value - high
    middle = rest.astype(bf16).astype(f32)
    return high, middle, rest - middle


def one_head(values, head):
    lane = lax.broadcasted_iota(jnp.int32, values.shape, 1)
    return jnp.where((lane // HEAD_DIM) == head, values, jnp.zeros_like(values))


def attend_kernel(rank_ref, q, k, v, side, bias, out, norm, kcat, vcat, *, near, blocks):
    rank = rank_ref[0]
    pair = pl.program_id(1)
    queries = q.shape[0]

    @pl.when(pair == 0)
    def _():
        kcat[:, SIDE:] = side[...]
        vcat[:, SIDE:] = side[...]
        norm[...] = jnp.zeros_like(norm)

    for step in range(2 * blocks):
        source = pl.ds(row_offset(rank, step, blocks), HALF)
        kcat[step * HALF : (step + 1) * HALF, :SIDE] = k[source, :]
        vcat[step * HALF : (step + 1) * HALF, :SIDE] = v[source, :]

    lane = lax.broadcasted_iota(jnp.int32, (queries, SIDE), 1)
    halves = []
    for head in range(2):
        index = 2 * pair + head
        extra = side_lanes(queries, [(0, 1.0), (1 + index, 1.0)])
        wide = jnp.concatenate([one_head(q[...], head), extra], axis=1)
        logits = nt(wide, kcat[...])
        close = logits[:, :near] + bias[head].astype(f32)
        away = logits[:, near:]
        top = jnp.maximum(
            jnp.max(close, axis=-1, keepdims=True), jnp.max(away, axis=-1, keepdims=True)
        )
        close = jnp.exp(close - top).astype(bf16)
        away = jnp.exp(away - top).astype(bf16)
        mixed = nn(close, vcat[:near, :]) + nn(away, vcat[near:, :])
        total = mixed[:, SIDE + ONES : SIDE + ONES + 1]
        halves.append(mixed[:, :SIDE] * (1.0 / total))
        norm[...] = jnp.where(lane == index, top + jnp.log(total), norm[...])
    out[...] = jnp.where(lane < HEAD_DIM, halves[0], halves[1]).astype(bf16)


def attend(rank, q, kv, side, bias):
    seqs, queries, _ = q.shape
    keys = kv.shape[1]
    near = bias.shape[-1]
    blocks = keys // queries
    return pl.pallas_call(
        partial(attend_kernel, near=near, blocks=blocks),
        grid=(seqs, PAIRS),
        in_specs=[
            pl.BlockSpec(memory_space=pltpu.SMEM),
            pl.BlockSpec((None, queries, SIDE), lambda s, i: (s, 0, i)),
            pl.BlockSpec((None, keys, SIDE), lambda s, i: (s, 0, i)),
            pl.BlockSpec((None, keys, SIDE), lambda s, i: (s, 0, i + PAIRS)),
            pl.BlockSpec((None, keys, SIDE), lambda s, i: (s, 0, 0)),
            pl.BlockSpec((2, queries, near), lambda s, i: (i, 0, 0)),
        ],
        out_specs=[
            pl.BlockSpec((None, queries, SIDE), lambda s, i: (s, 0, i)),
            pl.BlockSpec((None, queries, SIDE), lambda s, i: (s, 0, 0)),
        ],
        out_shape=[
            jax.ShapeDtypeStruct((seqs, queries, D), bf16),
            jax.ShapeDtypeStruct((seqs, queries, SIDE), f32),
        ],
        scratch_shapes=[pltpu.VMEM((keys, 2 * SIDE), bf16)] * 2,
        cost_estimate=pl.CostEstimate(flops=25_000_000_000, bytes_accessed=8_000_000, transcendentals=0),
        name="attend",
    )(rank, q, kv, kv, side, bias)


def attend_back_kernel(
    rank_ref, q, k, v, side, bias, norm, mixed, grad, *rest, near, blocks, part,
):
    dq, dk, dv, dnear, dfar, kcat, vcat, kturn = rest[-8:]
    rank = rank_ref[0]
    pair = pl.program_id(0)
    queries = q.shape[0]
    keys = k.shape[0]

    @pl.when(pair == 0)
    def _():
        kcat[:, SIDE:] = side[...]
        vcat[:, SIDE:] = side[...]
        kturn[SIDE:, :] = side[...].astype(f32).T[ONES : 2 * ONES, :].astype(bf16)

    for step in range(2 * blocks):
        source = pl.ds(row_offset(rank, step, blocks), HALF)
        kcat[step * HALF : (step + 1) * HALF, :SIDE] = k[source, :]
        vcat[step * HALF : (step + 1) * HALF, :SIDE] = v[source, :]
    kturn[:SIDE, :] = kcat[:, :SIDE].astype(f32).T.astype(bf16)

    lane = lax.broadcasted_iota(jnp.int32, (queries, SIDE), 1)
    queries_of, grads_of, wide_q, wide_g = [], [], [], []
    products = grad[...].astype(f32) * mixed[...].astype(f32)
    for head in range(2):
        index = 2 * pair + head
        level = jnp.sum(jnp.where(lane == index, norm[...], 0.0), axis=-1, keepdims=True)
        delta = jnp.sum(
            jnp.where((lane // HEAD_DIM) == head, products, 0.0), axis=-1, keepdims=True
        )
        la, lb, lc = three_parts(-level)
        da, db, dc = three_parts(-delta)
        queries_of.append(one_head(q[...], head))
        grads_of.append(one_head(grad[...], head))
        extra = [(0, 1.0), (1 + index, 1.0), (ONES, la), (ONES + 1, lb), (ONES + 2, lc)]
        wide_q.append(jnp.concatenate([queries_of[head], side_lanes(queries, extra)], axis=1))
        extra = [(ONES, da), (ONES + 1, db), (ONES + 2, dc)]
        wide_g.append(jnp.concatenate([grads_of[head], side_lanes(queries, extra)], axis=1))

    sums = [jnp.zeros((kturn.shape[0], queries), f32) for _ in range(2)]
    for base in range(0, keys, part):
        span = slice(base, base + part)
        value_part = jnp.zeros((part, SIDE), f32)
        key_part = jnp.zeros((part, SIDE), f32)
        for head in range(2):
            logits = nt(kcat[span, :], wide_q[head])
            if base < near:
                logits = logits + bias[head, span, :].astype(f32)
            probs = jnp.exp(logits)
            pull = nt(vcat[span, :], wide_g[head])
            low = (probs * pull).astype(bf16)
            value_part += nn(probs.astype(bf16), grads_of[head])
            key_part += nn(low, queries_of[head])
            sums[head] += nn(kturn[:, span], low)
            if base < near:
                dnear[head, span, :] = low
        for step in range(base // HALF, (base + part) // HALF):
            target = pl.ds(row_offset(rank, step, blocks), HALF)
            inner = slice(step * HALF - base, (step + 1) * HALF - base)
            dk[target, :] = key_part[inner].astype(bf16)
            dv[target, :] = value_part[inner].astype(bf16)
    turned = jnp.concatenate([sums[0][:HEAD_DIM], sums[1][HEAD_DIM:SIDE]], axis=0)
    dq[...] = turned.T.astype(bf16)
    for head in range(2):
        dfar[head] = sums[head][SIDE:, :]


def attend_back(seq, rank, q, kv, side, bias, norm, mixed, grad, earlier):
    seqs, queries, _ = q.shape
    keys = kv.shape[1]
    near = bias.shape[1]
    blocks = keys // queries
    own = pl.BlockSpec((None, queries, SIDE), lambda i: (seq, 0, i))
    every = pl.BlockSpec((None, keys, SIDE), lambda i: (seq, 0, i))
    return pl.pallas_call(
        partial(attend_back_kernel, near=near, blocks=blocks, part=2 * HALF),
        grid=(PAIRS,),
        in_specs=[
            pl.BlockSpec(memory_space=pltpu.SMEM),
            own,
            every,
            pl.BlockSpec((None, keys, SIDE), lambda i: (seq, 0, i + PAIRS)),
            pl.BlockSpec((None, keys, SIDE), lambda i: (seq, 0, 0)),
            pl.BlockSpec((2, near, queries), lambda i: (i, 0, 0)),
            pl.BlockSpec((None, queries, SIDE), lambda i: (seq, 0, 0)),
            own,
            own,
        ]
        + [pl.BlockSpec(memory_space=pl.ANY)] * len(earlier),
        out_specs=[
            own,
            every,
            every,
            pl.BlockSpec((None, 2, near, queries), lambda i: (seq, i, 0, 0)),
            pl.BlockSpec((None, 2, ONES, queries), lambda i: (seq, i, 0, 0)),
        ],
        out_shape=[
            jax.ShapeDtypeStruct((seqs, queries, D), bf16),
            jax.ShapeDtypeStruct((seqs, keys, D), bf16),
            jax.ShapeDtypeStruct((seqs, keys, D), bf16),
            jax.ShapeDtypeStruct((seqs, HEADS, near, queries), bf16),
            jax.ShapeDtypeStruct((seqs, HEADS, ONES, queries), f32),
        ],
        scratch_shapes=[
            pltpu.VMEM((keys, 2 * SIDE), bf16),
            pltpu.VMEM((keys, 2 * SIDE), bf16),
            pltpu.VMEM((SIDE + ONES, keys), bf16),
        ],
        input_output_aliases={9 + i: i for i in range(len(earlier))},
        cost_estimate=pl.CostEstimate(flops=15_000_000_000, bytes_accessed=12_000_000, transcendentals=0),
        name="attend_back",
    )(rank, q, kv, kv, side, bias, norm, mixed, grad, *earlier)


def bias_grad_kernel(rank_ref, near, far, out, hot, *, parts):
    rank = rank_ref[0]
    seqs = near.shape[0]
    steps = near.shape[1] // HALF - 2

    @pl.when(pl.program_id(0) == 0)
    def _():
        place = lax.broadcasted_iota(jnp.int32, hot.shape, 0)
        lane = lax.broadcasted_iota(jnp.int32, hot.shape, 1)
        segment = place // (2 * HALF)
        relative = (segment - 1) * HALF + HALF - 1 - lax.rem(place, 2 * HALF)
        bucket = jnp.where(segment == 3, 15, jnp.where(segment == 4, 31, bucket_of(relative)))
        hot[...] = (bucket == lane).astype(bf16)

    row = lax.broadcasted_iota(jnp.int32, (HALF, HALF), 0)
    lane = lax.broadcasted_iota(jnp.int32, (HALF, HALF), 1)
    flip = (row + lane == HALF - 1).astype(bf16)
    ones = jnp.ones((8, HALF), bf16)
    first_in, last_in = rank != 0, rank != parts - 1

    def block(s, n, q):
        return near[s, n * HALF : (n + 1) * HALF, q * HALF : (q + 1) * HALF]

    sums = [jnp.zeros((HALF, HALF), f32) for _ in range(3)]
    left = [far[s, LEFT - ONES : LEFT - ONES + 1, :] for s in range(seqs)]
    right = [far[s, RIGHT - ONES : RIGHT - ONES + 1, :] for s in range(seqs)]
    left, right = sum(left), sum(right)
    for n in range(steps + 2):
        inside = first_in if n == 0 else last_in if n == steps + 1 else None
        tails = []
        for q in range(steps):
            apart = n - 1 - q
            if abs(apart) <= 1:
                value = sum(nn(flip, block(s, n, q)) for s in range(seqs))
                if inside is not None:
                    value = jnp.where(inside, value, 0.0)
                sums[apart + 1] += value
        if inside is not None:
            span = slice(n * HALF, (n + 1) * HALF)
            column = sum(nn(ones, near[s, span, :]) for s in range(seqs))[:1]
            at = lax.broadcasted_iota(jnp.int32, column.shape, 1) // HALF
            outside = (n - 1 - at < -1) | (n - 1 - at > 1)
            kept = jnp.where(outside, column, 0.0)
            if n == 0:
                left += jnp.where(inside, kept, 0.0)
                right += jnp.where(inside, 0.0, column)
            else:
                right += jnp.where(inside, kept, 0.0)
                left += jnp.where(inside, 0.0, column)
    lines = []
    for value in sums:
        wide = jnp.concatenate([value, jnp.zeros((HALF, HALF), f32)], axis=1)
        rolled = pltpu.roll(wide, 0, 1, stride=1, stride_axis=0)
        lines.append(jnp.sum(rolled, axis=0, keepdims=True))
    line = jnp.concatenate(lines + [left, right], axis=1)
    line = jnp.broadcast_to(line, (8, line.shape[1]))
    total = sum(nn(part.astype(bf16), hot[...]) for part in three_parts(line))
    out[...] = total[:1]


def bias_sums(rank, near_parts, far_parts, parts):
    seqs, heads, near, queries = near_parts.shape
    return pl.pallas_call(
        partial(bias_grad_kernel, parts=parts),
        grid=(heads,),
        in_specs=[
            pl.BlockSpec(memory_space=pltpu.SMEM),
            pl.BlockSpec((seqs, None, near, queries), lambda i: (0, i, 0, 0)),
            pl.BlockSpec((seqs, None, ONES, queries), lambda i: (0, i, 0, 0)),
        ],
        out_specs=pl.BlockSpec((None, 1, 128), lambda i: (i, 0, 0)),
        out_shape=jax.ShapeDtypeStruct((heads, 1, 128), f32),
        scratch_shapes=[pltpu.VMEM((10 * HALF, 128), bf16)],
        cost_estimate=pl.CostEstimate(flops=6_000_000_000, bytes_accessed=9_000_000, transcendentals=0),
        name="bias_sums",
    )(rank, near_parts, far_parts)


def gelu_parts(x):
    inner = 0.7978845608028654 * (x + 0.044715 * (x * x * x))
    t = jnp.tanh(inner)
    half = 0.5 * (1.0 + t)
    slope = half + 0.5 * x * (1.0 - t * t) * (
        0.7978845608028654 * (1.0 + 0.134145 * (x * x))
    )
    return x * half, slope


def feed_kernel(
    place_ref, count_ref, lengths_ref, att, resid, teacher, gain, gate_w, up_w, down_w, output_w,
    block_out, normed, hidden, branch, gate_low, up_low, after_grad, after_low, att_grad, stats,
    act, steep, *, chunk,
):
    step = pl.program_id(0)
    rows = att.shape[0]
    ffn_dim = gate_w.shape[1]

    @pl.when(step == 0)
    def _():
        stats[...] = jnp.zeros_like(stats)

    after = resid[...] + nn(att[...], output_w[...])
    scale = lax.rsqrt(jnp.mean(after * after, axis=-1, keepdims=True) + epsilon)
    normed[...] = (after * scale * gain[...]).astype(bf16)
    out = after
    for base in range(0, ffn_dim, chunk):
        span = slice(base, base + chunk)
        gate = nn(normed[...], gate_w[:, span])
        up_part = nn(normed[...], up_w[:, span])
        value, slope = gelu_parts(gate)
        act[:, span] = value
        steep[:, span] = slope * up_part
        low = (value * up_part).astype(bf16)
        hidden[:, span] = low
        out = out + nn(low, down_w[span, :])
    block_out[...] = out
    token = place_ref[0] + lax.broadcasted_iota(jnp.int32, (rows, D), 0)
    live = (2 * token < lengths_ref[step]).astype(f32)
    error = live * (out - teacher[...])
    stats[1:2, :] += jnp.sum(error * error, axis=0, keepdims=True)
    out_grad = (2.0 / count_ref[0]) * error
    branch[...] = out_grad.astype(bf16)
    back = jnp.zeros((rows, D), f32)
    for base in range(0, ffn_dim, chunk):
        span = slice(base, base + chunk)
        pull = nt(branch[...], down_w[span, :])
        gate_part = (pull * steep[:, span]).astype(bf16)
        up_part = (pull * act[:, span]).astype(bf16)
        gate_low[:, span] = gate_part
        up_low[:, span] = up_part
        back = back + nt(gate_part, gate_w[:, span]) + nt(up_part, up_w[:, span])
    stats[0:1, :] += jnp.sum(back * after * scale, axis=0, keepdims=True)
    gained = back * gain[...]
    inner = jnp.mean(gained * after, axis=-1, keepdims=True)
    total = out_grad + scale * gained - after * (scale * scale * scale * inner)
    after_grad[...] = total
    low = total.astype(bf16)
    after_low[...] = low
    att_grad[...] = nt(low, output_w[...]).astype(bf16)


def feed(place, count, lengths, att, resid, teacher, gain, wide, down_w):
    tokens = att.shape[0]
    seqs = lengths.shape[0]
    rows = tokens // seqs
    ffn_dim = down_w.shape[0]
    once = pl.Buffered(1)
    own = pl.BlockSpec((rows, D), lambda i: (i, 0))
    broad = pl.BlockSpec((rows, ffn_dim), lambda i: (i, 0))
    smem = pl.BlockSpec(memory_space=pltpu.SMEM)
    return pl.pallas_call(
        partial(feed_kernel, chunk=512),
        grid=(seqs,),
        in_specs=[
            smem,
            smem,
            smem,
            own,
            pl.BlockSpec((None, rows, D), lambda i: (i, 0, 0)),
            own,
            pl.BlockSpec((1, D), lambda i: (0, 0)),
            pl.BlockSpec((D, ffn_dim), lambda i: (0, 0), pipeline_mode=once),
            pl.BlockSpec((D, ffn_dim), lambda i: (0, 1), pipeline_mode=once),
            pl.BlockSpec((ffn_dim, D), lambda i: (0, 0), pipeline_mode=once),
            pl.BlockSpec((D, D), lambda i: (0, 3 * ffn_dim // D), pipeline_mode=once),
        ],
        out_specs=[own, own, broad, own, broad, broad, own, own, own, pl.BlockSpec((8, D), lambda i: (0, 0))],
        out_shape=[
            jax.ShapeDtypeStruct((tokens, D), f32),
            jax.ShapeDtypeStruct((tokens, D), bf16),
            jax.ShapeDtypeStruct((tokens, ffn_dim), bf16),
            jax.ShapeDtypeStruct((tokens, D), bf16),
            jax.ShapeDtypeStruct((tokens, ffn_dim), bf16),
            jax.ShapeDtypeStruct((tokens, ffn_dim), bf16),
            jax.ShapeDtypeStruct((tokens, D), f32),
            jax.ShapeDtypeStruct((tokens, D), bf16),
            jax.ShapeDtypeStruct((tokens, D), bf16),
            jax.ShapeDtypeStruct((8, D), f32),
        ],
        scratch_shapes=[pltpu.VMEM((rows, ffn_dim), f32)] * 2,
        cost_estimate=pl.CostEstimate(flops=17_000_000_000, bytes_accessed=30_000_000, transcendentals=0),
        name="feed",
    )(place, count, lengths, att, resid, teacher, gain, wide, wide, down_w, wide)


def dot(a, b):
    return jnp.dot(a, b, preferred_element_type=f32)


def per_device(
    byte_ids,
    lengths,
    teacher,
    embed_table,
    conv_weight,
    score_weight,
    attn_gain,
    rel_bias,
    query_weight,
    key_weight,
    value_weight,
    output_weight,
    ffn_gain,
    gate_weight,
    up_weight,
    down_weight,
):
    seqs, own_bytes = byte_ids.shape
    own = own_bytes // 2
    parts = lax.axis_size("seq")
    dp_size = lax.axis_size("dp")
    rank = lax.axis_index("seq")
    total_tokens, total_bytes = own * parts, own_bytes * parts
    shard = score_weight.shape[0]
    rank_ref = rank.reshape(1).astype(jnp.int32)

    live_here = jnp.sum(jnp.minimum((lengths + 1) // 2, total_tokens))
    live_here = jnp.where(rank == 0, live_here, 0)
    counts = jnp.stack([live_here // 64, live_here % 64])
    at_count = (jnp.arange(shard) == 0).astype(jnp.int32)
    columns = jnp.concatenate(
        [
            embed_table,
            conv_weight,
            score_weight[None],
            attn_gain[None],
            ffn_gain[None],
            (counts[:, None] * at_count[None]).astype(bf16),
            jnp.zeros((TABLE - VOCAB - 9, shard), bf16),
        ],
        axis=0,
    ).T
    ids_low = jnp.stack([byte_ids // 16, byte_ids % 16]).astype(bf16)
    id_rows = ids_low.reshape(-1, TABLE)
    attn_rows = jnp.concatenate([query_weight, key_weight, value_weight], axis=1)
    cut = attn_rows.shape[1] // 2
    qkv_halves = [
        RowGather(attn_rows[:, :cut], gather_order("y")),
        RowGather(attn_rows[:, cut:], gather_order("x")),
    ]
    small = RowGather(columns, axis_bits("dp"))
    while small.order:
        small.start()
        for each in qkv_halves:
            each.finish()
            if len(each.order) > 3:
                each.start()
        small.finish()
    value = small.value.reshape(-1, TABLE)
    mine = jnp.concatenate([value, id_rows], axis=0)
    x_other = swap(mine, "seq", 2)
    pair = jnp.concatenate([mine, x_other], axis=0)
    c_other = swap(pair, "seq", 1)
    wide_rows = mine.shape[0]
    quarters = jnp.concatenate([pair, c_other], axis=0).reshape(parts, wide_rows, TABLE)
    apart = jnp.bitwise_xor(rank, jnp.arange(parts))
    slots = (apart % 2) * 2 + apart // 2
    ordered = jnp.take(quarters, slots, axis=0)
    table = (
        ordered[:, : dp_size * shard]
        .reshape(parts, dp_size, shard, TABLE)
        .transpose(1, 0, 2, 3)
        .reshape(D, TABLE)
    )
    all_ids = ordered[:, dp_size * shard :].reshape(parts, 2, seqs, own_bytes).astype(jnp.int32)
    all_ids = (all_ids[:, 0] * 16 + all_ids[:, 1]).transpose(1, 0, 2).reshape(seqs, total_bytes)
    counts = jnp.sum(table[:, VOCAB + 7 : VOCAB + 9].astype(f32), axis=0)
    live_count = counts[0] * 64.0 + counts[1]
    ffn_gain_full = table[:, VOCAB + 6].astype(f32)

    padded_ids = jnp.pad(all_ids, ((0, 0), (32, 32)), constant_values=-1)
    first_byte = (rank * own_bytes).astype(jnp.int32)
    first_other = (jnp.bitwise_xor(rank, 2) * own_bytes).astype(jnp.int32)

    def phases(start):
        window = lax.dynamic_slice_in_dim(padded_ids, start, own_bytes + 64, 1)
        return window.reshape(seqs, -1, 4).transpose(0, 2, 1).reshape(seqs, -1)

    phase_ids = phases(first_byte)
    other_ids = phases(first_other)

    ffn_dim = gate_weight.shape[1]
    tiled = down_weight.shape[0] % 64 == 0
    third = D // 3
    if tiled:
        down_packed = down_weight.reshape(-1, 8, 8, 3, third).transpose(0, 3, 2, 1, 4)
    else:
        down_packed = down_weight
    down_packed = down_packed.reshape(shard, ffn_dim)
    packed = jnp.concatenate([gate_weight, up_weight, down_packed, output_weight], axis=1)
    wide_full = lax.all_gather(packed, both, axis=0, tiled=True)
    down_full = wide_full[:, 2 * ffn_dim : 3 * ffn_dim]
    if tiled:
        down_full = down_full.reshape(-1, 3, 8, 8, third).transpose(0, 3, 2, 1, 4)
    down_full = down_full.reshape(ffn_dim, D)

    for each in qkv_halves:
        each.start()
    residual, normed_own = pool(first_byte.reshape(1), phase_ids[:, :, None], table, total_bytes)
    for each in qkv_halves:
        each.finish(normed_own)
        each.start()
    other_first = after(first_other.reshape(1), normed_own)
    _, normed_x = pool(other_first, other_ids[:, :, None], table, total_bytes)
    normed_two = jnp.concatenate([normed_own, normed_x], axis=1)
    normed_other = swap(normed_two, "seq", 1)
    tile, turned_tile, side = prepare(
        after(rank_ref, normed_x), lengths, rel_bias, own, total_tokens, parts
    )
    for each in qkv_halves:
        each.finish(tile)
        each.start()
        each.finish()
    qkv_full = jnp.concatenate(
        [each.result().reshape(D, cut) for each in qkv_halves], axis=1
    )
    query_full, kv_full = qkv_full[:, :D], qkv_full[:, D:]
    key_full, value_full = qkv_full[:, D : 2 * D], qkv_full[:, 2 * D :]
    normed = jnp.concatenate([normed_two, normed_other], axis=1)
    own_rows = normed_own.reshape(-1, D)
    queries = dot(own_rows, query_full).astype(bf16).reshape(seqs, own, D)
    pairs_kv = dot(normed.reshape(-1, D), kv_full).astype(bf16).reshape(seqs, total_tokens, 2 * D)
    attended, norms = attend(rank_ref, queries, pairs_kv, side, tile)

    token_rows = seqs * own
    att = attended.reshape(token_rows, D)
    (
        block_out, ffn_in, hidden, branch_grad, gate_low, up_low, after_grad, after_low,
        attended_grad, feed_stats,
    ) = feed(
        (rank * own).reshape(1), live_count.reshape(1), lengths, att,
        residual, teacher.reshape(token_rows, D), ffn_gain_full[None],
        wide_full, down_full,
    )
    down_grad = jnp.einsum("tf,td->fd", hidden, branch_grad, preferred_element_type=f32)
    gate_grad = jnp.einsum("td,tf->df", ffn_in, gate_low, preferred_element_type=f32)
    up_grad = jnp.einsum("td,tf->df", ffn_in, up_low, preferred_element_type=f32)
    output_grad = jnp.einsum("td,te->de", att, after_low, preferred_element_type=f32).astype(bf16)
    down_sum = RowSum(down_grad.astype(bf16)[None], sum_order("z"))
    gate_sum = RowSum(gate_grad.astype(bf16)[None], sum_order("x"))
    up_sum = RowSum(up_grad.astype(bf16)[None], sum_order("y"))
    feed_sums = (down_sum, gate_sum, up_sum)
    for each in feed_sums:
        each.start()
    turn = after_sends(after(attended_grad, output_grad), *feed_sums).reshape(seqs, own, D)

    made = ()
    for s in range(seqs):
        made = attend_back(
            s, rank_ref, queries, pairs_kv, side, turned_tile, norms, attended, turn, made
        )
        for each in feed_sums:
            each.finish(made[4])
            each.start()
        if s < seqs - 1:
            turn = after_sends(turn, *feed_sums)
    dq, dk, dv, near_parts, far_parts = made
    dk_rows, dv_rows = dk.reshape(-1, D), dv.reshape(-1, D)
    dk_rows = after_sends(dk_rows, *feed_sums)
    pulled = (
        jnp.einsum("te,de->td", dk_rows, key_full, preferred_element_type=f32)
        + jnp.einsum("te,de->td", dv_rows, value_full, preferred_element_type=f32)
    ).reshape(seqs, total_tokens, D)
    direct = jnp.einsum(
        "te,de->td", dq.reshape(-1, D), query_full, preferred_element_type=f32
    ).reshape(seqs, own, D)
    from_core = swap(pulled[:, 2 * own :].astype(bf16), "seq", 1)
    normed_rows = normed.reshape(-1, D)
    key_grad = jnp.einsum(
        "td,te->de", normed_rows, after(dk_rows, pulled), preferred_element_type=f32
    ).astype(bf16)
    from_core = after(from_core, key_grad)
    chip = pulled[:, : 2 * own] + from_core.astype(f32)
    from_x = swap(chip[:, own:].astype(bf16), "seq", 2)
    for each in feed_sums:
        each.finish(key_grad)
        each.start()
    dv_rows = after_sends(after(dv_rows, chip), *feed_sums)
    value_grad = jnp.einsum("td,te->de", normed_rows, dv_rows, preferred_element_type=f32)
    query_grad = jnp.einsum(
        "td,te->de", own_rows, after(dq.reshape(-1, D), chip), preferred_element_type=f32
    )
    attn_sum = RowSum(
        jnp.stack([query_grad.astype(bf16), key_grad, value_grad.astype(bf16), output_grad]),
        sum_order("y"),
    )
    attn_sum.start()
    bias_rows = bias_sums(rank_ref, after_sends(near_parts, attn_sum), far_parts, parts)
    attn_sum.finish(bias_rows)
    attn_sum.start()
    from_x = after_sends(after(from_x, bias_rows), attn_sum)
    normed_grad = chip[:, :own] + direct + from_x.astype(f32)
    shared = SumEverywhere(
        jnp.concatenate(
            [
                bias_rows.reshape(HEADS, 128),
                jnp.broadcast_to(jnp.sum(feed_stats[1]), (16 - HEADS, 128)),
            ],
            axis=0,
        )
    )
    shared.start()

    embed_part, small_part = 0.0, 0.0
    for s in range(seqs):
        a, b = pool_back(
            s, first_byte.reshape(1), phase_ids[:, :, None], phase_ids[:, None, :], table,
            normed_grad, residual, after_grad.reshape(seqs, own, D), total_bytes,
        )
        embed_part, small_part = embed_part + a, small_part + b
        attn_sum.finish(b)
        shared.finish(b)
        attn_sum.start()
        shared.start()
        if s < seqs - 1:
            normed_grad = after(after_sends(normed_grad, attn_sum), shared.value)
    front = jnp.concatenate(
        [
            embed_part[:VOCAB],
            small_part[:6],
            feed_stats[:1],
            jnp.zeros((TABLE - VOCAB - 7, D), f32),
        ],
        axis=0,
    )
    front_sum = RowSum(front.T[None], sum_order("x"))
    front_sum = front_sum.result().reshape(shard, TABLE).T
    sums = shared.result()
    bias_grad = sums[:HEADS, :BUCKETS].T
    attn_sum = attn_sum.result()
    gate_sum, up_sum, down_sum = [each.result()[0] for each in (gate_sum, up_sum, down_sum)]

    return (
        block_out.reshape(seqs, own, D),
        sums[HEADS, 0] / live_count,
        front_sum[:VOCAB],
        front_sum[VOCAB : VOCAB + 4],
        front_sum[VOCAB + 4],
        front_sum[VOCAB + 5],
        bias_grad,
        attn_sum[0],
        attn_sum[1],
        attn_sum[2],
        attn_sum[3],
        front_sum[VOCAB + 6],
        gate_sum,
        up_sum,
        down_sum,
    )


def solution(mesh):
    tokens = P("dp", "seq", None)
    features = P(("dp", "seq"))
    columns = P(None, ("dp", "seq"))
    rows = P(("dp", "seq"), None)
    in_specs = (
        P("dp", "seq"), P("dp"), tokens, columns, columns, features, features, P(),
        rows, rows, rows, rows, features, rows, rows, rows,
    )
    out_specs = (
        tokens, P(), columns, columns, features, features, P(), rows, rows, rows, rows,
        features, rows, rows, rows,
    )
    return jax.shard_map(
        per_device, mesh=mesh, in_specs=in_specs, out_specs=out_specs, check_vma=False
    )
```

```python
from functools import partial

import jax
import jax.numpy as jnp
from jax import lax
from jax.experimental import pallas as pl
from jax.experimental.pallas import tpu as pltpu
from jax.sharding import PartitionSpec as P

D = 768
HEADS = 12
HEAD_DIM = 64
VOCAB = 259
BUCKETS = 32
TABLE = 384
PAIRS = HEADS // 2
SIDE = 128
ONES = 16
LEFT = 20
RIGHT = 21
HALF = 128
KEY_PART = 1024

epsilon = 1e-06
thresholds = (12, 16, 23, 32, 46, 64, 91)
masked_score = -1000000000.0
highest = lax.Precision.HIGHEST
bf16 = jnp.bfloat16
f32 = jnp.float32
both = ("dp", "seq")


def nt(a, b):
    return lax.dot_general(a, b, (((1,), (1,)), ((), ())), preferred_element_type=f32)


def nn(a, b):
    return lax.dot_general(a, b, (((1,), (0,)), ((), ())), preferred_element_type=f32)


def bucket_of(relative):
    distance = jnp.abs(relative)
    far_bucket = 8 + sum(((distance >= border).astype(jnp.int32) for border in thresholds))
    return jnp.where(relative > 0, 16, 0).astype(jnp.int32) + jnp.where(
        distance < 8, distance, far_bucket
    )


def hot_buckets(relative):
    return (bucket_of(relative)[..., None] == jnp.arange(BUCKETS, dtype=jnp.int32)).astype(f32)


def swap(value, axis, bit):
    peers = lax.axis_size(axis)
    return lax.ppermute(value, axis, [(i, i ^ bit) for i in range(peers)])


def axis_bits(axis):
    bits, bit = [], lax.axis_size(axis) // 2
    while bit:
        bits.append((axis, bit))
        bit //= 2
    return bits


def my_bit(axis, bit):
    return (lax.axis_index(axis) // bit) % 2


def gather_stage(value, axis, bit, position):
    other = swap(value, axis, bit)
    upper = my_bit(axis, bit) == 1
    return jnp.stack(
        [jnp.where(upper, other, value), jnp.where(upper, value, other)], axis=position
    )


class RowGather:
    def __init__(self, rows, order):
        self.value = rows
        self.order = list(order)
        self.places = axis_bits("dp") + axis_bits("seq")
        self.done = []
        self.got = None

    def start(self):
        if self.order:
            self.stage = self.order.pop(0)
            self.got = swap(self.value, *self.stage)

    def finish(self, *others):
        if self.got is None:
            return
        got = after(self.got, *others) if others else self.got
        self.got = None
        place = self.places.index(self.stage)
        position = sum(p < place for p in self.done)
        self.done.append(place)
        upper = my_bit(*self.stage) == 1
        self.value = jnp.stack(
            [jnp.where(upper, got, self.value), jnp.where(upper, self.value, got)],
            axis=position,
        )

    def result(self):
        self.finish()
        while self.order:
            self.start()
            self.finish()
        return self.value


def gather_order(first_axis):
    seq, dp = axis_bits("seq"), axis_bits("dp")
    if first_axis == "y":
        return dp + seq
    return dp[:-1] + seq[:-1] + dp[-1:] + seq[-1:]


def after(value, *others):
    return lax.optimization_barrier((value,) + others)[0]


def hold(value, other):
    return value + (other[(0,) * other.ndim] * 0).astype(value.dtype)


def sum_order(first):
    seq, dp = axis_bits("seq")[::-1], axis_bits("dp")[::-1]
    if first == "x":
        return seq + dp
    if first == "y":
        return seq[:1] + dp[:1] + seq[1:] + dp[1:]
    return seq[:1] + dp[1:] + dp[:1] + seq[1:]


class RowSum:
    def __init__(self, total, order):
        self.parts = [total]
        self.left = axis_bits("dp") + axis_bits("seq")
        self.order = list(order)
        self.sent = self.got = None

    def start(self):
        if not self.order:
            return
        axis, bit = self.order.pop(0)
        position = self.left.index((axis, bit))
        self.left.remove((axis, bit))
        mine = my_bit(axis, bit)

        def half(value, which):
            lead, rows, cols = value.shape
            outer = lead << position
            cut = value.reshape(outer, 2, lead * rows // (2 * outer), cols)
            picked = lax.dynamic_index_in_dim(cut, which, 1, keepdims=False)
            return picked.reshape(lead, rows // 2, cols)

        send = sum(half(value, 1 - mine).astype(f32) for value in self.parts)
        self.sent = send.astype(bf16)
        self.parts = [half(value, mine) for value in self.parts]
        self.got = swap(self.sent, axis, bit)

    def finish(self, other=None, hard=False):
        if self.got is not None:
            order = hold if hard else after
            self.parts.append(self.got if other is None else order(self.got, other))
            self.got = None

    def result(self):
        self.finish()
        while self.order:
            self.start()
            self.finish()
        return sum(value.astype(f32) for value in self.parts)


def after_sends(value, *sums):
    sends = [each.sent for each in sums if each.sent is not None]
    return after(value, *sends)


class SumEverywhere:
    def __init__(self, value):
        self.value = value
        self.order = axis_bits("seq")[::-1] + axis_bits("dp")[::-1]
        self.got = None

    def start(self):
        if self.order:
            self.got = swap(self.value, *self.order.pop(0))

    def finish(self, *others):
        if self.got is not None:
            self.value = self.value + (after(self.got, *others) if others else self.got)
            self.got = None

    def result(self):
        self.finish()
        while self.order:
            self.start()
            self.finish()
        return self.value


def pack_kernel(
    rank_ref, lengths_ref, table, taps, scorer, gain_a, gain_f, query, key, value, gate, up, down,
    output, columns, first_half, second_half, packed, rows, *, total_tokens,
):
    shard = table.shape[1]
    live = jnp.int32(0)
    for s in range(lengths_ref.shape[0]):
        live += jnp.minimum((lengths_ref[s] + 1) // 2, total_tokens)
    live = jnp.where(rank_ref[0] == 0, live, 0)
    first = lax.broadcasted_iota(jnp.int32, (1, shard), 1) == 0
    rows[...] = jnp.zeros_like(rows)
    rows[0:VOCAB, 0:shard] = table[...].astype(f32)
    rows[VOCAB : VOCAB + 4, 0:shard] = taps[...].astype(f32)
    for i, vector in enumerate((scorer, gain_a, gain_f)):
        rows[VOCAB + 4 + i : VOCAB + 5 + i, 0:shard] = vector[...].astype(f32)
    for i, part in enumerate((live // 64, live % 64)):
        at = VOCAB + 7 + i
        rows[at : at + 1, 0:shard] = jnp.where(first, part, 0).astype(f32)
    columns[...] = rows[...].T[0:shard, :].astype(bf16)

    pieces = [query[:, i * SIDE : (i + 1) * SIDE] for i in range(PAIRS)]
    for i in range(PAIRS):
        pieces += [key[:, i * SIDE : (i + 1) * SIDE], value[:, i * SIDE : (i + 1) * SIDE]]
    for half in (first_half, second_half):
        count = half.shape[1] // SIDE
        for i in range(count):
            half[:, i * SIDE : (i + 1) * SIDE] = pieces.pop(0)

    ffn_dim = gate.shape[1]
    packed[:, 0:ffn_dim] = gate[...]
    packed[:, ffn_dim : 2 * ffn_dim] = up[...]
    packed[:, 3 * ffn_dim :] = output[...]
    third = D // 3
    wide = down[...].astype(f32)
    for group in range(down.shape[0] // 64):
        for i in range(8):
            at = group * 64 + i * 8
            tiles = [wide[at : at + 8, j * third : (j + 1) * third] for j in range(3)]
            start = 2 * ffn_dim + i * third
            packed[group * 24 : (group + 1) * 24, start : start + third] = jnp.concatenate(
                tiles, axis=0
            ).astype(bf16)


def pack(rank, lengths, table, taps, vectors, attn, feed_weights, total_tokens):
    smem = pl.BlockSpec(memory_space=pltpu.SMEM)
    vmem = pl.BlockSpec(memory_space=pltpu.VMEM)
    shard, ffn_dim = table.shape[1], feed_weights[0].shape[1]
    shapes = [(shard, TABLE), (shard, 3 * D // 2), (shard, 3 * D // 2), (shard, 3 * ffn_dim + D)]
    return pl.pallas_call(
        partial(pack_kernel, total_tokens=total_tokens),
        in_specs=[smem, smem] + [vmem] * 12,
        out_specs=[vmem] * 4,
        out_shape=[jax.ShapeDtypeStruct(shape, bf16) for shape in shapes],
        scratch_shapes=[pltpu.VMEM((TABLE, -(-shard // 128) * 128), f32)],
        cost_estimate=pl.CostEstimate(flops=100_000_000, bytes_accessed=1_000_000, transcendentals=0),
        name="pack",
    )(rank, lengths, table, taps, *vectors, *attn, *feed_weights)


def pack_plain(rank, lengths, table, taps, vectors, attn, feed_weights, total_tokens):
    shard = table.shape[1]
    live = jnp.sum(jnp.minimum((lengths + 1) // 2, total_tokens))
    live = jnp.where(rank[0] == 0, live, 0)
    counts = jnp.stack([live // 64, live % 64])
    at_count = (jnp.arange(shard) == 0).astype(jnp.int32)
    columns = jnp.concatenate(
        [table, taps, *vectors, (counts[:, None] * at_count[None]).astype(bf16)], axis=0
    )
    columns = jnp.pad(columns, ((0, TABLE - columns.shape[0]), (0, 0))).T
    query, key, value = attn
    pairs = jnp.stack([key.reshape(shard, PAIRS, SIDE), value.reshape(shard, PAIRS, SIDE)], axis=2)
    rows = jnp.concatenate([query, pairs.reshape(shard, 2 * D)], axis=1)
    gate, up, down, output = feed_weights
    packed = jnp.concatenate([gate, up, down.reshape(shard, gate.shape[1]), output], axis=1)
    return columns, rows[:, : 3 * D // 2], rows[:, 3 * D // 2 :], packed


def up(x):
    return pltpu.roll(x, x.shape[0] - 1, 0)


def down(x):
    return pltpu.roll(x, 1, 0)


def ahead_lane(x):
    return pltpu.roll(x, x.shape[1] - 1, 1)


def behind_lane(x):
    return pltpu.roll(x, 1, 1)


def triples(c, m0, m1):
    c0, c1, c2, c3 = c
    p01, p23 = c0 + c1, c2 + c3
    t0, t1, t2, t3 = behind_lane(c3) + p01, p01 + c2, c1 + p23, p23 + ahead_lane(c0)
    before, after = (behind_lane(t3), t0, t1, t2), (t1, t2, t3, ahead_lane(t0))
    here = (t0, t1, t2, t3)
    return tuple(
        jnp.where(m0[k], after[k], jnp.where(m1[k], here[k], before[k])) for k in range(4)
    )


def live_rows(first, rows, total_bytes):
    row = lax.broadcasted_iota(jnp.int32, (rows, 128), 0)
    live = []
    for k in range(4):
        pos = first + 4 * (row - 8) + k
        live.append(((pos >= 0) & (pos < total_bytes)).astype(f32))
    return live


def lane_marks(first, wide, total_bytes):
    row = lax.broadcasted_iota(jnp.int32, (1, wide), 1)
    live, m0, m1 = [], [], []
    for k in range(4):
        pos = first + 4 * (row - 8) + k
        live.append(((pos >= 0) & (pos < total_bytes)).astype(f32))
        shifted = (pos + 48).astype(f32)
        third = jnp.floor((shifted + 0.5) * (1.0 / 3.0))
        rest = shifted - 3.0 * third
        m0.append(rest < 0.5)
        m1.append((rest > 0.5) & (rest < 1.5))
    return live, m0, m1


def to_lanes(accs, count, flat):
    rows = accs.shape[1]
    lane = lax.broadcasted_iota(jnp.int32, (rows, 128), 1)
    value = jnp.zeros((rows, 128), f32)
    for k in range(count):
        value = jnp.where(lane == k, jnp.sum(accs[k], axis=-1, keepdims=True), value)
    flat[0:rows, :] = value
    turned = flat[...].T
    return [turned[k : k + 1, :] for k in range(count)]


def to_rows(lines, lines_ref, accs):
    rows = accs.shape[1]
    for k, line in enumerate(lines):
        lines_ref[k : k + 1, :] = line
    turned = lines_ref[...].T
    for k in range(len(lines)):
        accs[k] = jnp.broadcast_to(turned[0:rows, k : k + 1], (rows, 128))


def lane_chunk(i):
    return pl.ds(pl.multiple_of(i * 128, 128), 128)


def embed_bytes(ids, table, emb):
    lane = lax.broadcasted_iota(jnp.int32, (ids.shape[0], TABLE), 1)
    emb[...] = nt((ids == lane).astype(bf16), table)


def small_rows(table, small):
    lane = lax.broadcasted_iota(jnp.int32, (8, TABLE), 1)
    row = lax.broadcasted_iota(jnp.int32, (8, TABLE), 0)
    small[...] = nt((lane == row + VOCAB).astype(bf16), table)


def block_probs(emb, small, conv, accs, flat, live, m0, m1, rows):
    accs[0:4] = jnp.zeros((4, rows, 128), f32)

    def step(i, _):
        chunk = lane_chunk(i)
        w0, w1, w2, w3 = [small[k : k + 1, chunk] for k in range(4)]
        scorer = small[4:5, chunk]
        e0, e1, e2, e3 = [emb[k * rows : (k + 1) * rows, chunk] for k in range(4)]
        e3d, e0u, e1u = down(e3), up(e0), up(e1)
        c = (
            w0 * e3d + w1 * e0 + w2 * e1 + w3 * e2,
            w0 * e0 + w1 * e1 + w2 * e2 + w3 * e3,
            w0 * e1 + w1 * e2 + w2 * e3 + w3 * e0u,
            w0 * e2 + w1 * e3 + w2 * e0u + w3 * e1u,
        )
        for k in range(4):
            value = c[k] * live[k]
            conv[k, :, chunk] = value
            accs[k] += value * scorer
        return 0

    lax.fori_loop(0, D // 128, step, 0)
    score = to_lanes(accs, 4, flat)
    three = triples(score, m0, m1)
    p01, p23 = score[0] + score[1], score[2] + score[3]
    quad = 0.25 * (p01 + p23)
    probs = []
    for k in range(4):
        scores = (score[k], 0.5 * (p01, p01, p23, p23)[k], three[k] * (1.0 / 3.0), quad)
        top = jnp.maximum(jnp.maximum(scores[0], scores[1]), jnp.maximum(scores[2], scores[3]))
        powers = [jnp.exp(value - top) for value in scores]
        norm = 1.0 / (powers[0] + powers[1] + powers[2] + powers[3])
        probs.append([power * norm for power in powers])
    return probs


def reach(m0, m1, k, ahead):
    one = jnp.ones(m0[k].shape, f32)
    zero = jnp.zeros_like(one)
    if ahead == 0:
        return one
    if ahead == 1:
        return jnp.where(m0[k] | m1[k], one, zero)
    if ahead == 2:
        return jnp.where(m0[k], one, zero)
    if ahead == -1:
        return jnp.where(m0[k], zero, one)
    return jnp.where(m0[k] | m1[k], zero, one)


def token_weights(probs, m0, m1):
    weights = []
    for half in range(2):
        first, second = probs[2 * half], probs[2 * half + 1]
        pair = 0.5 * (first[1] + second[1])
        quad = 0.25 * (first[3] + second[3])
        row = []
        for j in range(6):
            place = 2 * half - 2 + j
            value = jnp.zeros_like(pair)
            for k, p in ((2 * half, first), (2 * half + 1, second)):
                ahead = place - k
                if abs(ahead) <= 2:
                    value += p[2] * (1.0 / 3.0) * reach(m0, m1, k, ahead)
                if ahead == 0:
                    value += p[0]
            if 0 <= place < 4:
                value += quad
            if place // 2 == half:
                value += pair
            row.append(value)
        weights.append(row)
    return weights


def places(c):
    c0, c1, c2, c3 = c
    return ((down(c2), down(c3), c0, c1, c2, c3), (c0, c1, c2, c3, up(c0), up(c1)))


def pool_kernel(first_ref, ids, table, resid, normed, emb, small, conv, accs, flat, lines, tokens, *, rows, total_bytes):
    first = first_ref[0]
    embed_bytes(ids[...], table[...], emb)
    small_rows(table[...], small)

    @pl.when(pl.program_id(0) == 0)
    def _():
        flat[...] = jnp.zeros_like(flat)
        lines[...] = jnp.zeros_like(lines)

    _, m0, m1 = lane_marks(first, flat.shape[0], total_bytes)
    live = live_rows(first, rows, total_bytes)
    probs = block_probs(emb, small, conv, accs, flat, live, m0, m1, rows)
    weights = token_weights(probs, m0, m1)
    to_rows([0.5 * weights[half][j] for half in range(2) for j in range(6)], lines, accs)
    own = rows - 16

    def step(i, square):
        chunk = lane_chunk(i)
        around = places([conv[k, :, chunk] for k in range(4)])
        for half in range(2):
            token = accs[6 * half] * around[half][0]
            for j in range(1, 6):
                token += accs[6 * half + j] * around[half][j]
            tokens[i, pl.ds(half, own, stride=2), :] = token[8 : 8 + own]
        values = tokens[i]
        resid[:, chunk] = values
        return square + values * values

    square = lax.fori_loop(0, D // 128, step, jnp.zeros((2 * own, 128), f32))
    scale = lax.rsqrt(jnp.sum(square, axis=-1, keepdims=True) * (1.0 / D) + epsilon)
    normed[...] = (resid[...] * scale * small[5:6, :]).astype(bf16)


def pool(first, ids, table, total_bytes):
    count, wide, _ = ids.shape
    rows = wide // 4
    tokens = 2 * (rows - 16)
    return pl.pallas_call(
        partial(pool_kernel, rows=rows, total_bytes=total_bytes),
        grid=(count,),
        in_specs=[
            pl.BlockSpec(memory_space=pltpu.SMEM),
            pl.BlockSpec((None, wide, 1), lambda i: (i, 0, 0)),
            pl.BlockSpec((D, TABLE), lambda i: (0, 0)),
        ],
        out_specs=[
            pl.BlockSpec((None, tokens, D), lambda i: (i, 0, 0)),
            pl.BlockSpec((None, tokens, D), lambda i: (i, 0, 0)),
        ],
        out_shape=[
            jax.ShapeDtypeStruct((count, tokens, D), f32),
            jax.ShapeDtypeStruct((count, tokens, D), bf16),
        ],
        scratch_shapes=[
            pltpu.VMEM((wide, D), f32),
            pltpu.VMEM((8, D), f32),
            pltpu.VMEM((4, rows, D), f32),
            pltpu.VMEM((12, rows, 128), f32),
            pltpu.VMEM((2 * 128, 128), f32),
            pltpu.VMEM((16, 2 * 128), f32),
            pltpu.VMEM((D // 128, tokens, 128), f32),
        ],
        cost_estimate=pl.CostEstimate(flops=count * 3_000_000_000, bytes_accessed=4_000_000, transcendentals=0),
        name="pool",
    )(first, ids, table)


def pool_back_kernel(
    first_ref, ids, ids_row, table, pulled_own, from_core, from_x, dq, query_w, resid, after,
    feed_stats, *rest, rows, total_bytes, given, last, deps,
):
    if given:
        embed_before, small_before = rest[:2]
        rest = rest[2:]
    rest = rest[deps:]
    if last:
        turned = rest[0]
        embed_grad, small_grad = rest[-2:]
        rest = rest[1:-2]
    else:
        embed_grad, small_grad = rest[:2]
        rest = rest[2:]
    emb, small, conv, accs, flat, lines, tokens, pulls, emb_grad = rest
    first = first_ref[0]
    own = rows - 16
    chunks = D // 128

    if given:
        small_grad[...] = small_before[...]
    else:
        small_grad[...] = jnp.zeros_like(small_grad)
    flat[...] = jnp.zeros_like(flat)
    lines[...] = jnp.zeros_like(lines)

    embed_bytes(ids[...], table[...], emb)
    small_rows(table[...], small)
    live_lane, m0, m1 = lane_marks(first, flat.shape[0], total_bytes)
    live = live_rows(first, rows, total_bytes)

    x = resid[...]
    gn = pulled_own[...].astype(f32) + from_core[...].astype(f32) + from_x[...].astype(f32)
    gn = gn + nt(dq[...], query_w[...])
    scale = lax.rsqrt(jnp.mean(x * x, axis=-1, keepdims=True) + epsilon)
    gain = small[5:6, :]
    small_grad[5:6, :] += jnp.sum(gn * x * scale, axis=0, keepdims=True)
    gg = gain * gn
    inner = jnp.mean(gg * x, axis=-1, keepdims=True)
    total = after[...] + scale * gg - x * (scale * scale * scale * inner)
    for i in range(chunks):
        tokens[i] = total[:, i * 128 : (i + 1) * 128]

    probs = block_probs(emb, small, conv, accs, flat, live, m0, m1, rows)
    accs[0:12] = jnp.zeros((12, rows, 128), f32)
    pulls[:, 0:8, :] = jnp.zeros((2, 8, D), f32)
    pulls[:, rows - 8 : rows, :] = jnp.zeros((2, 8, D), f32)

    def dots(i, _):
        chunk = lane_chunk(i)
        around = places([conv[k, :, chunk] for k in range(4)])
        for half in range(2):
            pulls[half, 8 : 8 + own, chunk] = 0.5 * tokens[i, pl.ds(half, own, stride=2), :]
            g = pulls[half, :, chunk]
            for j in range(6):
                accs[6 * half + j] += g * around[half][j]
        return 0

    lax.fori_loop(0, chunks, dots, 0)
    every = to_lanes(accs, 12, flat)
    pulled = []
    for half in range(2):
        at = every[6 * half : 6 * half + 6]
        pair = 0.5 * (at[2] + at[3])
        quad = 0.25 * (at[2] + at[3] + (at[4] + at[5] if half == 0 else at[0] + at[1]))
        for k in (2 * half, 2 * half + 1):
            middle = k - (2 * half - 2)
            three = sum(
                at[middle + ahead] * reach(m0, m1, k, ahead)
                for ahead in range(-2, 3)
                if 0 <= middle + ahead < 6
            ) * (1.0 / 3.0)
            gd = (at[middle], pair, three, quad)
            p = probs[k]
            mean = p[0] * gd[0] + p[1] * gd[1] + p[2] * gd[2] + p[3] * gd[3]
            pulled.append([p[b] * (gd[b] - mean) for b in range(4)])

    spread = triples([pulled[k][2] for k in range(4)], m0, m1)
    quad = 0.25 * (pulled[0][3] + pulled[1][3] + pulled[2][3] + pulled[3][3])
    weights = token_weights(probs, m0, m1)
    factors = []
    for k in range(4):
        half = k // 2
        pair = 0.5 * (pulled[2 * half][1] + pulled[2 * half + 1][1])
        factors.append((pulled[k][0] + pair + spread[k] * (1.0 / 3.0) + quad) * live_lane[k])
    at_row = lax.broadcasted_iota(jnp.int32, (1, flat.shape[0]), 1)
    inside = (at_row >= 8) & (at_row < 8 + own)
    even = [jnp.where(inside, weight, 0.0) for weight in weights[0]]
    odd = [jnp.where(inside, weight, 0.0) for weight in weights[1]]
    reached = (
        (behind_lane(odd[4]), even[2], odd[0]),
        (behind_lane(odd[5]), even[3], odd[1]),
        (even[4], odd[2], ahead_lane(even[0])),
        (even[5], odd[3], ahead_lane(even[1])),
    )
    for k in range(4):
        for j in range(3):
            factors.append(reached[k][j] * live_lane[k])
    to_rows(factors, lines, accs)

    def back(i, _):
        chunk = lane_chunk(i)
        w0, w1, w2, w3 = [small[k : k + 1, chunk] for k in range(4)]
        scorer = small[4:5, chunk]
        g0, g1 = pulls[0, :, chunk], pulls[1, :, chunk]
        g1d, g0u = down(g1), up(g0)
        e0, e1, e2, e3 = [emb[k * rows : (k + 1) * rows, chunk] for k in range(4)]
        near = ((g1d, g0, g1), (g1d, g0, g1), (g0, g1, g0u), (g0, g1, g0u))
        score = jnp.zeros((rows, 128), f32)
        gc = []
        for k in range(4):
            score += accs[k] * conv[k, :, chunk]
            value = accs[k] * scorer
            for j in range(3):
                value += accs[4 + 3 * k + j] * near[k][j]
            gc.append(value)
        small_grad[4:5, chunk] += jnp.sum(score, axis=0, keepdims=True)
        gc0, gc1, gc2, gc3 = gc
        e3d, e0u, e1u = down(e3), up(e0), up(e1)
        taps = (
            gc0 * e3d + gc1 * e0 + gc2 * e1 + gc3 * e2,
            gc0 * e0 + gc1 * e1 + gc2 * e2 + gc3 * e3,
            gc0 * e1 + gc1 * e2 + gc2 * e3 + gc3 * e0u,
            gc0 * e2 + gc1 * e3 + gc2 * e0u + gc3 * e1u,
        )
        for k in range(4):
            small_grad[k : k + 1, chunk] += jnp.sum(taps[k], axis=0, keepdims=True)
        gc3d, gc2d, gc0u = down(gc3), down(gc2), up(gc0)
        grads = (
            w0 * gc1 + w1 * gc0 + w2 * gc3d + w3 * gc2d,
            w0 * gc2 + w1 * gc1 + w2 * gc0 + w3 * gc3d,
            w0 * gc3 + w1 * gc2 + w2 * gc1 + w3 * gc0,
            w0 * gc0u + w1 * gc3 + w2 * gc2 + w3 * gc1,
        )
        for k in range(4):
            emb_grad[k * rows : (k + 1) * rows, chunk] = grads[k].astype(bf16)
        return 0

    lax.fori_loop(0, chunks, back, 0)
    row = lax.broadcasted_iota(jnp.int32, (TABLE, 4 * rows), 0)
    total = nn((ids_row[...] == row).astype(bf16), emb_grad[...])
    if given:
        total = total + embed_before[...]
    embed_grad[...] = total
    if last:
        small_grad[6:7, :] = feed_stats[0:1, :]
        embed_grad[VOCAB : VOCAB + 7, :] = small_grad[0:7, :]
        turned[...] = embed_grad[...].T.astype(bf16)


def pool_back(
    seq, first, ids, ids_row, table, pulled, from_core, from_x, dq, qkv, resid, after_grad,
    feed_stats, before, deps, total_bytes,
):
    count, wide, _ = ids.shape
    rows = wide // 4
    tokens = 2 * (rows - 16)
    last = seq == count - 1
    token_spec = pl.BlockSpec((None, tokens, D), lambda i: (seq, 0, 0))
    table_sum = pl.BlockSpec((TABLE, D), lambda i: (0, 0))
    small_sum = pl.BlockSpec((8, D), lambda i: (0, 0))
    sums = [pltpu.VMEM((TABLE, D), f32), pltpu.VMEM((8, D), f32)]
    return pl.pallas_call(
        partial(
            pool_back_kernel, rows=rows, total_bytes=total_bytes, given=bool(before), last=last,
            deps=len(deps),
        ),
        grid=(1,),
        in_specs=[
            pl.BlockSpec(memory_space=pltpu.SMEM),
            pl.BlockSpec((None, wide, 1), lambda i: (seq, 0, 0)),
            pl.BlockSpec((None, 1, wide), lambda i: (seq, 0, 0)),
            pl.BlockSpec((D, TABLE), lambda i: (0, 0)),
            token_spec,
            token_spec,
            pl.BlockSpec((tokens, D), lambda i: (0, 0)),
            token_spec,
            pl.BlockSpec((D, D), lambda i: (0, 0)),
            token_spec,
            token_spec,
            small_sum,
        ]
        + ([table_sum, small_sum] if before else [])
        + [pl.BlockSpec(memory_space=pl.ANY)] * len(deps),
        out_specs=pl.BlockSpec((D, TABLE), lambda i: (0, 0)) if last else [table_sum, small_sum],
        out_shape=jax.ShapeDtypeStruct((D, TABLE), bf16)
        if last
        else [jax.ShapeDtypeStruct((TABLE, D), f32), jax.ShapeDtypeStruct((8, D), f32)],
        scratch_shapes=[
            pltpu.VMEM((wide, D), f32),
            pltpu.VMEM((8, D), f32),
            pltpu.VMEM((4, rows, D), f32),
            pltpu.VMEM((16, rows, 128), f32),
            pltpu.VMEM((2 * 128, 128), f32),
            pltpu.VMEM((16, 2 * 128), f32),
            pltpu.VMEM((D // 128, tokens, 128), f32),
            pltpu.VMEM((2, rows, D), f32),
            pltpu.VMEM((wide, D), bf16),
        ]
        + (sums if last else []),
        cost_estimate=pl.CostEstimate(flops=9_000_000_000, bytes_accessed=8_000_000, transcendentals=0),
        name="pool_back",
    )(
        first, ids, ids_row, table, pulled, from_core, from_x, dq, qkv, resid, after_grad,
        feed_stats, *before, *deps,
    )


def prepare_kernel(
    rank_ref, lengths_ref, bias_ref, lanes_bias, tile, turned, side, diag, *, queries, keys, parts
):
    head = pl.program_id(0)
    rank = rank_ref[0]

    @pl.when(head == 0)
    def _():
        place = lax.broadcasted_iota(jnp.int32, (BUCKETS, 6 * HALF), 1)
        inside = lax.rem(place, 2 * HALF)
        offset = jnp.where(inside < HALF, inside, inside - 2 * HALF)
        relative = (place // (2 * HALF) - 1) * HALF + offset
        bucket = lax.broadcasted_iota(jnp.int32, (BUCKETS, 6 * HALF), 0)
        hot = (bucket_of(relative) == bucket).astype(bf16)
        diag[...] = lax.dot_general(
            lanes_bias[...], hot, (((0,), (0,)), ((), ())), preferred_element_type=f32
        )
        row = lax.broadcasted_iota(jnp.int32, (keys, SIDE), 0)
        lane = lax.broadcasted_iota(jnp.int32, (keys, SIDE), 1)
        at = lax.rem(rank * queries - HALF + row + keys, keys)
        far = row >= queries + 2 * HALF
        right = far & (at > rank * queries)
        left = far & (at <= rank * queries)
        fixed = jnp.where(
            right,
            lanes_bias[31:32, :].astype(f32),
            jnp.where(left, lanes_bias[15:16, :].astype(f32), 0.0),
        )
        fixed = jnp.where((lane >= ONES) & (lane < ONES + 3), 1.0, fixed)
        fixed = jnp.where((lane == LEFT) & left | (lane == RIGHT) & right, 1.0, fixed)
        for s in range(side.shape[0]):
            masked = jnp.where(2 * at < lengths_ref[s], 0.0, masked_score)
            side[s] = jnp.where(lane == 0, masked, fixed).astype(bf16)

    blocks = []
    for index in range(3):
        line = diag[pl.ds(head + 1, 1), index * 2 * HALF : (index + 1) * 2 * HALF]
        full = jnp.broadcast_to(line, (HALF, 2 * HALF))
        blocks.append(pltpu.roll(full, 0, 1, stride=1, stride_axis=0)[:, :HALF])
    turned_blocks = [block.T.astype(bf16) for block in blocks]
    blocks = [block.astype(bf16) for block in blocks]
    behind = jnp.full((HALF, HALF), bias_ref[15, head], f32).astype(bf16)
    ahead = jnp.full((HALF, HALF), bias_ref[31, head], f32).astype(bf16)
    steps = queries // HALF
    for q in range(steps):
        for n in range(steps + 2):
            apart = n - 1 - q
            wrapped = ((n == 0) & (rank == 0), (n == steps + 1) & (rank == parts - 1))
            plain = behind if apart < -1 else ahead if apart > 1 else blocks[apart + 1]
            flipped = behind if apart < -1 else ahead if apart > 1 else turned_blocks[apart + 1]
            if n == 0:
                plain = jnp.where(wrapped[0], ahead, plain)
                flipped = jnp.where(wrapped[0], ahead, flipped)
            if n == steps + 1:
                plain = jnp.where(wrapped[1], behind, plain)
                flipped = jnp.where(wrapped[1], behind, flipped)
            tile[q * HALF : (q + 1) * HALF, n * HALF : (n + 1) * HALF] = plain
            turned[n * HALF : (n + 1) * HALF, q * HALF : (q + 1) * HALF] = flipped


def prepare(rank, lengths, bias, queries, keys, parts):
    near = queries + 2 * HALF
    seqs = lengths.shape[0]
    lanes_bias = jnp.pad(bias, ((0, 0), (1, SIDE - 1 - HEADS)))
    smem = pl.BlockSpec(memory_space=pltpu.SMEM)
    return pl.pallas_call(
        partial(prepare_kernel, queries=queries, keys=keys, parts=parts),
        grid=(HEADS,),
        in_specs=[smem, smem, smem, pl.BlockSpec((BUCKETS, SIDE), lambda i: (0, 0))],
        out_specs=[
            pl.BlockSpec((None, queries, near), lambda i: (i, 0, 0)),
            pl.BlockSpec((None, near, queries), lambda i: (i, 0, 0)),
            pl.BlockSpec((seqs, keys, SIDE), lambda i: (0, 0, 0)),
        ],
        out_shape=[
            jax.ShapeDtypeStruct((HEADS, queries, near), bf16),
            jax.ShapeDtypeStruct((HEADS, near, queries), bf16),
            jax.ShapeDtypeStruct((seqs, keys, SIDE), bf16),
        ],
        scratch_shapes=[pltpu.VMEM((SIDE, 6 * HALF), f32)],
        cost_estimate=pl.CostEstimate(flops=6_000_000_000, bytes_accessed=7_000_000, transcendentals=0),
        name="prepare",
    )(rank, lengths, bias.astype(f32), lanes_bias)


def row_offset(rank, step, blocks):
    half = lax.rem(2 * rank - 1 + step + 2 * blocks, 2 * blocks)
    apart = jnp.bitwise_xor(rank, half // 2)
    slot = (apart % 2) * 2 + apart // 2
    return pl.multiple_of(slot * (2 * HALF) + (half % 2) * HALF, HALF)


def side_lanes(rows, picks):
    lane = lax.broadcasted_iota(jnp.int32, (rows, SIDE), 1)
    value = jnp.zeros((rows, SIDE), f32)
    for index, entry in picks:
        value = jnp.where(lane == index, entry, value)
    return value.astype(bf16)


def three_parts(value):
    high = value.astype(bf16).astype(f32)
    rest = value - high
    middle = rest.astype(bf16).astype(f32)
    return high, middle, rest - middle


def one_head(values, head):
    lane = lax.broadcasted_iota(jnp.int32, values.shape, 1)
    return jnp.where((lane // HEAD_DIM) == head, values, jnp.zeros_like(values))


def attend_kernel(rank_ref, q, kv, side, bias, out, norm, kcat, vcat, *, near, blocks):
    rank = rank_ref[0]
    pair = pl.program_id(1)
    queries = q.shape[0]

    @pl.when(pair == 0)
    def _():
        kcat[:, SIDE:] = side[...]
        vcat[:, SIDE:] = side[...]
        norm[...] = jnp.zeros_like(norm)

    for step in range(2 * blocks):
        source = pl.ds(row_offset(rank, step, blocks), HALF)
        kcat[step * HALF : (step + 1) * HALF, :SIDE] = kv[source, :SIDE]
        vcat[step * HALF : (step + 1) * HALF, :SIDE] = kv[source, SIDE:]

    lane = lax.broadcasted_iota(jnp.int32, (queries, SIDE), 1)
    halves = []
    for head in range(2):
        index = 2 * pair + head
        extra = side_lanes(queries, [(0, 1.0), (1 + index, 1.0)])
        wide = jnp.concatenate([one_head(q[...], head), extra], axis=1)
        logits = nt(wide, kcat[...])
        close = logits[:, :near] + bias[head].astype(f32)
        away = logits[:, near:]
        top = jnp.maximum(
            jnp.max(close, axis=-1, keepdims=True), jnp.max(away, axis=-1, keepdims=True)
        )
        close = jnp.exp(close - top).astype(bf16)
        away = jnp.exp(away - top).astype(bf16)
        mixed = nn(close, vcat[:near, :]) + nn(away, vcat[near:, :])
        total = mixed[:, SIDE + ONES : SIDE + ONES + 1]
        halves.append(mixed[:, :SIDE] * (1.0 / total))
        norm[...] = jnp.where(lane == index, top + jnp.log(total), norm[...])
    out[...] = jnp.where(lane < HEAD_DIM, halves[0], halves[1]).astype(bf16)


def attend(rank, q, kv, side, bias):
    seqs, queries, _ = q.shape
    keys = kv.shape[1]
    near = bias.shape[-1]
    blocks = keys // queries
    return pl.pallas_call(
        partial(attend_kernel, near=near, blocks=blocks),
        grid=(seqs, PAIRS),
        in_specs=[
            pl.BlockSpec(memory_space=pltpu.SMEM),
            pl.BlockSpec((None, queries, SIDE), lambda s, i: (s, 0, i)),
            pl.BlockSpec((None, keys, 2 * SIDE), lambda s, i: (s, 0, i)),
            pl.BlockSpec((None, keys, SIDE), lambda s, i: (s, 0, 0)),
            pl.BlockSpec((2, queries, near), lambda s, i: (i, 0, 0)),
        ],
        out_specs=[
            pl.BlockSpec((None, queries, SIDE), lambda s, i: (s, 0, i)),
            pl.BlockSpec((None, queries, SIDE), lambda s, i: (s, 0, 0)),
        ],
        out_shape=[
            jax.ShapeDtypeStruct((seqs, queries, D), bf16),
            jax.ShapeDtypeStruct((seqs, queries, SIDE), f32),
        ],
        scratch_shapes=[pltpu.VMEM((keys, 2 * SIDE), bf16)] * 2,
        cost_estimate=pl.CostEstimate(flops=25_000_000_000, bytes_accessed=8_000_000, transcendentals=0),
        name="attend",
    )(rank, q, kv, side, bias)


def attend_back_kernel(
    rank_ref, q, kv, side, bias, norm, mixed, grad, dq, dkv, dnear, dfar, kcat, vcat, kturn, *,
    near, blocks, part,
):
    rank = rank_ref[0]
    pair = pl.program_id(1)
    queries = q.shape[0]
    keys = kv.shape[0]

    @pl.when(pair == 0)
    def _():
        kcat[:, SIDE:] = side[...]
        vcat[:, SIDE:] = side[...]
        kturn[SIDE:, :] = side[...].astype(f32).T[ONES : 2 * ONES, :].astype(bf16)

    for step in range(2 * blocks):
        source = pl.ds(row_offset(rank, step, blocks), HALF)
        kcat[step * HALF : (step + 1) * HALF, :SIDE] = kv[source, :SIDE]
        vcat[step * HALF : (step + 1) * HALF, :SIDE] = kv[source, SIDE:]
    kturn[:SIDE, :] = kcat[:, :SIDE].astype(f32).T.astype(bf16)

    lane = lax.broadcasted_iota(jnp.int32, (queries, SIDE), 1)
    queries_of, grads_of, wide_q, wide_g = [], [], [], []
    products = grad[...].astype(f32) * mixed[...].astype(f32)
    for head in range(2):
        index = 2 * pair + head
        level = jnp.sum(jnp.where(lane == index, norm[...], 0.0), axis=-1, keepdims=True)
        delta = jnp.sum(
            jnp.where((lane // HEAD_DIM) == head, products, 0.0), axis=-1, keepdims=True
        )
        la, lb, lc = three_parts(-level)
        da, db, dc = three_parts(-delta)
        queries_of.append(one_head(q[...], head))
        grads_of.append(one_head(grad[...], head))
        extra = [(0, 1.0), (1 + index, 1.0), (ONES, la), (ONES + 1, lb), (ONES + 2, lc)]
        wide_q.append(jnp.concatenate([queries_of[head], side_lanes(queries, extra)], axis=1))
        extra = [(ONES, da), (ONES + 1, db), (ONES + 2, dc)]
        wide_g.append(jnp.concatenate([grads_of[head], side_lanes(queries, extra)], axis=1))

    sums = [jnp.zeros((kturn.shape[0], queries), f32) for _ in range(2)]
    for base in range(0, keys, part):
        span = slice(base, base + part)
        value_part = jnp.zeros((part, SIDE), f32)
        key_part = jnp.zeros((part, SIDE), f32)
        for head in range(2):
            logits = nt(kcat[span, :], wide_q[head])
            if base < near:
                here = min(near, base + part) - base
                close = logits[:here] + bias[head, base : base + here, :].astype(f32)
                logits = close if here == part else jnp.concatenate([close, logits[here:]], axis=0)
            probs = jnp.exp(logits)
            pull = nt(vcat[span, :], wide_g[head])
            low = (probs * pull).astype(bf16)
            value_part += nn(probs.astype(bf16), grads_of[head])
            key_part += nn(low, queries_of[head])
            sums[head] += nn(kturn[:, span], low)
            if base < near:
                here = min(near, base + part) - base
                dnear[head, base : base + here, :] = low[:here]
        for step in range(base // HALF, (base + part) // HALF):
            target = pl.ds(row_offset(rank, step, blocks), HALF)
            inner = slice(step * HALF - base, (step + 1) * HALF - base)
            dkv[target, :SIDE] = key_part[inner].astype(bf16)
            dkv[target, SIDE:] = value_part[inner].astype(bf16)
    turned = jnp.concatenate([sums[0][:HEAD_DIM], sums[1][HEAD_DIM:SIDE]], axis=0)
    dq[...] = turned.T.astype(bf16)
    for head in range(2):
        dfar[head] = sums[head][SIDE:, :]


def attend_back(rank, q, kv, side, bias, norm, mixed, grad):
    seqs, queries, _ = q.shape
    keys = kv.shape[1]
    near = bias.shape[1]
    blocks = keys // queries
    own = pl.BlockSpec((None, queries, SIDE), lambda s, i: (s, 0, i))
    every = pl.BlockSpec((None, keys, 2 * SIDE), lambda s, i: (s, 0, i))
    return pl.pallas_call(
        partial(attend_back_kernel, near=near, blocks=blocks, part=KEY_PART),
        grid=(seqs, PAIRS),
        in_specs=[
            pl.BlockSpec(memory_space=pltpu.SMEM),
            own,
            every,
            pl.BlockSpec((None, keys, SIDE), lambda s, i: (s, 0, 0)),
            pl.BlockSpec((2, near, queries), lambda s, i: (i, 0, 0)),
            pl.BlockSpec((None, queries, SIDE), lambda s, i: (s, 0, 0)),
            own,
            own,
        ],
        out_specs=[
            own,
            every,
            pl.BlockSpec((None, 2, near, queries), lambda s, i: (s, i, 0, 0)),
            pl.BlockSpec((None, 2, ONES, queries), lambda s, i: (s, i, 0, 0)),
        ],
        out_shape=[
            jax.ShapeDtypeStruct((seqs, queries, D), bf16),
            jax.ShapeDtypeStruct((seqs, keys, 2 * D), bf16),
            jax.ShapeDtypeStruct((seqs, HEADS, near, queries), bf16),
            jax.ShapeDtypeStruct((seqs, HEADS, ONES, queries), f32),
        ],
        scratch_shapes=[
            pltpu.VMEM((keys, 2 * SIDE), bf16),
            pltpu.VMEM((keys, 2 * SIDE), bf16),
            pltpu.VMEM((SIDE + ONES, keys), bf16),
        ],
        cost_estimate=pl.CostEstimate(flops=40_000_000_000, bytes_accessed=12_000_000, transcendentals=0),
        name="attend_back",
    )(rank, q, kv, side, bias, norm, mixed, grad)


def bias_grad_kernel(rank_ref, near, far, *rest, parts):
    out, lines = rest[-2:]
    rank = rank_ref[0]
    head = pl.program_id(0)
    seqs = near.shape[0]
    steps = near.shape[1] // HALF - 2
    first_in, last_in = rank != 0, rank != parts - 1

    def block(n, q):
        rows, cols = slice(n * HALF, (n + 1) * HALF), slice(q * HALF, (q + 1) * HALF)
        return sum(near[s, rows, cols].astype(f32) for s in range(seqs))

    sums = [jnp.zeros((HALF, HALF), f32) for _ in range(3)]
    left = sum(far[s, LEFT - ONES : LEFT - ONES + 1, :] for s in range(seqs))
    right = sum(far[s, RIGHT - ONES : RIGHT - ONES + 1, :] for s in range(seqs))
    left = [left[:, q * HALF : (q + 1) * HALF] for q in range(steps)]
    right = [right[:, q * HALF : (q + 1) * HALF] for q in range(steps)]
    for n in range(steps + 2):
        inside = first_in if n == 0 else last_in if n == steps + 1 else None
        for q in range(steps):
            value = block(n, q)
            apart = n - 1 - q
            if inside is not None:
                column = jnp.sum(value, axis=0, keepdims=True)
                outer = jnp.where(inside, 0.0, column)
                if n == 0:
                    right[q] += outer
                else:
                    left[q] += outer
                kept = jnp.where(inside, column, 0.0)
                if apart < -1:
                    left[q] += kept
                elif apart > 1:
                    right[q] += kept
                value = jnp.where(inside, value, 0.0)
            if abs(apart) <= 1:
                sums[apart + 1] += value
    found = []
    for value in sums:
        wide = jnp.concatenate([value, jnp.zeros((HALF, HALF), f32)], axis=1)
        folded = wide[0:8, :]
        for a in range(8, HALF, 8):
            folded += pltpu.roll(wide[a : a + 8, :], 2 * HALF - a, 1)
        line = folded[0:1, :]
        for b in range(1, 8):
            line += pltpu.roll(folded[b : b + 1, :], 2 * HALF - b, 1)
        found.append(line)
    found += [jnp.concatenate(left, axis=1), jnp.concatenate(right, axis=1)]
    lines[pl.ds(head, 1), :] = jnp.concatenate(found, axis=1)

    @pl.when(head == pl.num_programs(0) - 1)
    def _():
        shape = (10 * HALF, 128)
        place = lax.broadcasted_iota(jnp.int32, shape, 0)
        lane = lax.broadcasted_iota(jnp.int32, shape, 1)
        segment, inner = place // (2 * HALF), lax.rem(place, 2 * HALF)
        behind = jnp.where(inner < HALF, inner, inner - 2 * HALF)
        relative = (segment - 1) * HALF - behind
        bucket = jnp.where(segment == 3, 15, jnp.where(segment == 4, 31, bucket_of(relative)))
        hot = (bucket == lane).astype(bf16)
        split = jnp.concatenate([part.astype(bf16) for part in three_parts(lines[...])], axis=0)
        total = nn(split, hot)
        rows = lines.shape[0]
        out[...] = total[:rows] + total[rows : 2 * rows] + total[2 * rows :]


def bias_sums(rank, near_parts, far_parts, parts, deps):
    seqs, heads, near, queries = near_parts.shape
    assert queries == 2 * HALF
    return pl.pallas_call(
        partial(bias_grad_kernel, parts=parts),
        grid=(heads,),
        in_specs=[
            pl.BlockSpec(memory_space=pltpu.SMEM),
            pl.BlockSpec((seqs, None, near, queries), lambda i: (0, i, 0, 0)),
            pl.BlockSpec((seqs, None, ONES, queries), lambda i: (0, i, 0, 0)),
        ]
        + [pl.BlockSpec(memory_space=pl.ANY)] * len(deps),
        out_specs=pl.BlockSpec((16, 128), lambda i: (0, 0)),
        out_shape=jax.ShapeDtypeStruct((16, 128), f32),
        scratch_shapes=[pltpu.VMEM((16, 10 * HALF), f32)],
        cost_estimate=pl.CostEstimate(flops=6_000_000_000, bytes_accessed=9_000_000, transcendentals=0),
        name="bias_sums",
    )(rank, near_parts, far_parts, *deps)


def gelu_parts(x):
    inner = 0.7978845608028654 * (x + 0.044715 * (x * x * x))
    t = jnp.tanh(inner)
    half = 0.5 * (1.0 + t)
    slope = half + 0.5 * x * (1.0 - t * t) * (
        0.7978845608028654 * (1.0 + 0.134145 * (x * x))
    )
    return x * half, slope


def feed_kernel(
    place_ref, count_ref, lengths_ref, att, resid, teacher, gain, gate_w, up_w, down_w, output_w,
    block_out, normed, hidden, branch, gate_low, up_low, after_grad, after_low, att_grad, stats,
    act, steep, *, chunk,
):
    step = pl.program_id(0)
    rows = att.shape[0]
    ffn_dim = gate_w.shape[1]

    @pl.when(step == 0)
    def _():
        stats[...] = jnp.zeros_like(stats)

    after = resid[...] + nn(att[...], output_w[...])
    scale = lax.rsqrt(jnp.mean(after * after, axis=-1, keepdims=True) + epsilon)
    normed[...] = (after * scale * gain[...]).astype(bf16)
    out = after
    for base in range(0, ffn_dim, chunk):
        span = slice(base, base + chunk)
        gate = nn(normed[...], gate_w[:, span])
        up_part = nn(normed[...], up_w[:, span])
        value, slope = gelu_parts(gate)
        act[:, span] = value
        steep[:, span] = slope * up_part
        low = (value * up_part).astype(bf16)
        hidden[:, span] = low
        out = out + nn(low, down_w[span, :])
    block_out[...] = out
    token = place_ref[0] + lax.broadcasted_iota(jnp.int32, (rows, D), 0)
    live = (2 * token < lengths_ref[step]).astype(f32)
    error = live * (out - teacher[...])
    stats[1:2, :] += jnp.sum(error * error, axis=0, keepdims=True)
    out_grad = (2.0 / count_ref[0]) * error
    branch[...] = out_grad.astype(bf16)
    back = jnp.zeros((rows, D), f32)
    for base in range(0, ffn_dim, chunk):
        span = slice(base, base + chunk)
        pull = nt(branch[...], down_w[span, :])
        gate_part = (pull * steep[:, span]).astype(bf16)
        up_part = (pull * act[:, span]).astype(bf16)
        gate_low[:, span] = gate_part
        up_low[:, span] = up_part
        back = back + nt(gate_part, gate_w[:, span]) + nt(up_part, up_w[:, span])
    stats[0:1, :] += jnp.sum(back * after * scale, axis=0, keepdims=True)
    gained = back * gain[...]
    inner = jnp.mean(gained * after, axis=-1, keepdims=True)
    total = out_grad + scale * gained - after * (scale * scale * scale * inner)
    after_grad[...] = total
    low = total.astype(bf16)
    after_low[...] = low
    att_grad[...] = nt(low, output_w[...]).astype(bf16)


def feed(place, count, lengths, att, resid, teacher, gain, wide, down_w):
    tokens = att.shape[0]
    seqs = lengths.shape[0]
    rows = tokens // seqs
    ffn_dim = down_w.shape[0]
    once = pl.Buffered(1)
    own = pl.BlockSpec((rows, D), lambda i: (i, 0))
    broad = pl.BlockSpec((rows, ffn_dim), lambda i: (i, 0))
    smem = pl.BlockSpec(memory_space=pltpu.SMEM)
    return pl.pallas_call(
        partial(feed_kernel, chunk=512),
        grid=(seqs,),
        in_specs=[
            smem,
            smem,
            smem,
            own,
            pl.BlockSpec((None, rows, D), lambda i: (i, 0, 0)),
            own,
            pl.BlockSpec((1, D), lambda i: (0, 0)),
            pl.BlockSpec((D, ffn_dim), lambda i: (0, 0), pipeline_mode=once),
            pl.BlockSpec((D, ffn_dim), lambda i: (0, 1), pipeline_mode=once),
            pl.BlockSpec((ffn_dim, D), lambda i: (0, 0), pipeline_mode=once),
            pl.BlockSpec((D, D), lambda i: (0, 3 * ffn_dim // D), pipeline_mode=once),
        ],
        out_specs=[own, own, broad, own, broad, broad, own, own, own, pl.BlockSpec((8, D), lambda i: (0, 0))],
        out_shape=[
            jax.ShapeDtypeStruct((tokens, D), f32),
            jax.ShapeDtypeStruct((tokens, D), bf16),
            jax.ShapeDtypeStruct((tokens, ffn_dim), bf16),
            jax.ShapeDtypeStruct((tokens, D), bf16),
            jax.ShapeDtypeStruct((tokens, ffn_dim), bf16),
            jax.ShapeDtypeStruct((tokens, ffn_dim), bf16),
            jax.ShapeDtypeStruct((tokens, D), f32),
            jax.ShapeDtypeStruct((tokens, D), bf16),
            jax.ShapeDtypeStruct((tokens, D), bf16),
            jax.ShapeDtypeStruct((8, D), f32),
        ],
        scratch_shapes=[pltpu.VMEM((rows, ffn_dim), f32)] * 2,
        cost_estimate=pl.CostEstimate(flops=17_000_000_000, bytes_accessed=30_000_000, transcendentals=0),
        name="feed",
    )(place, count, lengths, att, resid, teacher, gain, wide, wide, down_w, wide)


def dot(a, b):
    return jnp.dot(a, b, preferred_element_type=f32)


def per_device(
    byte_ids,
    lengths,
    teacher,
    embed_table,
    conv_weight,
    score_weight,
    attn_gain,
    rel_bias,
    query_weight,
    key_weight,
    value_weight,
    output_weight,
    ffn_gain,
    gate_weight,
    up_weight,
    down_weight,
):
    seqs, own_bytes = byte_ids.shape
    own = own_bytes // 2
    parts = lax.axis_size("seq")
    dp_size = lax.axis_size("dp")
    rank = lax.axis_index("seq")
    total_tokens, total_bytes = own * parts, own_bytes * parts
    shard = score_weight.shape[0]
    rank_ref = rank.reshape(1).astype(jnp.int32)

    tiled = down_weight.shape[0] % 64 == 0
    third = D // 3
    columns, *attn_halves, packed = (pack if tiled else pack_plain)(
        rank_ref, lengths, embed_table, conv_weight,
        (score_weight[None], attn_gain[None], ffn_gain[None]),
        (query_weight, key_weight, value_weight),
        (gate_weight, up_weight, down_weight, output_weight), total_tokens,
    )
    ids_low = jnp.stack([byte_ids // 16, byte_ids % 16]).astype(bf16)
    id_rows = ids_low.reshape(-1, TABLE)
    cut = attn_halves[0].shape[1]
    qkv_halves = [
        RowGather(attn_halves[0], gather_order("y")),
        RowGather(attn_halves[1], gather_order("x")),
    ]
    small = RowGather(columns, axis_bits("dp"))
    while small.order:
        small.start()
        for each in qkv_halves:
            each.finish()
            if len(each.order) > 3:
                each.start()
        small.finish()
    value = small.value.reshape(-1, TABLE)
    mine = jnp.concatenate([value, id_rows], axis=0)
    x_other = swap(mine, "seq", 2)
    pair = jnp.concatenate([mine, x_other], axis=0)
    c_other = swap(pair, "seq", 1)
    wide_rows = mine.shape[0]
    quarters = jnp.concatenate([pair, c_other], axis=0).reshape(parts, wide_rows, TABLE)
    apart = jnp.bitwise_xor(rank, jnp.arange(parts))
    slots = (apart % 2) * 2 + apart // 2
    ordered = jnp.take(quarters, slots, axis=0)
    table = (
        ordered[:, : dp_size * shard]
        .reshape(parts, dp_size, shard, TABLE)
        .transpose(1, 0, 2, 3)
        .reshape(D, TABLE)
    )
    all_ids = ordered[:, dp_size * shard :].reshape(parts, 2, seqs, own_bytes).astype(jnp.int32)
    all_ids = (all_ids[:, 0] * 16 + all_ids[:, 1]).transpose(1, 0, 2).reshape(seqs, total_bytes)
    counts = jnp.sum(table[:, VOCAB + 7 : VOCAB + 9].astype(f32), axis=0)
    live_count = counts[0] * 64.0 + counts[1]
    ffn_gain_full = table[:, VOCAB + 6].astype(f32)

    padded_ids = jnp.pad(all_ids, ((0, 0), (32, 32)), constant_values=-1)
    first_byte = (rank * own_bytes).astype(jnp.int32)
    first_other = (jnp.bitwise_xor(rank, 2) * own_bytes).astype(jnp.int32)

    def phases(start):
        window = lax.dynamic_slice_in_dim(padded_ids, start, own_bytes + 64, 1)
        return window.reshape(seqs, -1, 4).transpose(0, 2, 1).reshape(seqs, -1)

    phase_ids = phases(first_byte)
    other_ids = phases(first_other)

    ffn_dim = gate_weight.shape[1]
    ffn_dim = gate_weight.shape[1]
    wide_full = lax.all_gather(packed, both, axis=0, tiled=True)
    down_full = wide_full[:, 2 * ffn_dim : 3 * ffn_dim]
    if tiled:
        down_full = down_full.reshape(-1, 3, 8, 8, third).transpose(0, 3, 2, 1, 4)
    down_full = down_full.reshape(ffn_dim, D)

    for each in qkv_halves:
        each.start()
    residual, normed_own = pool(first_byte.reshape(1), phase_ids[:, :, None], table, total_bytes)
    for each in qkv_halves:
        each.finish(normed_own)
        each.start()
    other_first = after(first_other.reshape(1), normed_own)
    _, normed_x = pool(other_first, other_ids[:, :, None], table, total_bytes)
    normed_two = jnp.concatenate([normed_own, normed_x], axis=1)
    normed_other = swap(normed_two, "seq", 1)
    tile, turned_tile, side = prepare(
        after(rank_ref, normed_x), lengths, rel_bias, own, total_tokens, parts
    )
    for each in qkv_halves:
        each.finish(tile)
        each.start()
        each.finish()
    qkv_full = jnp.concatenate([each.result().reshape(D, cut) for each in qkv_halves], axis=1)
    query_full, kv_full = qkv_full[:, :D], qkv_full[:, D:]
    normed = jnp.concatenate([normed_two, normed_other], axis=1)
    own_rows = normed_own.reshape(-1, D)
    queries = dot(own_rows, query_full).astype(bf16).reshape(seqs, own, D)
    pairs_kv = dot(normed.reshape(-1, D), kv_full).astype(bf16).reshape(seqs, total_tokens, 2 * D)
    attended, norms = attend(rank_ref, queries, pairs_kv, side, tile)

    token_rows = seqs * own
    att = attended.reshape(token_rows, D)
    (
        block_out, ffn_in, hidden, branch_grad, gate_low, up_low, after_grad, after_low,
        attended_grad, feed_stats,
    ) = feed(
        (rank * own).reshape(1), live_count.reshape(1), lengths, att,
        residual, teacher.reshape(token_rows, D), ffn_gain_full[None],
        wide_full, down_full,
    )
    down_grad = jnp.einsum("tf,td->fd", hidden, branch_grad, preferred_element_type=f32)
    gate_grad = jnp.einsum("td,tf->df", ffn_in, gate_low, preferred_element_type=f32)
    up_grad = jnp.einsum("td,tf->df", ffn_in, up_low, preferred_element_type=f32)
    output_grad = jnp.einsum("td,te->de", att, after_low, preferred_element_type=f32).astype(bf16)
    down_grad = down_grad.astype(bf16)
    if tiled:
        down_grad = down_grad.reshape(-1, 8, 8, 3, third).transpose(0, 3, 2, 1, 4)
    wide_grad = jnp.concatenate(
        [
            gate_grad.astype(bf16),
            up_grad.astype(bf16),
            down_grad.reshape(D, ffn_dim),
            output_grad,
        ],
        axis=1,
    )
    wide_sum = lax.psum_scatter(wide_grad, both, scatter_dimension=0, tiled=True)
    turn = after(attended_grad, wide_grad).reshape(seqs, own, D)
    dq, dkv, near_parts, far_parts = attend_back(
        rank_ref, queries, pairs_kv, side, turned_tile, norms, attended, turn
    )
    dq_rows, dkv_rows = dq.reshape(-1, D), dkv.reshape(-1, 2 * D)
    pulled = jnp.einsum("te,de->td", dkv_rows, kv_full, preferred_element_type=f32)
    pulled = pulled.astype(bf16).reshape(seqs, total_tokens, D)
    to_core = pulled[:, 2 * own :]
    from_core = swap(to_core, "seq", 1)
    query_grad = jnp.einsum(
        "td,te->de", own_rows, after(dq_rows, to_core), preferred_element_type=f32
    ).astype(bf16)
    from_core = after(from_core, query_grad)
    to_x = [
        (pulled[s, own : 2 * own].astype(f32) + from_core[s, own:].astype(f32)).astype(bf16)
        for s in range(seqs)
    ]
    from_x = [swap(rows, "seq", 2) for rows in to_x]
    normed_rows = normed.reshape(-1, D)
    kv_grad = jnp.einsum(
        "td,te->de", normed_rows, after(dkv_rows, *to_x), preferred_element_type=f32
    ).astype(bf16)
    attn_sum = RowSum(jnp.concatenate([query_grad, kv_grad], axis=1)[None], sum_order("y"))
    attn_sum.start()
    bias_rows = bias_sums(rank_ref, near_parts, far_parts, parts, [attn_sum.sent])
    attn_sum.finish(bias_rows)
    attn_sum.start()
    shared = SumEverywhere(
        jnp.where(
            (jnp.arange(16) < HEADS)[:, None],
            bias_rows,
            jnp.broadcast_to(jnp.sum(feed_stats[1]), (16, 128)),
        )
    )
    shared.start()
    sums, deps = (), [attn_sum.sent]
    for s in range(seqs):
        sums = pool_back(
            s, first_byte.reshape(1), phase_ids[:, :, None], phase_ids[:, None, :], table,
            pulled, from_core, from_x[s], dq, qkv_full, residual,
            after_grad.reshape(seqs, own, D), feed_stats, sums, deps, total_bytes,
        )
        if s < seqs - 1:
            shared.finish(sums[1])
            shared.start()
            deps = [shared.value]
        if s == seqs - 2:
            attn_sum.finish(sums[1])
            attn_sum.start()
            deps.append(attn_sum.sent)
    shared.finish(sums)
    shared.start()
    front_sum = RowSum(sums[None], sum_order("x"))
    while front_sum.order:
        front_sum.start()
        for each in (attn_sum, shared):
            each.finish()
            each.start()
        front_sum.finish()
    front_sum = front_sum.result().reshape(shard, TABLE).T
    every = shared.result()
    bias_grad = every[:HEADS, :BUCKETS].T
    attn_sum = attn_sum.result()[0]
    kv_sum = attn_sum[:, D : 3 * D].reshape(shard, PAIRS, 2, SIDE)
    wide_sum = wide_sum.astype(f32)
    gate_sum, up_sum = wide_sum[:, :ffn_dim], wide_sum[:, ffn_dim : 2 * ffn_dim]
    down_sum = wide_sum[:, 2 * ffn_dim : 3 * ffn_dim]
    if tiled:
        down_sum = down_sum.reshape(-1, 3, 8, 8, third).transpose(0, 3, 2, 1, 4)
    down_sum = down_sum.reshape(-1, D)

    return (
        block_out.reshape(seqs, own, D),
        every[HEADS, 0] / live_count,
        front_sum[:VOCAB],
        front_sum[VOCAB : VOCAB + 4],
        front_sum[VOCAB + 4],
        front_sum[VOCAB + 5],
        bias_grad,
        attn_sum[:, :D],
        kv_sum[:, :, 0].reshape(shard, D),
        kv_sum[:, :, 1].reshape(shard, D),
        wide_sum[:, 3 * ffn_dim :],
        front_sum[VOCAB + 6],
        gate_sum,
        up_sum,
        down_sum,
    )


def solution(mesh):
    tokens = P("dp", "seq", None)
    features = P(("dp", "seq"))
    columns = P(None, ("dp", "seq"))
    rows = P(("dp", "seq"), None)
    in_specs = (
        P("dp", "seq"), P("dp"), tokens, columns, columns, features, features, P(),
        rows, rows, rows, rows, features, rows, rows, rows,
    )
    out_specs = (
        tokens, P(), columns, columns, features, features, P(), rows, rows, rows, rows,
        features, rows, rows, rows,
    )
    return jax.shard_map(
        per_device, mesh=mesh, in_specs=in_specs, out_specs=out_specs, check_vma=False
    )
```

```python
from functools import partial

import jax
import jax.numpy as jnp
from jax import lax
from jax.experimental import pallas as pl
from jax.experimental.pallas import tpu as pltpu
from jax.sharding import PartitionSpec as P

D = 768
HEADS = 12
HEAD_DIM = 64
VOCAB = 259
BUCKETS = 32
TABLE = 384
PAIRS = HEADS // 2
SIDE = 128
ONES = 16
LEFT = 20
RIGHT = 21
HALF = 128
KEY_PART = 1024

epsilon = 1e-06
thresholds = (12, 16, 23, 32, 46, 64, 91)
masked_score = -1000000000.0
highest = lax.Precision.HIGHEST
bf16 = jnp.bfloat16
f32 = jnp.float32
both = ("dp", "seq")


def nt(a, b):
    return lax.dot_general(a, b, (((1,), (1,)), ((), ())), preferred_element_type=f32)


def nn(a, b):
    return lax.dot_general(a, b, (((1,), (0,)), ((), ())), preferred_element_type=f32)


def bucket_of(relative):
    distance = jnp.abs(relative)
    far_bucket = 8 + sum(((distance >= border).astype(jnp.int32) for border in thresholds))
    return jnp.where(relative > 0, 16, 0).astype(jnp.int32) + jnp.where(
        distance < 8, distance, far_bucket
    )


def hot_buckets(relative):
    return (bucket_of(relative)[..., None] == jnp.arange(BUCKETS, dtype=jnp.int32)).astype(f32)


def swap(value, axis, bit):
    peers = lax.axis_size(axis)
    return lax.ppermute(value, axis, [(i, i ^ bit) for i in range(peers)])


def axis_bits(axis):
    bits, bit = [], lax.axis_size(axis) // 2
    while bit:
        bits.append((axis, bit))
        bit //= 2
    return bits


def my_bit(axis, bit):
    return (lax.axis_index(axis) // bit) % 2


def gather_stage(value, axis, bit, position):
    other = swap(value, axis, bit)
    upper = my_bit(axis, bit) == 1
    return jnp.stack(
        [jnp.where(upper, other, value), jnp.where(upper, value, other)], axis=position
    )


class RowGather:
    def __init__(self, rows, order):
        self.value = rows
        self.order = list(order)
        self.places = axis_bits("dp") + axis_bits("seq")
        self.done = []
        self.got = None

    def start(self):
        if self.order:
            self.stage = self.order.pop(0)
            self.got = swap(self.value, *self.stage)

    def finish(self, *others):
        if self.got is None:
            return
        got = after(self.got, *others) if others else self.got
        self.got = None
        place = self.places.index(self.stage)
        position = sum(p < place for p in self.done)
        self.done.append(place)
        upper = my_bit(*self.stage) == 1
        self.value = jnp.stack(
            [jnp.where(upper, got, self.value), jnp.where(upper, self.value, got)],
            axis=position,
        )

    def result(self):
        self.finish()
        while self.order:
            self.start()
            self.finish()
        return self.value


def gather_order(first_axis):
    seq, dp = axis_bits("seq"), axis_bits("dp")
    if first_axis == "y":
        return dp + seq
    return dp[:-1] + seq[:-1] + dp[-1:] + seq[-1:]


def after(value, *others):
    return lax.optimization_barrier((value,) + others)[0]


def hold(value, other):
    return value + (other[(0,) * other.ndim] * 0).astype(value.dtype)


def sum_order(first):
    seq, dp = axis_bits("seq")[::-1], axis_bits("dp")[::-1]
    if first == "x":
        return seq + dp
    if first == "y":
        return seq[:1] + dp[:1] + seq[1:] + dp[1:]
    return seq[:1] + dp[1:] + dp[:1] + seq[1:]


class RowSum:
    def __init__(self, total, order):
        self.parts = [total]
        self.left = axis_bits("dp") + axis_bits("seq")
        self.order = list(order)
        self.sent = self.got = None

    def start(self):
        if not self.order:
            return
        axis, bit = self.order.pop(0)
        position = self.left.index((axis, bit))
        self.left.remove((axis, bit))
        mine = my_bit(axis, bit)

        def half(value, which):
            lead, rows, cols = value.shape
            outer = lead << position
            cut = value.reshape(outer, 2, lead * rows // (2 * outer), cols)
            picked = lax.dynamic_index_in_dim(cut, which, 1, keepdims=False)
            return picked.reshape(lead, rows // 2, cols)

        send = sum(half(value, 1 - mine).astype(f32) for value in self.parts)
        self.sent = send.astype(bf16)
        self.parts = [half(value, mine) for value in self.parts]
        self.got = swap(self.sent, axis, bit)

    def finish(self, other=None, hard=False):
        if self.got is not None:
            order = hold if hard else after
            self.parts.append(self.got if other is None else order(self.got, other))
            self.got = None

    def result(self):
        self.finish()
        while self.order:
            self.start()
            self.finish()
        return sum(value.astype(f32) for value in self.parts)


def after_sends(value, *sums):
    sends = [each.sent for each in sums if each.sent is not None]
    return after(value, *sends)


class SumEverywhere:
    def __init__(self, value):
        self.value = value
        self.order = axis_bits("seq")[::-1] + axis_bits("dp")[::-1]
        self.got = None

    def start(self):
        if self.order:
            self.got = swap(self.value, *self.order.pop(0))

    def finish(self, *others):
        if self.got is not None:
            self.value = self.value + (after(self.got, *others) if others else self.got)
            self.got = None

    def result(self):
        self.finish()
        while self.order:
            self.start()
            self.finish()
        return self.value


def pack_kernel(
    rank_ref, lengths_ref, table, taps, scorer, gain_a, gain_f, query, key, value, gate, up, down,
    output, columns, first_half, second_half, packed, rows, *, total_tokens,
):
    shard = table.shape[1]
    live = jnp.int32(0)
    for s in range(lengths_ref.shape[0]):
        live += jnp.minimum((lengths_ref[s] + 1) // 2, total_tokens)
    live = jnp.where(rank_ref[0] == 0, live, 0)
    first = lax.broadcasted_iota(jnp.int32, (1, shard), 1) == 0
    rows[...] = jnp.zeros_like(rows)
    rows[0:VOCAB, 0:shard] = table[...].astype(f32)
    rows[VOCAB : VOCAB + 4, 0:shard] = taps[...].astype(f32)
    for i, vector in enumerate((scorer, gain_a, gain_f)):
        rows[VOCAB + 4 + i : VOCAB + 5 + i, 0:shard] = vector[...].astype(f32)
    for i, part in enumerate((live // 64, live % 64)):
        at = VOCAB + 7 + i
        rows[at : at + 1, 0:shard] = jnp.where(first, part, 0).astype(f32)
    columns[...] = rows[...].T[0:shard, :].astype(bf16)

    pieces = [query[:, i * SIDE : (i + 1) * SIDE] for i in range(PAIRS)]
    for i in range(PAIRS):
        pieces += [key[:, i * SIDE : (i + 1) * SIDE], value[:, i * SIDE : (i + 1) * SIDE]]
    for half in (first_half, second_half):
        count = half.shape[1] // SIDE
        for i in range(count):
            half[:, i * SIDE : (i + 1) * SIDE] = pieces.pop(0)

    ffn_dim = gate.shape[1]
    packed[:, 0:ffn_dim] = gate[...]
    packed[:, ffn_dim : 2 * ffn_dim] = up[...]
    packed[:, 3 * ffn_dim :] = output[...]
    third = D // 3
    wide = down[...].astype(f32)
    for group in range(down.shape[0] // 64):
        for i in range(8):
            at = group * 64 + i * 8
            tiles = [wide[at : at + 8, j * third : (j + 1) * third] for j in range(3)]
            start = 2 * ffn_dim + i * third
            packed[group * 24 : (group + 1) * 24, start : start + third] = jnp.concatenate(
                tiles, axis=0
            ).astype(bf16)


def pack(rank, lengths, table, taps, vectors, attn, feed_weights, total_tokens):
    smem = pl.BlockSpec(memory_space=pltpu.SMEM)
    shard, ffn_dim = table.shape[1], feed_weights[0].shape[1]
    shapes = [(shard, TABLE), (shard, 3 * D // 2), (shard, 3 * D // 2), (shard, 3 * ffn_dim + D)]
    arrays = (table, taps, *vectors, *attn, *feed_weights)

    def whole(shape):
        return pl.BlockSpec(shape, lambda i: (0, 0))

    return pl.pallas_call(
        partial(pack_kernel, total_tokens=total_tokens),
        grid=(1,),
        in_specs=[smem, smem] + [whole(array.shape) for array in arrays],
        out_specs=[whole(shape) for shape in shapes],
        out_shape=[jax.ShapeDtypeStruct(shape, bf16) for shape in shapes],
        scratch_shapes=[pltpu.VMEM((TABLE, -(-shard // 128) * 128), f32)],
        cost_estimate=pl.CostEstimate(flops=100_000_000, bytes_accessed=1_000_000, transcendentals=0),
        name="pack",
    )(rank, lengths, *arrays)


def pack_plain(rank, lengths, table, taps, vectors, attn, feed_weights, total_tokens):
    shard = table.shape[1]
    live = jnp.sum(jnp.minimum((lengths + 1) // 2, total_tokens))
    live = jnp.where(rank[0] == 0, live, 0)
    counts = jnp.stack([live // 64, live % 64])
    at_count = (jnp.arange(shard) == 0).astype(jnp.int32)
    columns = jnp.concatenate(
        [table, taps, *vectors, (counts[:, None] * at_count[None]).astype(bf16)], axis=0
    )
    columns = jnp.pad(columns, ((0, TABLE - columns.shape[0]), (0, 0))).T
    query, key, value = attn
    pairs = jnp.stack([key.reshape(shard, PAIRS, SIDE), value.reshape(shard, PAIRS, SIDE)], axis=2)
    rows = jnp.concatenate([query, pairs.reshape(shard, 2 * D)], axis=1)
    gate, up, down, output = feed_weights
    packed = jnp.concatenate([gate, up, down.reshape(shard, gate.shape[1]), output], axis=1)
    return columns, rows[:, : 3 * D // 2], rows[:, 3 * D // 2 :], packed


def up(x):
    return pltpu.roll(x, x.shape[0] - 1, 0)


def down(x):
    return pltpu.roll(x, 1, 0)


def ahead_lane(x):
    return pltpu.roll(x, x.shape[1] - 1, 1)


def behind_lane(x):
    return pltpu.roll(x, 1, 1)


def triples(c, m0, m1):
    c0, c1, c2, c3 = c
    p01, p23 = c0 + c1, c2 + c3
    t0, t1, t2, t3 = behind_lane(c3) + p01, p01 + c2, c1 + p23, p23 + ahead_lane(c0)
    before, after = (behind_lane(t3), t0, t1, t2), (t1, t2, t3, ahead_lane(t0))
    here = (t0, t1, t2, t3)
    return tuple(
        jnp.where(m0[k], after[k], jnp.where(m1[k], here[k], before[k])) for k in range(4)
    )


def live_rows(first, rows, total_bytes):
    row = lax.broadcasted_iota(jnp.int32, (rows, 128), 0)
    live = []
    for k in range(4):
        pos = first + 4 * (row - 8) + k
        live.append(((pos >= 0) & (pos < total_bytes)).astype(f32))
    return live


def lane_marks(first, wide, total_bytes):
    row = lax.broadcasted_iota(jnp.int32, (1, wide), 1)
    live, m0, m1 = [], [], []
    for k in range(4):
        pos = first + 4 * (row - 8) + k
        live.append(((pos >= 0) & (pos < total_bytes)).astype(f32))
        shifted = (pos + 48).astype(f32)
        third = jnp.floor((shifted + 0.5) * (1.0 / 3.0))
        rest = shifted - 3.0 * third
        m0.append(rest < 0.5)
        m1.append((rest > 0.5) & (rest < 1.5))
    return live, m0, m1


def to_lanes(accs, count, flat):
    rows = accs.shape[1]
    lane = lax.broadcasted_iota(jnp.int32, (rows, 128), 1)
    value = jnp.zeros((rows, 128), f32)
    for k in range(count):
        value = jnp.where(lane == k, jnp.sum(accs[k], axis=-1, keepdims=True), value)
    flat[0:rows, :] = value
    turned = flat[...].T
    return [turned[k : k + 1, :] for k in range(count)]


def to_rows(lines, lines_ref, accs):
    rows = accs.shape[1]
    for k, line in enumerate(lines):
        lines_ref[k : k + 1, :] = line
    turned = lines_ref[...].T
    for k in range(len(lines)):
        accs[k] = jnp.broadcast_to(turned[0:rows, k : k + 1], (rows, 128))


def lane_chunk(i):
    return pl.ds(pl.multiple_of(i * 128, 128), 128)


def embed_bytes(ids, table, emb):
    lane = lax.broadcasted_iota(jnp.int32, (ids.shape[0], TABLE), 1)
    emb[...] = nt((ids == lane).astype(bf16), table)


def small_rows(table, small):
    lane = lax.broadcasted_iota(jnp.int32, (8, TABLE), 1)
    row = lax.broadcasted_iota(jnp.int32, (8, TABLE), 0)
    small[...] = nt((lane == row + VOCAB).astype(bf16), table)


def block_probs(emb, small, conv, accs, flat, live, m0, m1, rows):
    accs[0:4] = jnp.zeros((4, rows, 128), f32)

    def step(i, _):
        chunk = lane_chunk(i)
        w0, w1, w2, w3 = [small[k : k + 1, chunk] for k in range(4)]
        scorer = small[4:5, chunk]
        e0, e1, e2, e3 = [emb[k * rows : (k + 1) * rows, chunk] for k in range(4)]
        e3d, e0u, e1u = down(e3), up(e0), up(e1)
        c = (
            w0 * e3d + w1 * e0 + w2 * e1 + w3 * e2,
            w0 * e0 + w1 * e1 + w2 * e2 + w3 * e3,
            w0 * e1 + w1 * e2 + w2 * e3 + w3 * e0u,
            w0 * e2 + w1 * e3 + w2 * e0u + w3 * e1u,
        )
        for k in range(4):
            value = c[k] * live[k]
            conv[k, :, chunk] = value
            accs[k] += value * scorer
        return 0

    lax.fori_loop(0, D // 128, step, 0)
    score = to_lanes(accs, 4, flat)
    three = triples(score, m0, m1)
    p01, p23 = score[0] + score[1], score[2] + score[3]
    quad = 0.25 * (p01 + p23)
    probs = []
    for k in range(4):
        scores = (score[k], 0.5 * (p01, p01, p23, p23)[k], three[k] * (1.0 / 3.0), quad)
        top = jnp.maximum(jnp.maximum(scores[0], scores[1]), jnp.maximum(scores[2], scores[3]))
        powers = [jnp.exp(value - top) for value in scores]
        norm = 1.0 / (powers[0] + powers[1] + powers[2] + powers[3])
        probs.append([power * norm for power in powers])
    return probs


def reach(m0, m1, k, ahead):
    one = jnp.ones(m0[k].shape, f32)
    zero = jnp.zeros_like(one)
    if ahead == 0:
        return one
    if ahead == 1:
        return jnp.where(m0[k] | m1[k], one, zero)
    if ahead == 2:
        return jnp.where(m0[k], one, zero)
    if ahead == -1:
        return jnp.where(m0[k], zero, one)
    return jnp.where(m0[k] | m1[k], zero, one)


def token_weights(probs, m0, m1):
    weights = []
    for half in range(2):
        first, second = probs[2 * half], probs[2 * half + 1]
        pair = 0.5 * (first[1] + second[1])
        quad = 0.25 * (first[3] + second[3])
        row = []
        for j in range(6):
            place = 2 * half - 2 + j
            value = jnp.zeros_like(pair)
            for k, p in ((2 * half, first), (2 * half + 1, second)):
                ahead = place - k
                if abs(ahead) <= 2:
                    value += p[2] * (1.0 / 3.0) * reach(m0, m1, k, ahead)
                if ahead == 0:
                    value += p[0]
            if 0 <= place < 4:
                value += quad
            if place // 2 == half:
                value += pair
            row.append(value)
        weights.append(row)
    return weights


def places(c):
    c0, c1, c2, c3 = c
    return ((down(c2), down(c3), c0, c1, c2, c3), (c0, c1, c2, c3, up(c0), up(c1)))


def pool_kernel(first_ref, ids, table, *rest, rows, total_bytes):
    resid, normed, emb, small, conv, accs, flat, lines, tokens = rest[-9:]
    first = first_ref[0]
    embed_bytes(ids[...], table[...], emb)
    small_rows(table[...], small)

    @pl.when(pl.program_id(0) == 0)
    def _():
        flat[...] = jnp.zeros_like(flat)
        lines[...] = jnp.zeros_like(lines)

    _, m0, m1 = lane_marks(first, flat.shape[0], total_bytes)
    live = live_rows(first, rows, total_bytes)
    probs = block_probs(emb, small, conv, accs, flat, live, m0, m1, rows)
    weights = token_weights(probs, m0, m1)
    to_rows([0.5 * weights[half][j] for half in range(2) for j in range(6)], lines, accs)
    own = rows - 16

    def step(i, square):
        chunk = lane_chunk(i)
        around = places([conv[k, :, chunk] for k in range(4)])
        for half in range(2):
            token = accs[6 * half] * around[half][0]
            for j in range(1, 6):
                token += accs[6 * half + j] * around[half][j]
            tokens[i, pl.ds(half, own, stride=2), :] = token[8 : 8 + own]
        values = tokens[i]
        resid[:, chunk] = values
        return square + values * values

    square = lax.fori_loop(0, D // 128, step, jnp.zeros((2 * own, 128), f32))
    scale = lax.rsqrt(jnp.sum(square, axis=-1, keepdims=True) * (1.0 / D) + epsilon)
    normed[...] = (resid[...] * scale * small[5:6, :]).astype(bf16)


def pool(first, ids, table, deps, total_bytes):
    count, wide, _ = ids.shape
    rows = wide // 4
    tokens = 2 * (rows - 16)
    return pl.pallas_call(
        partial(pool_kernel, rows=rows, total_bytes=total_bytes),
        grid=(count,),
        in_specs=[
            pl.BlockSpec(memory_space=pltpu.SMEM),
            pl.BlockSpec((None, wide, 1), lambda i: (i, 0, 0)),
            pl.BlockSpec((D, TABLE), lambda i: (0, 0)),
        ]
        + [pl.BlockSpec(memory_space=pl.ANY)] * len(deps),
        out_specs=[
            pl.BlockSpec((None, tokens, D), lambda i: (i, 0, 0)),
            pl.BlockSpec((None, tokens, D), lambda i: (i, 0, 0)),
        ],
        out_shape=[
            jax.ShapeDtypeStruct((count, tokens, D), f32),
            jax.ShapeDtypeStruct((count, tokens, D), bf16),
        ],
        scratch_shapes=[
            pltpu.VMEM((wide, D), f32),
            pltpu.VMEM((8, D), f32),
            pltpu.VMEM((4, rows, D), f32),
            pltpu.VMEM((12, rows, 128), f32),
            pltpu.VMEM((2 * 128, 128), f32),
            pltpu.VMEM((16, 2 * 128), f32),
            pltpu.VMEM((D // 128, tokens, 128), f32),
        ],
        cost_estimate=pl.CostEstimate(flops=count * 3_000_000_000, bytes_accessed=4_000_000, transcendentals=0),
        name="pool",
    )(first, ids, table, *deps)


def pool_back_kernel(
    first_ref, ids, ids_row, table, pulled_own, from_core, from_x, dq, query_w, resid, after,
    feed_stats, *rest, rows, total_bytes, given, last, deps,
):
    if given:
        embed_before, small_before = rest[:2]
        rest = rest[2:]
    rest = rest[deps:]
    if last:
        turned = rest[0]
        embed_grad, small_grad = rest[-2:]
        rest = rest[1:-2]
    else:
        embed_grad, small_grad = rest[:2]
        rest = rest[2:]
    emb, small, conv, accs, flat, lines, tokens, pulls, emb_grad = rest
    first = first_ref[0]
    own = rows - 16
    chunks = D // 128

    if given:
        small_grad[...] = small_before[...]
    else:
        small_grad[...] = jnp.zeros_like(small_grad)
    flat[...] = jnp.zeros_like(flat)
    lines[...] = jnp.zeros_like(lines)

    embed_bytes(ids[...], table[...], emb)
    small_rows(table[...], small)
    live_lane, m0, m1 = lane_marks(first, flat.shape[0], total_bytes)
    live = live_rows(first, rows, total_bytes)

    x = resid[...]
    gn = pulled_own[...].astype(f32) + from_core[...].astype(f32) + from_x[...].astype(f32)
    gn = gn + nt(dq[...], query_w[...])
    scale = lax.rsqrt(jnp.mean(x * x, axis=-1, keepdims=True) + epsilon)
    gain = small[5:6, :]
    small_grad[5:6, :] += jnp.sum(gn * x * scale, axis=0, keepdims=True)
    gg = gain * gn
    inner = jnp.mean(gg * x, axis=-1, keepdims=True)
    total = after[...] + scale * gg - x * (scale * scale * scale * inner)
    for i in range(chunks):
        tokens[i] = total[:, i * 128 : (i + 1) * 128]

    probs = block_probs(emb, small, conv, accs, flat, live, m0, m1, rows)
    accs[0:12] = jnp.zeros((12, rows, 128), f32)
    pulls[:, 0:8, :] = jnp.zeros((2, 8, D), f32)
    pulls[:, rows - 8 : rows, :] = jnp.zeros((2, 8, D), f32)

    def dots(i, _):
        chunk = lane_chunk(i)
        around = places([conv[k, :, chunk] for k in range(4)])
        for half in range(2):
            pulls[half, 8 : 8 + own, chunk] = 0.5 * tokens[i, pl.ds(half, own, stride=2), :]
            g = pulls[half, :, chunk]
            for j in range(6):
                accs[6 * half + j] += g * around[half][j]
        return 0

    lax.fori_loop(0, chunks, dots, 0)
    every = to_lanes(accs, 12, flat)
    pulled = []
    for half in range(2):
        at = every[6 * half : 6 * half + 6]
        pair = 0.5 * (at[2] + at[3])
        quad = 0.25 * (at[2] + at[3] + (at[4] + at[5] if half == 0 else at[0] + at[1]))
        for k in (2 * half, 2 * half + 1):
            middle = k - (2 * half - 2)
            three = sum(
                at[middle + ahead] * reach(m0, m1, k, ahead)
                for ahead in range(-2, 3)
                if 0 <= middle + ahead < 6
            ) * (1.0 / 3.0)
            gd = (at[middle], pair, three, quad)
            p = probs[k]
            mean = p[0] * gd[0] + p[1] * gd[1] + p[2] * gd[2] + p[3] * gd[3]
            pulled.append([p[b] * (gd[b] - mean) for b in range(4)])

    spread = triples([pulled[k][2] for k in range(4)], m0, m1)
    quad = 0.25 * (pulled[0][3] + pulled[1][3] + pulled[2][3] + pulled[3][3])
    weights = token_weights(probs, m0, m1)
    factors = []
    for k in range(4):
        half = k // 2
        pair = 0.5 * (pulled[2 * half][1] + pulled[2 * half + 1][1])
        factors.append((pulled[k][0] + pair + spread[k] * (1.0 / 3.0) + quad) * live_lane[k])
    at_row = lax.broadcasted_iota(jnp.int32, (1, flat.shape[0]), 1)
    inside = (at_row >= 8) & (at_row < 8 + own)
    even = [jnp.where(inside, weight, 0.0) for weight in weights[0]]
    odd = [jnp.where(inside, weight, 0.0) for weight in weights[1]]
    reached = (
        (behind_lane(odd[4]), even[2], odd[0]),
        (behind_lane(odd[5]), even[3], odd[1]),
        (even[4], odd[2], ahead_lane(even[0])),
        (even[5], odd[3], ahead_lane(even[1])),
    )
    for k in range(4):
        for j in range(3):
            factors.append(reached[k][j] * live_lane[k])
    to_rows(factors, lines, accs)

    def back(i, _):
        chunk = lane_chunk(i)
        w0, w1, w2, w3 = [small[k : k + 1, chunk] for k in range(4)]
        scorer = small[4:5, chunk]
        g0, g1 = pulls[0, :, chunk], pulls[1, :, chunk]
        g1d, g0u = down(g1), up(g0)
        e0, e1, e2, e3 = [emb[k * rows : (k + 1) * rows, chunk] for k in range(4)]
        near = ((g1d, g0, g1), (g1d, g0, g1), (g0, g1, g0u), (g0, g1, g0u))
        score = jnp.zeros((rows, 128), f32)
        gc = []
        for k in range(4):
            score += accs[k] * conv[k, :, chunk]
            value = accs[k] * scorer
            for j in range(3):
                value += accs[4 + 3 * k + j] * near[k][j]
            gc.append(value)
        small_grad[4:5, chunk] += jnp.sum(score, axis=0, keepdims=True)
        gc0, gc1, gc2, gc3 = gc
        e3d, e0u, e1u = down(e3), up(e0), up(e1)
        taps = (
            gc0 * e3d + gc1 * e0 + gc2 * e1 + gc3 * e2,
            gc0 * e0 + gc1 * e1 + gc2 * e2 + gc3 * e3,
            gc0 * e1 + gc1 * e2 + gc2 * e3 + gc3 * e0u,
            gc0 * e2 + gc1 * e3 + gc2 * e0u + gc3 * e1u,
        )
        for k in range(4):
            small_grad[k : k + 1, chunk] += jnp.sum(taps[k], axis=0, keepdims=True)
        gc3d, gc2d, gc0u = down(gc3), down(gc2), up(gc0)
        grads = (
            w0 * gc1 + w1 * gc0 + w2 * gc3d + w3 * gc2d,
            w0 * gc2 + w1 * gc1 + w2 * gc0 + w3 * gc3d,
            w0 * gc3 + w1 * gc2 + w2 * gc1 + w3 * gc0,
            w0 * gc0u + w1 * gc3 + w2 * gc2 + w3 * gc1,
        )
        for k in range(4):
            emb_grad[k * rows : (k + 1) * rows, chunk] = grads[k].astype(bf16)
        return 0

    lax.fori_loop(0, chunks, back, 0)
    row = lax.broadcasted_iota(jnp.int32, (TABLE, 4 * rows), 0)
    total = nn((ids_row[...] == row).astype(bf16), emb_grad[...])
    if given:
        total = total + embed_before[...]
    embed_grad[...] = total
    if last:
        small_grad[6:7, :] = feed_stats[0:1, :]
        embed_grad[VOCAB : VOCAB + 7, :] = small_grad[0:7, :]
        turned[...] = embed_grad[...].T.astype(bf16)


def pool_back(
    seq, first, ids, ids_row, table, pulled, from_core, from_x, dq, qkv, resid, after_grad,
    feed_stats, before, deps, total_bytes,
):
    count, wide, _ = ids.shape
    rows = wide // 4
    tokens = 2 * (rows - 16)
    last = seq == count - 1
    token_spec = pl.BlockSpec((None, tokens, D), lambda i: (seq, 0, 0))
    table_sum = pl.BlockSpec((TABLE, D), lambda i: (0, 0))
    small_sum = pl.BlockSpec((8, D), lambda i: (0, 0))
    sums = [pltpu.VMEM((TABLE, D), f32), pltpu.VMEM((8, D), f32)]
    return pl.pallas_call(
        partial(
            pool_back_kernel, rows=rows, total_bytes=total_bytes, given=bool(before), last=last,
            deps=len(deps),
        ),
        grid=(1,),
        in_specs=[
            pl.BlockSpec(memory_space=pltpu.SMEM),
            pl.BlockSpec((None, wide, 1), lambda i: (seq, 0, 0)),
            pl.BlockSpec((None, 1, wide), lambda i: (seq, 0, 0)),
            pl.BlockSpec((D, TABLE), lambda i: (0, 0)),
            token_spec,
            token_spec,
            pl.BlockSpec((tokens, D), lambda i: (0, 0)),
            token_spec,
            pl.BlockSpec((D, D), lambda i: (0, 0)),
            token_spec,
            token_spec,
            small_sum,
        ]
        + ([table_sum, small_sum] if before else [])
        + [pl.BlockSpec(memory_space=pl.ANY)] * len(deps),
        out_specs=pl.BlockSpec((D, TABLE), lambda i: (0, 0)) if last else [table_sum, small_sum],
        out_shape=jax.ShapeDtypeStruct((D, TABLE), bf16)
        if last
        else [jax.ShapeDtypeStruct((TABLE, D), f32), jax.ShapeDtypeStruct((8, D), f32)],
        scratch_shapes=[
            pltpu.VMEM((wide, D), f32),
            pltpu.VMEM((8, D), f32),
            pltpu.VMEM((4, rows, D), f32),
            pltpu.VMEM((16, rows, 128), f32),
            pltpu.VMEM((2 * 128, 128), f32),
            pltpu.VMEM((16, 2 * 128), f32),
            pltpu.VMEM((D // 128, tokens, 128), f32),
            pltpu.VMEM((2, rows, D), f32),
            pltpu.VMEM((wide, D), bf16),
        ]
        + (sums if last else []),
        cost_estimate=pl.CostEstimate(flops=9_000_000_000, bytes_accessed=8_000_000, transcendentals=0),
        name="pool_back",
    )(
        first, ids, ids_row, table, pulled, from_core, from_x, dq, qkv, resid, after_grad,
        feed_stats, *before, *deps,
    )


def prepare_kernel(
    rank_ref, lengths_ref, bias_ref, lanes_bias, tile, turned, side, diag, *, queries, keys, parts
):
    head = pl.program_id(0)
    rank = rank_ref[0]

    @pl.when(head == 0)
    def _():
        place = lax.broadcasted_iota(jnp.int32, (BUCKETS, 6 * HALF), 1)
        inside = lax.rem(place, 2 * HALF)
        offset = jnp.where(inside < HALF, inside, inside - 2 * HALF)
        relative = (place // (2 * HALF) - 1) * HALF + offset
        bucket = lax.broadcasted_iota(jnp.int32, (BUCKETS, 6 * HALF), 0)
        hot = (bucket_of(relative) == bucket).astype(bf16)
        diag[...] = lax.dot_general(
            lanes_bias[...], hot, (((0,), (0,)), ((), ())), preferred_element_type=f32
        )
        row = lax.broadcasted_iota(jnp.int32, (keys, SIDE), 0)
        lane = lax.broadcasted_iota(jnp.int32, (keys, SIDE), 1)
        at = lax.rem(rank * queries - HALF + row + keys, keys)
        far = row >= queries + 2 * HALF
        right = far & (at > rank * queries)
        left = far & (at <= rank * queries)
        fixed = jnp.where(
            right,
            lanes_bias[31:32, :].astype(f32),
            jnp.where(left, lanes_bias[15:16, :].astype(f32), 0.0),
        )
        fixed = jnp.where((lane >= ONES) & (lane < ONES + 3), 1.0, fixed)
        fixed = jnp.where((lane == LEFT) & left | (lane == RIGHT) & right, 1.0, fixed)
        for s in range(side.shape[0]):
            masked = jnp.where(2 * at < lengths_ref[s], 0.0, masked_score)
            side[s] = jnp.where(lane == 0, masked, fixed).astype(bf16)

    blocks = []
    for index in range(3):
        line = diag[pl.ds(head + 1, 1), index * 2 * HALF : (index + 1) * 2 * HALF]
        full = jnp.broadcast_to(line, (HALF, 2 * HALF))
        blocks.append(pltpu.roll(full, 0, 1, stride=1, stride_axis=0)[:, :HALF])
    turned_blocks = [block.T.astype(bf16) for block in blocks]
    blocks = [block.astype(bf16) for block in blocks]
    behind = jnp.full((HALF, HALF), bias_ref[15, head], f32).astype(bf16)
    ahead = jnp.full((HALF, HALF), bias_ref[31, head], f32).astype(bf16)
    steps = queries // HALF
    for q in range(steps):
        for n in range(steps + 2):
            apart = n - 1 - q
            wrapped = ((n == 0) & (rank == 0), (n == steps + 1) & (rank == parts - 1))
            plain = behind if apart < -1 else ahead if apart > 1 else blocks[apart + 1]
            flipped = behind if apart < -1 else ahead if apart > 1 else turned_blocks[apart + 1]
            if n == 0:
                plain = jnp.where(wrapped[0], ahead, plain)
                flipped = jnp.where(wrapped[0], ahead, flipped)
            if n == steps + 1:
                plain = jnp.where(wrapped[1], behind, plain)
                flipped = jnp.where(wrapped[1], behind, flipped)
            tile[q * HALF : (q + 1) * HALF, n * HALF : (n + 1) * HALF] = plain
            turned[n * HALF : (n + 1) * HALF, q * HALF : (q + 1) * HALF] = flipped


def prepare(rank, lengths, bias, queries, keys, parts):
    near = queries + 2 * HALF
    seqs = lengths.shape[0]
    lanes_bias = jnp.pad(bias, ((0, 0), (1, SIDE - 1 - HEADS)))
    smem = pl.BlockSpec(memory_space=pltpu.SMEM)
    return pl.pallas_call(
        partial(prepare_kernel, queries=queries, keys=keys, parts=parts),
        grid=(HEADS,),
        in_specs=[smem, smem, smem, pl.BlockSpec((BUCKETS, SIDE), lambda i: (0, 0))],
        out_specs=[
            pl.BlockSpec((None, queries, near), lambda i: (i, 0, 0)),
            pl.BlockSpec((None, near, queries), lambda i: (i, 0, 0)),
            pl.BlockSpec((seqs, keys, SIDE), lambda i: (0, 0, 0)),
        ],
        out_shape=[
            jax.ShapeDtypeStruct((HEADS, queries, near), bf16),
            jax.ShapeDtypeStruct((HEADS, near, queries), bf16),
            jax.ShapeDtypeStruct((seqs, keys, SIDE), bf16),
        ],
        scratch_shapes=[pltpu.VMEM((SIDE, 6 * HALF), f32)],
        cost_estimate=pl.CostEstimate(flops=6_000_000_000, bytes_accessed=7_000_000, transcendentals=0),
        name="prepare",
    )(rank, lengths, bias.astype(f32), lanes_bias)


def row_offset(rank, step, blocks):
    half = lax.rem(2 * rank - 1 + step + 2 * blocks, 2 * blocks)
    apart = jnp.bitwise_xor(rank, half // 2)
    slot = (apart % 2) * 2 + apart // 2
    return pl.multiple_of(slot * (2 * HALF) + (half % 2) * HALF, HALF)


def side_lanes(rows, picks):
    lane = lax.broadcasted_iota(jnp.int32, (rows, SIDE), 1)
    value = jnp.zeros((rows, SIDE), f32)
    for index, entry in picks:
        value = jnp.where(lane == index, entry, value)
    return value.astype(bf16)


def three_parts(value):
    high = value.astype(bf16).astype(f32)
    rest = value - high
    middle = rest.astype(bf16).astype(f32)
    return high, middle, rest - middle


def one_head(values, head):
    lane = lax.broadcasted_iota(jnp.int32, values.shape, 1)
    return jnp.where((lane // HEAD_DIM) == head, values, jnp.zeros_like(values))


def attend_kernel(rank_ref, q, kv, side, bias, out, norm, kcat, vcat, *, near, blocks):
    rank = rank_ref[0]
    pair = pl.program_id(1)
    queries = q.shape[0]

    @pl.when(pair == 0)
    def _():
        kcat[:, SIDE:] = side[...]
        norm[...] = jnp.zeros_like(norm)

    for step in range(2 * blocks):
        source = pl.ds(row_offset(rank, step, blocks), HALF)
        kcat[step * HALF : (step + 1) * HALF, :SIDE] = kv[source, :SIDE]
        vcat[step * HALF : (step + 1) * HALF, :] = kv[source, SIDE:]

    lane = lax.broadcasted_iota(jnp.int32, (queries, SIDE), 1)
    halves, every = [], []
    for head in range(2):
        extra = side_lanes(queries, [(0, 1.0), (1 + 2 * pair + head, 1.0)])
        wide = jnp.concatenate([one_head(q[...], head), extra], axis=1)
        every.append(nt(wide, kcat[...]))
    for head in range(2):
        logits = every[head]
        close = logits[:, :near] + bias[head].astype(f32)
        away = logits[:, near:]
        top = jnp.maximum(
            jnp.max(close, axis=-1, keepdims=True), jnp.max(away, axis=-1, keepdims=True)
        )
        close = jnp.exp(close - top)
        away = jnp.exp(away - top)
        total = jnp.sum(close, axis=-1, keepdims=True) + jnp.sum(away, axis=-1, keepdims=True)
        mixed = nn(close.astype(bf16), vcat[:near, :]) + nn(away.astype(bf16), vcat[near:, :])
        halves.append(mixed * (1.0 / total))
        norm[...] = jnp.where(lane == 2 * pair + head, top + jnp.log(total), norm[...])
    out[...] = jnp.where(lane < HEAD_DIM, halves[0], halves[1]).astype(bf16)


def attend(rank, q, kv, side, bias):
    seqs, queries, _ = q.shape
    keys = kv.shape[1]
    near = bias.shape[-1]
    blocks = keys // queries
    return pl.pallas_call(
        partial(attend_kernel, near=near, blocks=blocks),
        grid=(seqs, PAIRS),
        in_specs=[
            pl.BlockSpec(memory_space=pltpu.SMEM),
            pl.BlockSpec((None, queries, SIDE), lambda s, i: (s, 0, i)),
            pl.BlockSpec((None, keys, 2 * SIDE), lambda s, i: (s, 0, i)),
            pl.BlockSpec((None, keys, SIDE), lambda s, i: (s, 0, 0)),
            pl.BlockSpec((2, queries, near), lambda s, i: (i, 0, 0)),
        ],
        out_specs=[
            pl.BlockSpec((None, queries, SIDE), lambda s, i: (s, 0, i)),
            pl.BlockSpec((None, queries, SIDE), lambda s, i: (s, 0, 0)),
        ],
        out_shape=[
            jax.ShapeDtypeStruct((seqs, queries, D), bf16),
            jax.ShapeDtypeStruct((seqs, queries, SIDE), f32),
        ],
        scratch_shapes=[pltpu.VMEM((keys, 2 * SIDE), bf16), pltpu.VMEM((keys, SIDE), bf16)],
        cost_estimate=pl.CostEstimate(flops=25_000_000_000, bytes_accessed=8_000_000, transcendentals=0),
        name="attend",
    )(rank, q, kv, side, bias)


def attend_back_kernel(
    rank_ref, q, kv, side, bias, norm, mixed, grad, dq, dkv, dnear, dfar, kcat, vcat, kturn, *,
    near, blocks, part,
):
    rank = rank_ref[0]
    pair = pl.program_id(1)
    queries = q.shape[0]
    keys = kv.shape[0]

    @pl.when(pair == 0)
    def _():
        kcat[:, SIDE:] = side[...]
        vcat[:, SIDE:] = side[...]
        kturn[SIDE:, :] = side[...].astype(f32).T[ONES : 2 * ONES, :].astype(bf16)

    for step in range(2 * blocks):
        source = pl.ds(row_offset(rank, step, blocks), HALF)
        kcat[step * HALF : (step + 1) * HALF, :SIDE] = kv[source, :SIDE]
        vcat[step * HALF : (step + 1) * HALF, :SIDE] = kv[source, SIDE:]
    kturn[:SIDE, :] = kcat[:, :SIDE].astype(f32).T.astype(bf16)

    lane = lax.broadcasted_iota(jnp.int32, (queries, SIDE), 1)
    queries_of, grads_of, wide_q, wide_g = [], [], [], []
    products = grad[...].astype(f32) * mixed[...].astype(f32)
    for head in range(2):
        index = 2 * pair + head
        level = jnp.sum(jnp.where(lane == index, norm[...], 0.0), axis=-1, keepdims=True)
        delta = jnp.sum(
            jnp.where((lane // HEAD_DIM) == head, products, 0.0), axis=-1, keepdims=True
        )
        la, lb, lc = three_parts(-level)
        da, db, dc = three_parts(-delta)
        queries_of.append(one_head(q[...], head))
        grads_of.append(one_head(grad[...], head))
        extra = [(0, 1.0), (1 + index, 1.0), (ONES, la), (ONES + 1, lb), (ONES + 2, lc)]
        wide_q.append(jnp.concatenate([queries_of[head], side_lanes(queries, extra)], axis=1))
        extra = [(ONES, da), (ONES + 1, db), (ONES + 2, dc)]
        wide_g.append(jnp.concatenate([grads_of[head], side_lanes(queries, extra)], axis=1))

    sums = [jnp.zeros((kturn.shape[0], queries), f32) for _ in range(2)]
    for base in range(0, keys, part):
        span = slice(base, base + part)
        value_part = jnp.zeros((part, SIDE), f32)
        key_part = jnp.zeros((part, SIDE), f32)
        for head in range(2):
            logits = nt(kcat[span, :], wide_q[head])
            if base < near:
                here = min(near, base + part) - base
                close = logits[:here] + bias[head, base : base + here, :].astype(f32)
                logits = close if here == part else jnp.concatenate([close, logits[here:]], axis=0)
            probs = jnp.exp(logits)
            pull = nt(vcat[span, :], wide_g[head])
            low = (probs * pull).astype(bf16)
            value_part += nn(probs.astype(bf16), grads_of[head])
            key_part += nn(low, queries_of[head])
            sums[head] += nn(kturn[:, span], low)
            if base < near:
                here = min(near, base + part) - base
                dnear[head, base : base + here, :] = low[:here]
        for step in range(base // HALF, (base + part) // HALF):
            target = pl.ds(row_offset(rank, step, blocks), HALF)
            inner = slice(step * HALF - base, (step + 1) * HALF - base)
            dkv[target, :SIDE] = key_part[inner].astype(bf16)
            dkv[target, SIDE:] = value_part[inner].astype(bf16)
    turned = jnp.concatenate([sums[0][:HEAD_DIM], sums[1][HEAD_DIM:SIDE]], axis=0)
    dq[...] = turned.T.astype(bf16)
    for head in range(2):
        dfar[head] = sums[head][SIDE:, :]


def attend_back(rank, q, kv, side, bias, norm, mixed, grad):
    seqs, queries, _ = q.shape
    keys = kv.shape[1]
    near = bias.shape[1]
    blocks = keys // queries
    own = pl.BlockSpec((None, queries, SIDE), lambda s, i: (s, 0, i))
    every = pl.BlockSpec((None, keys, 2 * SIDE), lambda s, i: (s, 0, i))
    return pl.pallas_call(
        partial(attend_back_kernel, near=near, blocks=blocks, part=KEY_PART),
        grid=(seqs, PAIRS),
        in_specs=[
            pl.BlockSpec(memory_space=pltpu.SMEM),
            own,
            every,
            pl.BlockSpec((None, keys, SIDE), lambda s, i: (s, 0, 0)),
            pl.BlockSpec((2, near, queries), lambda s, i: (i, 0, 0)),
            pl.BlockSpec((None, queries, SIDE), lambda s, i: (s, 0, 0)),
            own,
            own,
        ],
        out_specs=[
            own,
            every,
            pl.BlockSpec((None, 2, near, queries), lambda s, i: (s, i, 0, 0)),
            pl.BlockSpec((None, 2, ONES, queries), lambda s, i: (s, i, 0, 0)),
        ],
        out_shape=[
            jax.ShapeDtypeStruct((seqs, queries, D), bf16),
            jax.ShapeDtypeStruct((seqs, keys, 2 * D), bf16),
            jax.ShapeDtypeStruct((seqs, HEADS, near, queries), bf16),
            jax.ShapeDtypeStruct((seqs, HEADS, ONES, queries), f32),
        ],
        scratch_shapes=[
            pltpu.VMEM((keys, 2 * SIDE), bf16),
            pltpu.VMEM((keys, 2 * SIDE), bf16),
            pltpu.VMEM((SIDE + ONES, keys), bf16),
        ],
        cost_estimate=pl.CostEstimate(flops=40_000_000_000, bytes_accessed=12_000_000, transcendentals=0),
        name="attend_back",
    )(rank, q, kv, side, bias, norm, mixed, grad)


def bias_grad_kernel(rank_ref, near, far, *rest, parts):
    out, lines = rest[-2:]
    rank = rank_ref[0]
    head = pl.program_id(0)
    seqs = near.shape[0]
    steps = near.shape[1] // HALF - 2
    first_in, last_in = rank != 0, rank != parts - 1

    def block(n, q):
        rows, cols = slice(n * HALF, (n + 1) * HALF), slice(q * HALF, (q + 1) * HALF)
        return sum(near[s, rows, cols].astype(f32) for s in range(seqs))

    sums = [jnp.zeros((HALF, HALF), f32) for _ in range(3)]
    left = sum(far[s, LEFT - ONES : LEFT - ONES + 1, :] for s in range(seqs))
    right = sum(far[s, RIGHT - ONES : RIGHT - ONES + 1, :] for s in range(seqs))
    left = [left[:, q * HALF : (q + 1) * HALF] for q in range(steps)]
    right = [right[:, q * HALF : (q + 1) * HALF] for q in range(steps)]
    for n in range(steps + 2):
        inside = first_in if n == 0 else last_in if n == steps + 1 else None
        for q in range(steps):
            value = block(n, q)
            apart = n - 1 - q
            if inside is not None:
                column = jnp.sum(value, axis=0, keepdims=True)
                outer = jnp.where(inside, 0.0, column)
                if n == 0:
                    right[q] += outer
                else:
                    left[q] += outer
                kept = jnp.where(inside, column, 0.0)
                if apart < -1:
                    left[q] += kept
                elif apart > 1:
                    right[q] += kept
                value = jnp.where(inside, value, 0.0)
            if abs(apart) <= 1:
                sums[apart + 1] += value
    found = []
    for value in sums:
        wide = jnp.concatenate([value, jnp.zeros((HALF, HALF), f32)], axis=1)
        folded = wide[0:8, :]
        for a in range(8, HALF, 8):
            folded += pltpu.roll(wide[a : a + 8, :], 2 * HALF - a, 1)
        line = folded[0:1, :]
        for b in range(1, 8):
            line += pltpu.roll(folded[b : b + 1, :], 2 * HALF - b, 1)
        found.append(line)
    found += [jnp.concatenate(left, axis=1), jnp.concatenate(right, axis=1)]
    lines[pl.ds(head, 1), :] = jnp.concatenate(found, axis=1)

    @pl.when(head == pl.num_programs(0) - 1)
    def _():
        shape = (10 * HALF, 128)
        place = lax.broadcasted_iota(jnp.int32, shape, 0)
        lane = lax.broadcasted_iota(jnp.int32, shape, 1)
        segment, inner = place // (2 * HALF), lax.rem(place, 2 * HALF)
        behind = jnp.where(inner < HALF, inner, inner - 2 * HALF)
        relative = (segment - 1) * HALF - behind
        bucket = jnp.where(segment == 3, 15, jnp.where(segment == 4, 31, bucket_of(relative)))
        hot = (bucket == lane).astype(bf16)
        split = jnp.concatenate([part.astype(bf16) for part in three_parts(lines[...])], axis=0)
        total = nn(split, hot)
        rows = lines.shape[0]
        out[...] = total[:rows] + total[rows : 2 * rows] + total[2 * rows :]


def bias_sums(rank, near_parts, far_parts, parts, deps):
    seqs, heads, near, queries = near_parts.shape
    assert queries == 2 * HALF
    return pl.pallas_call(
        partial(bias_grad_kernel, parts=parts),
        grid=(heads,),
        in_specs=[
            pl.BlockSpec(memory_space=pltpu.SMEM),
            pl.BlockSpec((seqs, None, near, queries), lambda i: (0, i, 0, 0)),
            pl.BlockSpec((seqs, None, ONES, queries), lambda i: (0, i, 0, 0)),
        ]
        + [pl.BlockSpec(memory_space=pl.ANY)] * len(deps),
        out_specs=pl.BlockSpec((16, 128), lambda i: (0, 0)),
        out_shape=jax.ShapeDtypeStruct((16, 128), f32),
        scratch_shapes=[pltpu.VMEM((16, 10 * HALF), f32)],
        cost_estimate=pl.CostEstimate(flops=6_000_000_000, bytes_accessed=9_000_000, transcendentals=0),
        name="bias_sums",
    )(rank, near_parts, far_parts, *deps)


def gelu_parts(x):
    inner = 0.7978845608028654 * (x + 0.044715 * (x * x * x))
    t = jnp.tanh(inner)
    half = 0.5 * (1.0 + t)
    slope = half + 0.5 * x * (1.0 - t * t) * (
        0.7978845608028654 * (1.0 + 0.134145 * (x * x))
    )
    return x * half, slope


def feed_kernel(
    place_ref, count_ref, lengths_ref, att, resid, teacher, gain, wide_hbm, down_hbm,
    block_out, normed, hidden, branch, gate_low, up_low, after_grad, after_low, att_grad, stats,
    act, steep, gate_w, up_w, down_w, output_w, sems, *, chunk,
):
    step = pl.program_id(0)
    rows = att.shape[0]
    ffn_dim = gate_w.shape[1]
    copies = [
        pltpu.make_async_copy(wide_hbm.at[:, 3 * ffn_dim : 3 * ffn_dim + D], output_w, sems.at[0]),
        pltpu.make_async_copy(wide_hbm.at[:, 0:ffn_dim], gate_w, sems.at[1]),
        pltpu.make_async_copy(wide_hbm.at[:, ffn_dim : 2 * ffn_dim], up_w, sems.at[2]),
        pltpu.make_async_copy(down_hbm, down_w, sems.at[3]),
    ]

    @pl.when(step == 0)
    def _():
        for copy in copies:
            copy.start()

    def arrived(index):
        @pl.when(step == 0)
        def _():
            copies[index].wait()

    @pl.when(step == 0)
    def _():
        stats[...] = jnp.zeros_like(stats)

    arrived(0)
    after = resid[...] + nn(att[...], output_w[...])
    scale = lax.rsqrt(jnp.mean(after * after, axis=-1, keepdims=True) + epsilon)
    normed[...] = (after * scale * gain[...]).astype(bf16)
    arrived(1)
    arrived(2)
    arrived(3)
    out = after
    for base in range(0, ffn_dim, chunk):
        span = slice(base, base + chunk)
        gate = nn(normed[...], gate_w[:, span])
        up_part = nn(normed[...], up_w[:, span])
        value, slope = gelu_parts(gate)
        act[:, span] = value
        steep[:, span] = slope * up_part
        low = (value * up_part).astype(bf16)
        hidden[:, span] = low
        out = out + nn(low, down_w[span, :])
    block_out[...] = out
    token = place_ref[0] + lax.broadcasted_iota(jnp.int32, (rows, D), 0)
    live = (2 * token < lengths_ref[step]).astype(f32)
    error = live * (out - teacher[...])
    stats[1:2, :] += jnp.sum(error * error, axis=0, keepdims=True)
    out_grad = (2.0 / count_ref[0]) * error
    branch[...] = out_grad.astype(bf16)
    back = jnp.zeros((rows, D), f32)
    for base in range(0, ffn_dim, chunk):
        span = slice(base, base + chunk)
        pull = nt(branch[...], down_w[span, :])
        gate_part = (pull * steep[:, span]).astype(bf16)
        up_part = (pull * act[:, span]).astype(bf16)
        gate_low[:, span] = gate_part
        up_low[:, span] = up_part
        back = back + nt(gate_part, gate_w[:, span]) + nt(up_part, up_w[:, span])
    stats[0:1, :] += jnp.sum(back * after * scale, axis=0, keepdims=True)
    gained = back * gain[...]
    inner = jnp.mean(gained * after, axis=-1, keepdims=True)
    total = out_grad + scale * gained - after * (scale * scale * scale * inner)
    after_grad[...] = total
    low = total.astype(bf16)
    after_low[...] = low
    att_grad[...] = nt(low, output_w[...]).astype(bf16)


def feed(place, count, lengths, att, resid, teacher, gain, wide, down_w):
    tokens = att.shape[0]
    seqs = lengths.shape[0]
    rows = tokens // seqs
    ffn_dim = down_w.shape[0]
    own = pl.BlockSpec((rows, D), lambda i: (i, 0))
    broad = pl.BlockSpec((rows, ffn_dim), lambda i: (i, 0))
    smem = pl.BlockSpec(memory_space=pltpu.SMEM)
    return pl.pallas_call(
        partial(feed_kernel, chunk=512),
        grid=(seqs,),
        in_specs=[
            smem,
            smem,
            smem,
            own,
            pl.BlockSpec((None, rows, D), lambda i: (i, 0, 0)),
            own,
            pl.BlockSpec((1, D), lambda i: (0, 0)),
            pl.BlockSpec(memory_space=pl.ANY),
            pl.BlockSpec(memory_space=pl.ANY),
        ],
        out_specs=[own, own, broad, own, broad, broad, own, own, own, pl.BlockSpec((8, D), lambda i: (0, 0))],
        out_shape=[
            jax.ShapeDtypeStruct((tokens, D), f32),
            jax.ShapeDtypeStruct((tokens, D), bf16),
            jax.ShapeDtypeStruct((tokens, ffn_dim), bf16),
            jax.ShapeDtypeStruct((tokens, D), bf16),
            jax.ShapeDtypeStruct((tokens, ffn_dim), bf16),
            jax.ShapeDtypeStruct((tokens, ffn_dim), bf16),
            jax.ShapeDtypeStruct((tokens, D), f32),
            jax.ShapeDtypeStruct((tokens, D), bf16),
            jax.ShapeDtypeStruct((tokens, D), bf16),
            jax.ShapeDtypeStruct((8, D), f32),
        ],
        scratch_shapes=[
            pltpu.VMEM((rows, ffn_dim), f32),
            pltpu.VMEM((rows, ffn_dim), f32),
            pltpu.VMEM((D, ffn_dim), bf16),
            pltpu.VMEM((D, ffn_dim), bf16),
            pltpu.VMEM((ffn_dim, D), bf16),
            pltpu.VMEM((D, D), bf16),
            pltpu.SemaphoreType.DMA((4,)),
        ],
        cost_estimate=pl.CostEstimate(flops=17_000_000_000, bytes_accessed=30_000_000, transcendentals=0),
        name="feed",
    )(place, count, lengths, att, resid, teacher, gain, wide, down_w)


def dot(a, b):
    return jnp.dot(a, b, preferred_element_type=f32)


def per_device(
    byte_ids,
    lengths,
    teacher,
    embed_table,
    conv_weight,
    score_weight,
    attn_gain,
    rel_bias,
    query_weight,
    key_weight,
    value_weight,
    output_weight,
    ffn_gain,
    gate_weight,
    up_weight,
    down_weight,
):
    seqs, own_bytes = byte_ids.shape
    own = own_bytes // 2
    parts = lax.axis_size("seq")
    dp_size = lax.axis_size("dp")
    rank = lax.axis_index("seq")
    total_tokens, total_bytes = own * parts, own_bytes * parts
    shard = score_weight.shape[0]
    rank_ref = rank.reshape(1).astype(jnp.int32)

    tiled = down_weight.shape[0] % 64 == 0
    third = D // 3
    columns, *attn_halves, packed = (pack if tiled else pack_plain)(
        rank_ref, lengths, embed_table, conv_weight,
        (score_weight[None], attn_gain[None], ffn_gain[None]),
        (query_weight, key_weight, value_weight),
        (gate_weight, up_weight, down_weight, output_weight), total_tokens,
    )
    ids_low = jnp.stack([byte_ids // 16, byte_ids % 16]).astype(bf16)
    id_rows = ids_low.reshape(-1, TABLE)
    cut = attn_halves[0].shape[1]
    qkv_halves = [
        RowGather(attn_halves[0], gather_order("y")),
        RowGather(attn_halves[1], gather_order("x")),
    ]
    small = RowGather(columns, axis_bits("dp"))
    while small.order:
        small.start()
        for each in qkv_halves:
            each.finish()
            if len(each.order) > 3:
                each.start()
        small.finish()
    value = small.value.reshape(-1, TABLE)
    mine = jnp.concatenate([value, id_rows], axis=0)
    x_other = swap(mine, "seq", 2)
    pair = jnp.concatenate([mine, x_other], axis=0)
    c_other = swap(pair, "seq", 1)
    wide_rows = mine.shape[0]
    quarters = jnp.concatenate([pair, c_other], axis=0).reshape(parts, wide_rows, TABLE)
    apart = jnp.bitwise_xor(rank, jnp.arange(parts))
    slots = (apart % 2) * 2 + apart // 2
    ordered = jnp.take(quarters, slots, axis=0)
    table = (
        ordered[:, : dp_size * shard]
        .reshape(parts, dp_size, shard, TABLE)
        .transpose(1, 0, 2, 3)
        .reshape(D, TABLE)
    )
    all_ids = ordered[:, dp_size * shard :].reshape(parts, 2, seqs, own_bytes).astype(jnp.int32)
    all_ids = (all_ids[:, 0] * 16 + all_ids[:, 1]).transpose(1, 0, 2).reshape(seqs, total_bytes)
    counts = jnp.sum(table[:, VOCAB + 7 : VOCAB + 9].astype(f32), axis=0)
    live_count = counts[0] * 64.0 + counts[1]
    ffn_gain_full = table[:, VOCAB + 6].astype(f32)

    padded_ids = jnp.pad(all_ids, ((0, 0), (32, 32)), constant_values=-1)
    first_byte = (rank * own_bytes).astype(jnp.int32)
    first_other = (jnp.bitwise_xor(rank, 2) * own_bytes).astype(jnp.int32)

    def phases(start):
        window = lax.dynamic_slice_in_dim(padded_ids, start, own_bytes + 64, 1)
        return window.reshape(seqs, -1, 4).transpose(0, 2, 1).reshape(seqs, -1)

    phase_ids = phases(first_byte)
    other_ids = phases(first_other)

    ffn_dim = gate_weight.shape[1]
    ffn_dim = gate_weight.shape[1]
    wide_full = lax.all_gather(packed, both, axis=0, tiled=True)
    down_full = wide_full[:, 2 * ffn_dim : 3 * ffn_dim]
    if tiled:
        down_full = down_full.reshape(-1, 3, 8, 8, third).transpose(0, 3, 2, 1, 4)
    down_full = down_full.reshape(ffn_dim, D)

    for each in qkv_halves:
        each.start()
    tile, turned_tile, side = prepare(
        after(rank_ref, table), lengths, rel_bias, own, total_tokens, parts
    )
    for each in qkv_halves:
        each.finish(tile)
        each.start()
    residual, normed_own = pool(
        first_byte.reshape(1), phase_ids[:, :, None], table,
        [tile] + [each.value for each in qkv_halves], total_bytes,
    )
    own_other = swap(normed_own, "seq", 1)
    for each in qkv_halves:
        each.finish(normed_own)
        each.start()
    _, normed_x = pool(
        first_other.reshape(1), other_ids[:, :, None], table,
        [normed_own] + [each.value for each in qkv_halves], total_bytes,
    )
    x_side = swap(normed_x, "seq", 1)
    for each in qkv_halves:
        each.finish(normed_x)
    qkv_full = jnp.concatenate([each.result().reshape(D, cut) for each in qkv_halves], axis=1)
    query_full, kv_full = qkv_full[:, :D], qkv_full[:, D:]
    normed = jnp.concatenate([normed_own, normed_x, own_other, x_side], axis=1)
    own_rows = normed_own.reshape(-1, D)
    queries = dot(own_rows, query_full).astype(bf16).reshape(seqs, own, D)
    pairs_kv = dot(normed.reshape(-1, D), kv_full).astype(bf16).reshape(seqs, total_tokens, 2 * D)
    attended, norms = attend(rank_ref, queries, pairs_kv, side, tile)

    token_rows = seqs * own
    att = attended.reshape(token_rows, D)
    (
        block_out, ffn_in, hidden, branch_grad, gate_low, up_low, after_grad, after_low,
        attended_grad, feed_stats,
    ) = feed(
        (rank * own).reshape(1), live_count.reshape(1), lengths, att,
        residual, teacher.reshape(token_rows, D), ffn_gain_full[None],
        wide_full, down_full,
    )
    down_grad = jnp.einsum("tf,td->fd", hidden, branch_grad, preferred_element_type=f32)
    gate_grad = jnp.einsum("td,tf->df", ffn_in, gate_low, preferred_element_type=f32)
    up_grad = jnp.einsum("td,tf->df", ffn_in, up_low, preferred_element_type=f32)
    output_grad = jnp.einsum("td,te->de", att, after_low, preferred_element_type=f32).astype(bf16)
    down_grad = down_grad.astype(bf16)
    if tiled:
        down_grad = down_grad.reshape(-1, 8, 8, 3, third).transpose(0, 3, 2, 1, 4)
    wide_grad = jnp.concatenate(
        [
            gate_grad.astype(bf16),
            up_grad.astype(bf16),
            down_grad.reshape(D, ffn_dim),
            output_grad,
        ],
        axis=1,
    )
    wide_sum = lax.psum_scatter(wide_grad, both, scatter_dimension=0, tiled=True)
    turn = after(attended_grad, wide_grad).reshape(seqs, own, D)
    dq, dkv, near_parts, far_parts = attend_back(
        rank_ref, queries, pairs_kv, side, turned_tile, norms, attended, turn
    )
    dq_rows, dkv_rows = dq.reshape(-1, D), dkv.reshape(-1, 2 * D)
    pulled = jnp.einsum("te,de->td", dkv_rows, kv_full, preferred_element_type=f32)
    pulled = pulled.astype(bf16).reshape(seqs, total_tokens, D)
    to_core = pulled[:, 2 * own :]
    from_core = swap(to_core, "seq", 1)
    query_grad = jnp.einsum(
        "td,te->de", own_rows, after(dq_rows, to_core), preferred_element_type=f32
    ).astype(bf16)
    from_core = after(from_core, query_grad)
    to_x = [
        (pulled[s, own : 2 * own].astype(f32) + from_core[s, own:].astype(f32)).astype(bf16)
        for s in range(seqs)
    ]
    from_x = [swap(rows, "seq", 2) for rows in to_x]
    normed_rows = normed.reshape(-1, D)
    kv_grad = jnp.einsum(
        "td,te->de", normed_rows, after(dkv_rows, *to_x), preferred_element_type=f32
    ).astype(bf16)
    attn_sum = RowSum(jnp.concatenate([query_grad, kv_grad], axis=1)[None], sum_order("y"))
    attn_sum.start()
    attn_sum.finish()
    attn_sum.start()
    bias_rows = bias_sums(rank_ref, near_parts, far_parts, parts, [attn_sum.sent])
    shared = SumEverywhere(
        jnp.where(
            (jnp.arange(16) < HEADS)[:, None],
            bias_rows,
            jnp.broadcast_to(jnp.sum(feed_stats[1]), (16, 128)),
        )
    )
    shared.start()
    sums, deps = (), [bias_rows]
    for s in range(seqs):
        sums = pool_back(
            s, first_byte.reshape(1), phase_ids[:, :, None], phase_ids[:, None, :], table,
            pulled, from_core, from_x[s], dq, qkv_full, residual,
            after_grad.reshape(seqs, own, D), feed_stats, sums, deps, total_bytes,
        )
        if s < seqs - 1:
            shared.finish(sums[1])
            shared.start()
            deps = [shared.value]
        if s < seqs - 1:
            attn_sum.finish(sums[1])
            attn_sum.start()
            deps.append(attn_sum.sent)
    shared.finish(sums)
    shared.start()
    front_sum = RowSum(sums[None], sum_order("x"))
    while front_sum.order:
        front_sum.start()
        for each in (attn_sum, shared):
            each.finish()
            each.start()
        front_sum.finish()
    front_sum = front_sum.result().reshape(shard, TABLE).T
    every = shared.result()
    bias_grad = every[:HEADS, :BUCKETS].T
    attn_sum = attn_sum.result()[0]
    kv_sum = attn_sum[:, D : 3 * D].reshape(shard, PAIRS, 2, SIDE)
    wide_sum = wide_sum.astype(f32)
    gate_sum, up_sum = wide_sum[:, :ffn_dim], wide_sum[:, ffn_dim : 2 * ffn_dim]
    down_sum = wide_sum[:, 2 * ffn_dim : 3 * ffn_dim]
    if tiled:
        down_sum = down_sum.reshape(-1, 3, 8, 8, third).transpose(0, 3, 2, 1, 4)
    down_sum = down_sum.reshape(-1, D)

    return (
        block_out.reshape(seqs, own, D),
        every[HEADS, 0] / live_count,
        front_sum[:VOCAB],
        front_sum[VOCAB : VOCAB + 4],
        front_sum[VOCAB + 4],
        front_sum[VOCAB + 5],
        bias_grad,
        attn_sum[:, :D],
        kv_sum[:, :, 0].reshape(shard, D),
        kv_sum[:, :, 1].reshape(shard, D),
        wide_sum[:, 3 * ffn_dim :],
        front_sum[VOCAB + 6],
        gate_sum,
        up_sum,
        down_sum,
    )


def solution(mesh):
    tokens = P("dp", "seq", None)
    features = P(("dp", "seq"))
    columns = P(None, ("dp", "seq"))
    rows = P(("dp", "seq"), None)
    in_specs = (
        P("dp", "seq"), P("dp"), tokens, columns, columns, features, features, P(),
        rows, rows, rows, rows, features, rows, rows, rows,
    )
    out_specs = (
        tokens, P(), columns, columns, features, features, P(), rows, rows, rows, rows,
        features, rows, rows, rows,
    )
    return jax.shard_map(
        per_device, mesh=mesh, in_specs=in_specs, out_specs=out_specs, check_vma=False
    )
```

```python
from functools import partial

import jax
import jax.numpy as jnp
from jax import lax
from jax.experimental import pallas as pl
from jax.experimental.pallas import tpu as pltpu
from jax.sharding import PartitionSpec as P

D = 768
HEADS = 12
HEAD_DIM = 64
VOCAB = 259
BUCKETS = 32
TABLE = 384
PAIRS = HEADS // 2
SIDE = 128
ONES = 16
LEFT = 20
RIGHT = 21
HALF = 128
KEY_PART = 1024

epsilon = 1e-06
thresholds = (12, 16, 23, 32, 46, 64, 91)
masked_score = -1000000000.0
highest = lax.Precision.HIGHEST
bf16 = jnp.bfloat16
f32 = jnp.float32
both = ("dp", "seq")


def nt(a, b):
    return lax.dot_general(a, b, (((1,), (1,)), ((), ())), preferred_element_type=f32)


def nn(a, b):
    return lax.dot_general(a, b, (((1,), (0,)), ((), ())), preferred_element_type=f32)


def bucket_of(relative):
    distance = jnp.abs(relative)
    far_bucket = 8 + sum(((distance >= border).astype(jnp.int32) for border in thresholds))
    return jnp.where(relative > 0, 16, 0).astype(jnp.int32) + jnp.where(
        distance < 8, distance, far_bucket
    )


def hot_buckets(relative):
    return (bucket_of(relative)[..., None] == jnp.arange(BUCKETS, dtype=jnp.int32)).astype(f32)


def swap(value, axis, bit):
    peers = lax.axis_size(axis)
    return lax.ppermute(value, axis, [(i, i ^ bit) for i in range(peers)])


def axis_bits(axis):
    bits, bit = [], lax.axis_size(axis) // 2
    while bit:
        bits.append((axis, bit))
        bit //= 2
    return bits


def my_bit(axis, bit):
    return (lax.axis_index(axis) // bit) % 2


def gather_stage(value, axis, bit, position):
    other = swap(value, axis, bit)
    upper = my_bit(axis, bit) == 1
    return jnp.stack(
        [jnp.where(upper, other, value), jnp.where(upper, value, other)], axis=position
    )


class RowGather:
    def __init__(self, rows, order):
        self.value = rows
        self.order = list(order)
        self.places = axis_bits("dp") + axis_bits("seq")
        self.done = []
        self.got = None

    def start(self):
        if self.order:
            self.stage = self.order.pop(0)
            self.got = swap(self.value, *self.stage)

    def finish(self, *others):
        if self.got is None:
            return
        got = after(self.got, *others) if others else self.got
        self.got = None
        place = self.places.index(self.stage)
        position = sum(p < place for p in self.done)
        self.done.append(place)
        upper = my_bit(*self.stage) == 1
        self.value = jnp.stack(
            [jnp.where(upper, got, self.value), jnp.where(upper, self.value, got)],
            axis=position,
        )

    def result(self):
        self.finish()
        while self.order:
            self.start()
            self.finish()
        return self.value


def gather_order(first_axis):
    seq, dp = axis_bits("seq"), axis_bits("dp")
    if first_axis == "y":
        return dp + seq
    return dp[:-1] + seq[:-1] + dp[-1:] + seq[-1:]


def after(value, *others):
    return lax.optimization_barrier((value,) + others)[0]


def hold(value, other):
    return value + (other[(0,) * other.ndim] * 0).astype(value.dtype)


def sum_order(first):
    seq, dp = axis_bits("seq")[::-1], axis_bits("dp")[::-1]
    if first == "x":
        return seq + dp
    if first == "y":
        return seq[:1] + dp[:1] + seq[1:] + dp[1:]
    return seq[:1] + dp[1:] + dp[:1] + seq[1:]


class RowSum:
    def __init__(self, total, order):
        self.parts = [total]
        self.left = axis_bits("dp") + axis_bits("seq")
        self.order = list(order)
        self.sent = self.got = None

    def start(self):
        if not self.order:
            return
        axis, bit = self.order.pop(0)
        position = self.left.index((axis, bit))
        self.left.remove((axis, bit))
        mine = my_bit(axis, bit)

        def half(value, which):
            lead, rows, cols = value.shape
            outer = lead << position
            cut = value.reshape(outer, 2, lead * rows // (2 * outer), cols)
            picked = lax.dynamic_index_in_dim(cut, which, 1, keepdims=False)
            return picked.reshape(lead, rows // 2, cols)

        send = sum(half(value, 1 - mine).astype(f32) for value in self.parts)
        self.sent = send.astype(bf16)
        self.parts = [half(value, mine) for value in self.parts]
        self.got = swap(self.sent, axis, bit)

    def finish(self, other=None, hard=False):
        if self.got is not None:
            order = hold if hard else after
            self.parts.append(self.got if other is None else order(self.got, other))
            self.got = None

    def result(self):
        self.finish()
        while self.order:
            self.start()
            self.finish()
        return sum(value.astype(f32) for value in self.parts)


def after_sends(value, *sums):
    sends = [each.sent for each in sums if each.sent is not None]
    return after(value, *sends)


class SumEverywhere:
    def __init__(self, value):
        self.value = value
        self.order = axis_bits("seq")[::-1] + axis_bits("dp")[::-1]
        self.got = None

    def start(self):
        if self.order:
            self.got = swap(self.value, *self.order.pop(0))

    def finish(self, *others):
        if self.got is not None:
            self.value = self.value + (after(self.got, *others) if others else self.got)
            self.got = None

    def result(self):
        self.finish()
        while self.order:
            self.start()
            self.finish()
        return self.value


def pack_kernel(
    rank_ref, lengths_ref, table, taps, scorer, gain_a, gain_f, query, key, value, gate, up, down,
    output, columns, first_half, second_half, packed, rows, *, total_tokens,
):
    shard = table.shape[1]
    live = jnp.int32(0)
    for s in range(lengths_ref.shape[0]):
        live += jnp.minimum((lengths_ref[s] + 1) // 2, total_tokens)
    live = jnp.where(rank_ref[0] == 0, live, 0)
    first = lax.broadcasted_iota(jnp.int32, (1, shard), 1) == 0
    rows[...] = jnp.zeros_like(rows)
    rows[0:VOCAB, 0:shard] = table[...].astype(f32)
    rows[VOCAB : VOCAB + 4, 0:shard] = taps[...].astype(f32)
    for i, vector in enumerate((scorer, gain_a, gain_f)):
        rows[VOCAB + 4 + i : VOCAB + 5 + i, 0:shard] = vector[...].astype(f32)
    for i, part in enumerate((live // 64, live % 64)):
        at = VOCAB + 7 + i
        rows[at : at + 1, 0:shard] = jnp.where(first, part, 0).astype(f32)
    columns[...] = rows[...].T[0:shard, :].astype(bf16)

    pieces = [query[:, i * SIDE : (i + 1) * SIDE] for i in range(PAIRS)]
    for i in range(PAIRS):
        pieces += [key[:, i * SIDE : (i + 1) * SIDE], value[:, i * SIDE : (i + 1) * SIDE]]
    for half in (first_half, second_half):
        count = half.shape[1] // SIDE
        for i in range(count):
            half[:, i * SIDE : (i + 1) * SIDE] = pieces.pop(0)

    ffn_dim = gate.shape[1]
    packed[:, 0:ffn_dim] = gate[...]
    packed[:, ffn_dim : 2 * ffn_dim] = up[...]
    packed[:, 3 * ffn_dim :] = output[...]
    third = D // 3
    wide = down[...].astype(f32)
    for group in range(down.shape[0] // 64):
        for i in range(8):
            at = group * 64 + i * 8
            tiles = [wide[at : at + 8, j * third : (j + 1) * third] for j in range(3)]
            start = 2 * ffn_dim + i * third
            packed[group * 24 : (group + 1) * 24, start : start + third] = jnp.concatenate(
                tiles, axis=0
            ).astype(bf16)


def pack(rank, lengths, table, taps, vectors, attn, feed_weights, total_tokens):
    smem = pl.BlockSpec(memory_space=pltpu.SMEM)
    shard, ffn_dim = table.shape[1], feed_weights[0].shape[1]
    shapes = [(shard, TABLE), (shard, 3 * D // 2), (shard, 3 * D // 2), (shard, 3 * ffn_dim + D)]
    arrays = (table, taps, *vectors, *attn, *feed_weights)

    def whole(shape):
        return pl.BlockSpec(shape, lambda i: (0, 0))

    return pl.pallas_call(
        partial(pack_kernel, total_tokens=total_tokens),
        grid=(1,),
        in_specs=[smem, smem] + [whole(array.shape) for array in arrays],
        out_specs=[whole(shape) for shape in shapes],
        out_shape=[jax.ShapeDtypeStruct(shape, bf16) for shape in shapes],
        scratch_shapes=[pltpu.VMEM((TABLE, -(-shard // 128) * 128), f32)],
        cost_estimate=pl.CostEstimate(flops=100_000_000, bytes_accessed=1_000_000, transcendentals=0),
        name="pack",
    )(rank, lengths, *arrays)


def pack_plain(rank, lengths, table, taps, vectors, attn, feed_weights, total_tokens):
    shard = table.shape[1]
    live = jnp.sum(jnp.minimum((lengths + 1) // 2, total_tokens))
    live = jnp.where(rank[0] == 0, live, 0)
    counts = jnp.stack([live // 64, live % 64])
    at_count = (jnp.arange(shard) == 0).astype(jnp.int32)
    columns = jnp.concatenate(
        [table, taps, *vectors, (counts[:, None] * at_count[None]).astype(bf16)], axis=0
    )
    columns = jnp.pad(columns, ((0, TABLE - columns.shape[0]), (0, 0))).T
    query, key, value = attn
    pairs = jnp.stack([key.reshape(shard, PAIRS, SIDE), value.reshape(shard, PAIRS, SIDE)], axis=2)
    rows = jnp.concatenate([query, pairs.reshape(shard, 2 * D)], axis=1)
    gate, up, down, output = feed_weights
    packed = jnp.concatenate([gate, up, down.reshape(shard, gate.shape[1]), output], axis=1)
    return columns, rows[:, : 3 * D // 2], rows[:, 3 * D // 2 :], packed


def unpack_kernel(packed, gate, up, down, output):
    ffn_dim = gate.shape[1]
    third = D // 3
    value = packed[...].astype(f32)
    gate[...] = value[:, :ffn_dim]
    up[...] = value[:, ffn_dim : 2 * ffn_dim]
    output[...] = value[:, 3 * ffn_dim :]
    for group in range(down.shape[0] // 64):
        for i in range(8):
            at = group * 64 + i * 8
            start = 2 * ffn_dim + i * third
            for j in range(3):
                row = group * 24 + j * 8
                down[at : at + 8, j * third : (j + 1) * third] = value[
                    row : row + 8, start : start + third
                ]


def unpack(packed, ffn_dim, down_rows):
    shard = packed.shape[0]
    shapes = [(shard, ffn_dim), (shard, ffn_dim), (down_rows, D), (shard, D)]

    def whole(shape):
        return pl.BlockSpec(shape, lambda i: (0, 0))

    return pl.pallas_call(
        unpack_kernel,
        grid=(1,),
        in_specs=[whole(packed.shape)],
        out_specs=[whole(shape) for shape in shapes],
        out_shape=[jax.ShapeDtypeStruct(shape, f32) for shape in shapes],
        name="unpack",
    )(packed)


def up(x):
    return pltpu.roll(x, x.shape[0] - 1, 0)


def down(x):
    return pltpu.roll(x, 1, 0)


def ahead_lane(x):
    return pltpu.roll(x, x.shape[1] - 1, 1)


def behind_lane(x):
    return pltpu.roll(x, 1, 1)


def triples(c, m0, m1):
    c0, c1, c2, c3 = c
    p01, p23 = c0 + c1, c2 + c3
    t0, t1, t2, t3 = behind_lane(c3) + p01, p01 + c2, c1 + p23, p23 + ahead_lane(c0)
    before, after = (behind_lane(t3), t0, t1, t2), (t1, t2, t3, ahead_lane(t0))
    here = (t0, t1, t2, t3)
    return tuple(
        jnp.where(m0[k], after[k], jnp.where(m1[k], here[k], before[k])) for k in range(4)
    )


def live_rows(first, rows, total_bytes):
    row = lax.broadcasted_iota(jnp.int32, (rows, 128), 0)
    live = []
    for k in range(4):
        pos = first + 4 * (row - 8) + k
        live.append(((pos >= 0) & (pos < total_bytes)).astype(f32))
    return live


def lane_marks(first, wide, total_bytes):
    row = lax.broadcasted_iota(jnp.int32, (1, wide), 1)
    live, m0, m1 = [], [], []
    for k in range(4):
        pos = first + 4 * (row - 8) + k
        live.append(((pos >= 0) & (pos < total_bytes)).astype(f32))
        shifted = (pos + 48).astype(f32)
        third = jnp.floor((shifted + 0.5) * (1.0 / 3.0))
        rest = shifted - 3.0 * third
        m0.append(rest < 0.5)
        m1.append((rest > 0.5) & (rest < 1.5))
    return live, m0, m1


def to_lanes(accs, count, flat):
    rows = accs.shape[1]
    lane = lax.broadcasted_iota(jnp.int32, (rows, 128), 1)
    value = jnp.zeros((rows, 128), f32)
    for k in range(count):
        value = jnp.where(lane == k, jnp.sum(accs[k], axis=-1, keepdims=True), value)
    flat[0:rows, :] = value
    turned = flat[...].T
    return [turned[k : k + 1, :] for k in range(count)]


def to_rows(lines, lines_ref, accs):
    rows = accs.shape[1]
    for k, line in enumerate(lines):
        lines_ref[k : k + 1, :] = line
    turned = lines_ref[...].T
    for k in range(len(lines)):
        accs[k] = jnp.broadcast_to(turned[0:rows, k : k + 1], (rows, 128))


def lane_chunk(i):
    return pl.ds(pl.multiple_of(i * 128, 128), 128)


def embed_bytes(ids, table, emb):
    lane = lax.broadcasted_iota(jnp.int32, (ids.shape[0], TABLE), 1)
    emb[...] = nt((ids == lane).astype(bf16), table)


def small_rows(table, small):
    lane = lax.broadcasted_iota(jnp.int32, (8, TABLE), 1)
    row = lax.broadcasted_iota(jnp.int32, (8, TABLE), 0)
    small[...] = nt((lane == row + VOCAB).astype(bf16), table)


def block_probs(emb, small, conv, accs, flat, live, m0, m1, rows):
    accs[0:4] = jnp.zeros((4, rows, 128), f32)

    def step(i, _):
        chunk = lane_chunk(i)
        w0, w1, w2, w3 = [small[k : k + 1, chunk] for k in range(4)]
        scorer = small[4:5, chunk]
        e0, e1, e2, e3 = [emb[k * rows : (k + 1) * rows, chunk] for k in range(4)]
        e3d, e0u, e1u = down(e3), up(e0), up(e1)
        c = (
            w0 * e3d + w1 * e0 + w2 * e1 + w3 * e2,
            w0 * e0 + w1 * e1 + w2 * e2 + w3 * e3,
            w0 * e1 + w1 * e2 + w2 * e3 + w3 * e0u,
            w0 * e2 + w1 * e3 + w2 * e0u + w3 * e1u,
        )
        for k in range(4):
            value = c[k] * live[k]
            conv[k, :, chunk] = value
            accs[k] += value * scorer
        return 0

    lax.fori_loop(0, D // 128, step, 0)
    score = to_lanes(accs, 4, flat)
    three = triples(score, m0, m1)
    p01, p23 = score[0] + score[1], score[2] + score[3]
    quad = 0.25 * (p01 + p23)
    probs = []
    for k in range(4):
        scores = (score[k], 0.5 * (p01, p01, p23, p23)[k], three[k] * (1.0 / 3.0), quad)
        top = jnp.maximum(jnp.maximum(scores[0], scores[1]), jnp.maximum(scores[2], scores[3]))
        powers = [jnp.exp(value - top) for value in scores]
        norm = 1.0 / (powers[0] + powers[1] + powers[2] + powers[3])
        probs.append([power * norm for power in powers])
    return probs


def reach(m0, m1, k, ahead):
    one = jnp.ones(m0[k].shape, f32)
    zero = jnp.zeros_like(one)
    if ahead == 0:
        return one
    if ahead == 1:
        return jnp.where(m0[k] | m1[k], one, zero)
    if ahead == 2:
        return jnp.where(m0[k], one, zero)
    if ahead == -1:
        return jnp.where(m0[k], zero, one)
    return jnp.where(m0[k] | m1[k], zero, one)


def token_weights(probs, m0, m1):
    weights = []
    for half in range(2):
        first, second = probs[2 * half], probs[2 * half + 1]
        pair = 0.5 * (first[1] + second[1])
        quad = 0.25 * (first[3] + second[3])
        row = []
        for j in range(6):
            place = 2 * half - 2 + j
            value = jnp.zeros_like(pair)
            for k, p in ((2 * half, first), (2 * half + 1, second)):
                ahead = place - k
                if abs(ahead) <= 2:
                    value += p[2] * (1.0 / 3.0) * reach(m0, m1, k, ahead)
                if ahead == 0:
                    value += p[0]
            if 0 <= place < 4:
                value += quad
            if place // 2 == half:
                value += pair
            row.append(value)
        weights.append(row)
    return weights


def places(c):
    c0, c1, c2, c3 = c
    return ((down(c2), down(c3), c0, c1, c2, c3), (c0, c1, c2, c3, up(c0), up(c1)))


def pool_kernel(first_ref, ids, table, *rest, rows, total_bytes):
    resid, normed, emb, small, conv, accs, flat, lines, tokens = rest[-9:]
    first = first_ref[0]
    embed_bytes(ids[...], table[...], emb)
    small_rows(table[...], small)

    @pl.when(pl.program_id(0) == 0)
    def _():
        flat[...] = jnp.zeros_like(flat)
        lines[...] = jnp.zeros_like(lines)

    _, m0, m1 = lane_marks(first, flat.shape[0], total_bytes)
    live = live_rows(first, rows, total_bytes)
    probs = block_probs(emb, small, conv, accs, flat, live, m0, m1, rows)
    weights = token_weights(probs, m0, m1)
    to_rows([0.5 * weights[half][j] for half in range(2) for j in range(6)], lines, accs)
    own = rows - 16

    def step(i, square):
        chunk = lane_chunk(i)
        around = places([conv[k, :, chunk] for k in range(4)])
        for half in range(2):
            token = accs[6 * half] * around[half][0]
            for j in range(1, 6):
                token += accs[6 * half + j] * around[half][j]
            tokens[i, pl.ds(half, own, stride=2), :] = token[8 : 8 + own]
        values = tokens[i]
        resid[:, chunk] = values
        return square + values * values

    square = lax.fori_loop(0, D // 128, step, jnp.zeros((2 * own, 128), f32))
    scale = lax.rsqrt(jnp.sum(square, axis=-1, keepdims=True) * (1.0 / D) + epsilon)
    normed[...] = (resid[...] * scale * small[5:6, :]).astype(bf16)


def pool(first, ids, table, deps, total_bytes):
    count, wide, _ = ids.shape
    rows = wide // 4
    tokens = 2 * (rows - 16)
    return pl.pallas_call(
        partial(pool_kernel, rows=rows, total_bytes=total_bytes),
        grid=(count,),
        in_specs=[
            pl.BlockSpec(memory_space=pltpu.SMEM),
            pl.BlockSpec((None, wide, 1), lambda i: (i, 0, 0)),
            pl.BlockSpec((D, TABLE), lambda i: (0, 0)),
        ]
        + [pl.BlockSpec(memory_space=pl.ANY)] * len(deps),
        out_specs=[
            pl.BlockSpec((None, tokens, D), lambda i: (i, 0, 0)),
            pl.BlockSpec((None, tokens, D), lambda i: (i, 0, 0)),
        ],
        out_shape=[
            jax.ShapeDtypeStruct((count, tokens, D), f32),
            jax.ShapeDtypeStruct((count, tokens, D), bf16),
        ],
        scratch_shapes=[
            pltpu.VMEM((wide, D), f32),
            pltpu.VMEM((8, D), f32),
            pltpu.VMEM((4, rows, D), f32),
            pltpu.VMEM((12, rows, 128), f32),
            pltpu.VMEM((2 * 128, 128), f32),
            pltpu.VMEM((16, 2 * 128), f32),
            pltpu.VMEM((D // 128, tokens, 128), f32),
        ],
        cost_estimate=pl.CostEstimate(flops=count * 3_000_000_000, bytes_accessed=4_000_000, transcendentals=0),
        name="pool",
    )(first, ids, table, *deps)


def pool_back_kernel(
    first_ref, ids, ids_row, table, pulled_own, from_core, from_x, dq, query_w, resid, after,
    feed_stats, *rest, rows, total_bytes, given, last, deps,
):
    if given:
        embed_before, small_before = rest[:2]
        rest = rest[2:]
    rest = rest[deps:]
    if last:
        turned = rest[0]
        embed_grad, small_grad = rest[-2:]
        rest = rest[1:-2]
    else:
        embed_grad, small_grad = rest[:2]
        rest = rest[2:]
    emb, small, conv, accs, flat, lines, tokens, pulls, emb_grad = rest
    first = first_ref[0]
    own = rows - 16
    chunks = D // 128

    if given:
        small_grad[...] = small_before[...]
    else:
        small_grad[...] = jnp.zeros_like(small_grad)
    flat[...] = jnp.zeros_like(flat)
    lines[...] = jnp.zeros_like(lines)

    embed_bytes(ids[...], table[...], emb)
    small_rows(table[...], small)
    live_lane, m0, m1 = lane_marks(first, flat.shape[0], total_bytes)
    live = live_rows(first, rows, total_bytes)

    x = resid[...]
    gn = pulled_own[...].astype(f32) + from_core[...].astype(f32) + from_x[...].astype(f32)
    gn = gn + nt(dq[...], query_w[...])
    scale = lax.rsqrt(jnp.mean(x * x, axis=-1, keepdims=True) + epsilon)
    gain = small[5:6, :]
    small_grad[5:6, :] += jnp.sum(gn * x * scale, axis=0, keepdims=True)
    gg = gain * gn
    inner = jnp.mean(gg * x, axis=-1, keepdims=True)
    total = after[...] + scale * gg - x * (scale * scale * scale * inner)
    for i in range(chunks):
        tokens[i] = total[:, i * 128 : (i + 1) * 128]

    probs = block_probs(emb, small, conv, accs, flat, live, m0, m1, rows)
    accs[0:12] = jnp.zeros((12, rows, 128), f32)
    pulls[:, 0:8, :] = jnp.zeros((2, 8, D), f32)
    pulls[:, rows - 8 : rows, :] = jnp.zeros((2, 8, D), f32)

    def dots(i, _):
        chunk = lane_chunk(i)
        around = places([conv[k, :, chunk] for k in range(4)])
        for half in range(2):
            pulls[half, 8 : 8 + own, chunk] = 0.5 * tokens[i, pl.ds(half, own, stride=2), :]
            g = pulls[half, :, chunk]
            for j in range(6):
                accs[6 * half + j] += g * around[half][j]
        return 0

    lax.fori_loop(0, chunks, dots, 0)
    every = to_lanes(accs, 12, flat)
    pulled = []
    for half in range(2):
        at = every[6 * half : 6 * half + 6]
        pair = 0.5 * (at[2] + at[3])
        quad = 0.25 * (at[2] + at[3] + (at[4] + at[5] if half == 0 else at[0] + at[1]))
        for k in (2 * half, 2 * half + 1):
            middle = k - (2 * half - 2)
            three = sum(
                at[middle + ahead] * reach(m0, m1, k, ahead)
                for ahead in range(-2, 3)
                if 0 <= middle + ahead < 6
            ) * (1.0 / 3.0)
            gd = (at[middle], pair, three, quad)
            p = probs[k]
            mean = p[0] * gd[0] + p[1] * gd[1] + p[2] * gd[2] + p[3] * gd[3]
            pulled.append([p[b] * (gd[b] - mean) for b in range(4)])

    spread = triples([pulled[k][2] for k in range(4)], m0, m1)
    quad = 0.25 * (pulled[0][3] + pulled[1][3] + pulled[2][3] + pulled[3][3])
    weights = token_weights(probs, m0, m1)
    factors = []
    for k in range(4):
        half = k // 2
        pair = 0.5 * (pulled[2 * half][1] + pulled[2 * half + 1][1])
        factors.append((pulled[k][0] + pair + spread[k] * (1.0 / 3.0) + quad) * live_lane[k])
    at_row = lax.broadcasted_iota(jnp.int32, (1, flat.shape[0]), 1)
    inside = (at_row >= 8) & (at_row < 8 + own)
    even = [jnp.where(inside, weight, 0.0) for weight in weights[0]]
    odd = [jnp.where(inside, weight, 0.0) for weight in weights[1]]
    reached = (
        (behind_lane(odd[4]), even[2], odd[0]),
        (behind_lane(odd[5]), even[3], odd[1]),
        (even[4], odd[2], ahead_lane(even[0])),
        (even[5], odd[3], ahead_lane(even[1])),
    )
    for k in range(4):
        for j in range(3):
            factors.append(reached[k][j] * live_lane[k])
    to_rows(factors, lines, accs)

    def back(i, _):
        chunk = lane_chunk(i)
        w0, w1, w2, w3 = [small[k : k + 1, chunk] for k in range(4)]
        scorer = small[4:5, chunk]
        g0, g1 = pulls[0, :, chunk], pulls[1, :, chunk]
        g1d, g0u = down(g1), up(g0)
        e0, e1, e2, e3 = [emb[k * rows : (k + 1) * rows, chunk] for k in range(4)]
        near = ((g1d, g0, g1), (g1d, g0, g1), (g0, g1, g0u), (g0, g1, g0u))
        score = jnp.zeros((rows, 128), f32)
        gc = []
        for k in range(4):
            score += accs[k] * conv[k, :, chunk]
            value = accs[k] * scorer
            for j in range(3):
                value += accs[4 + 3 * k + j] * near[k][j]
            gc.append(value)
        small_grad[4:5, chunk] += jnp.sum(score, axis=0, keepdims=True)
        gc0, gc1, gc2, gc3 = gc
        e3d, e0u, e1u = down(e3), up(e0), up(e1)
        taps = (
            gc0 * e3d + gc1 * e0 + gc2 * e1 + gc3 * e2,
            gc0 * e0 + gc1 * e1 + gc2 * e2 + gc3 * e3,
            gc0 * e1 + gc1 * e2 + gc2 * e3 + gc3 * e0u,
            gc0 * e2 + gc1 * e3 + gc2 * e0u + gc3 * e1u,
        )
        for k in range(4):
            small_grad[k : k + 1, chunk] += jnp.sum(taps[k], axis=0, keepdims=True)
        gc3d, gc2d, gc0u = down(gc3), down(gc2), up(gc0)
        grads = (
            w0 * gc1 + w1 * gc0 + w2 * gc3d + w3 * gc2d,
            w0 * gc2 + w1 * gc1 + w2 * gc0 + w3 * gc3d,
            w0 * gc3 + w1 * gc2 + w2 * gc1 + w3 * gc0,
            w0 * gc0u + w1 * gc3 + w2 * gc2 + w3 * gc1,
        )
        for k in range(4):
            emb_grad[k * rows : (k + 1) * rows, chunk] = grads[k].astype(bf16)
        return 0

    lax.fori_loop(0, chunks, back, 0)
    row = lax.broadcasted_iota(jnp.int32, (TABLE, 4 * rows), 0)
    total = nn((ids_row[...] == row).astype(bf16), emb_grad[...])
    if given:
        total = total + embed_before[...]
    embed_grad[...] = total
    if last:
        small_grad[6:7, :] = feed_stats[0:1, :]
        embed_grad[VOCAB : VOCAB + 7, :] = small_grad[0:7, :]
        turned[...] = embed_grad[...].T.astype(bf16)


def pool_back(
    seq, first, ids, ids_row, table, pulled, from_core, from_x, dq, qkv, resid, after_grad,
    feed_stats, before, deps, total_bytes,
):
    count, wide, _ = ids.shape
    rows = wide // 4
    tokens = 2 * (rows - 16)
    last = seq == count - 1
    token_spec = pl.BlockSpec((None, tokens, D), lambda i: (seq, 0, 0))
    table_sum = pl.BlockSpec((TABLE, D), lambda i: (0, 0))
    small_sum = pl.BlockSpec((8, D), lambda i: (0, 0))
    sums = [pltpu.VMEM((TABLE, D), f32), pltpu.VMEM((8, D), f32)]
    return pl.pallas_call(
        partial(
            pool_back_kernel, rows=rows, total_bytes=total_bytes, given=bool(before), last=last,
            deps=len(deps),
        ),
        grid=(1,),
        in_specs=[
            pl.BlockSpec(memory_space=pltpu.SMEM),
            pl.BlockSpec((None, wide, 1), lambda i: (seq, 0, 0)),
            pl.BlockSpec((None, 1, wide), lambda i: (seq, 0, 0)),
            pl.BlockSpec((D, TABLE), lambda i: (0, 0)),
            token_spec,
            token_spec,
            pl.BlockSpec((tokens, D), lambda i: (0, 0)),
            token_spec,
            pl.BlockSpec((D, D), lambda i: (0, 0)),
            token_spec,
            token_spec,
            small_sum,
        ]
        + ([table_sum, small_sum] if before else [])
        + [pl.BlockSpec(memory_space=pl.ANY)] * len(deps),
        out_specs=pl.BlockSpec((D, TABLE), lambda i: (0, 0)) if last else [table_sum, small_sum],
        out_shape=jax.ShapeDtypeStruct((D, TABLE), bf16)
        if last
        else [jax.ShapeDtypeStruct((TABLE, D), f32), jax.ShapeDtypeStruct((8, D), f32)],
        scratch_shapes=[
            pltpu.VMEM((wide, D), f32),
            pltpu.VMEM((8, D), f32),
            pltpu.VMEM((4, rows, D), f32),
            pltpu.VMEM((16, rows, 128), f32),
            pltpu.VMEM((2 * 128, 128), f32),
            pltpu.VMEM((16, 2 * 128), f32),
            pltpu.VMEM((D // 128, tokens, 128), f32),
            pltpu.VMEM((2, rows, D), f32),
            pltpu.VMEM((wide, D), bf16),
        ]
        + (sums if last else []),
        cost_estimate=pl.CostEstimate(flops=9_000_000_000, bytes_accessed=8_000_000, transcendentals=0),
        name="pool_back",
    )(
        first, ids, ids_row, table, pulled, from_core, from_x, dq, qkv, resid, after_grad,
        feed_stats, *before, *deps,
    )


def prepare_kernel(
    rank_ref, lengths_ref, bias_ref, lanes_bias, tile, turned, side, diag, *, queries, keys, parts
):
    head = pl.program_id(0)
    rank = rank_ref[0]

    @pl.when(head == 0)
    def _():
        place = lax.broadcasted_iota(jnp.int32, (BUCKETS, 6 * HALF), 1)
        inside = lax.rem(place, 2 * HALF)
        offset = jnp.where(inside < HALF, inside, inside - 2 * HALF)
        relative = (place // (2 * HALF) - 1) * HALF + offset
        bucket = lax.broadcasted_iota(jnp.int32, (BUCKETS, 6 * HALF), 0)
        hot = (bucket_of(relative) == bucket).astype(bf16)
        diag[...] = lax.dot_general(
            lanes_bias[...], hot, (((0,), (0,)), ((), ())), preferred_element_type=f32
        )
        row = lax.broadcasted_iota(jnp.int32, (keys, SIDE), 0)
        lane = lax.broadcasted_iota(jnp.int32, (keys, SIDE), 1)
        at = lax.rem(rank * queries - HALF + row + keys, keys)
        far = row >= queries + 2 * HALF
        right = far & (at > rank * queries)
        left = far & (at <= rank * queries)
        fixed = jnp.where(
            right,
            lanes_bias[31:32, :].astype(f32),
            jnp.where(left, lanes_bias[15:16, :].astype(f32), 0.0),
        )
        fixed = jnp.where((lane >= ONES) & (lane < ONES + 3), 1.0, fixed)
        fixed = jnp.where((lane == LEFT) & left | (lane == RIGHT) & right, 1.0, fixed)
        for s in range(side.shape[0]):
            masked = jnp.where(2 * at < lengths_ref[s], 0.0, masked_score)
            side[s] = jnp.where(lane == 0, masked, fixed).astype(bf16)

    blocks = []
    for index in range(3):
        line = diag[pl.ds(head + 1, 1), index * 2 * HALF : (index + 1) * 2 * HALF]
        full = jnp.broadcast_to(line, (HALF, 2 * HALF))
        blocks.append(pltpu.roll(full, 0, 1, stride=1, stride_axis=0)[:, :HALF])
    turned_blocks = [block.T.astype(bf16) for block in blocks]
    blocks = [block.astype(bf16) for block in blocks]
    behind = jnp.full((HALF, HALF), bias_ref[15, head], f32).astype(bf16)
    ahead = jnp.full((HALF, HALF), bias_ref[31, head], f32).astype(bf16)
    steps = queries // HALF
    for q in range(steps):
        for n in range(steps + 2):
            apart = n - 1 - q
            wrapped = ((n == 0) & (rank == 0), (n == steps + 1) & (rank == parts - 1))
            plain = behind if apart < -1 else ahead if apart > 1 else blocks[apart + 1]
            flipped = behind if apart < -1 else ahead if apart > 1 else turned_blocks[apart + 1]
            if n == 0:
                plain = jnp.where(wrapped[0], ahead, plain)
                flipped = jnp.where(wrapped[0], ahead, flipped)
            if n == steps + 1:
                plain = jnp.where(wrapped[1], behind, plain)
                flipped = jnp.where(wrapped[1], behind, flipped)
            tile[q * HALF : (q + 1) * HALF, n * HALF : (n + 1) * HALF] = plain
            turned[n * HALF : (n + 1) * HALF, q * HALF : (q + 1) * HALF] = flipped


def prepare(rank, lengths, bias, queries, keys, parts):
    near = queries + 2 * HALF
    seqs = lengths.shape[0]
    lanes_bias = jnp.pad(bias, ((0, 0), (1, SIDE - 1 - HEADS)))
    smem = pl.BlockSpec(memory_space=pltpu.SMEM)
    return pl.pallas_call(
        partial(prepare_kernel, queries=queries, keys=keys, parts=parts),
        grid=(HEADS,),
        in_specs=[smem, smem, smem, pl.BlockSpec((BUCKETS, SIDE), lambda i: (0, 0))],
        out_specs=[
            pl.BlockSpec((None, queries, near), lambda i: (i, 0, 0)),
            pl.BlockSpec((None, near, queries), lambda i: (i, 0, 0)),
            pl.BlockSpec((seqs, keys, SIDE), lambda i: (0, 0, 0)),
        ],
        out_shape=[
            jax.ShapeDtypeStruct((HEADS, queries, near), bf16),
            jax.ShapeDtypeStruct((HEADS, near, queries), bf16),
            jax.ShapeDtypeStruct((seqs, keys, SIDE), bf16),
        ],
        scratch_shapes=[pltpu.VMEM((SIDE, 6 * HALF), f32)],
        cost_estimate=pl.CostEstimate(flops=6_000_000_000, bytes_accessed=7_000_000, transcendentals=0),
        name="prepare",
    )(rank, lengths, bias.astype(f32), lanes_bias)


def row_offset(rank, step, blocks):
    half = lax.rem(2 * rank - 1 + step + 2 * blocks, 2 * blocks)
    apart = jnp.bitwise_xor(rank, half // 2)
    slot = (apart % 2) * 2 + apart // 2
    return pl.multiple_of(slot * (2 * HALF) + (half % 2) * HALF, HALF)


def side_lanes(rows, picks):
    lane = lax.broadcasted_iota(jnp.int32, (rows, SIDE), 1)
    value = jnp.zeros((rows, SIDE), f32)
    for index, entry in picks:
        value = jnp.where(lane == index, entry, value)
    return value.astype(bf16)


def three_parts(value):
    high = value.astype(bf16).astype(f32)
    rest = value - high
    middle = rest.astype(bf16).astype(f32)
    return high, middle, rest - middle


def one_head(values, head):
    lane = lax.broadcasted_iota(jnp.int32, values.shape, 1)
    return jnp.where((lane // HEAD_DIM) == head, values, jnp.zeros_like(values))


def attend_kernel(rank_ref, q, kv, side, bias, *rest, near, blocks):
    out, norm, kcat, vcat = rest[-4:]
    rank = rank_ref[0]
    pair = pl.program_id(1)
    queries = q.shape[0]

    @pl.when(pair == 0)
    def _():
        kcat[:, SIDE:] = side[...]
        norm[...] = jnp.zeros_like(norm)

    for step in range(2 * blocks):
        source = pl.ds(row_offset(rank, step, blocks), HALF)
        kcat[step * HALF : (step + 1) * HALF, :SIDE] = kv[source, :SIDE]
        vcat[step * HALF : (step + 1) * HALF, :] = kv[source, SIDE:]

    lane = lax.broadcasted_iota(jnp.int32, (queries, SIDE), 1)
    halves, every = [], []
    for head in range(2):
        extra = side_lanes(queries, [(0, 1.0), (1 + 2 * pair + head, 1.0)])
        wide = jnp.concatenate([one_head(q[...], head), extra], axis=1)
        every.append(nt(wide, kcat[...]))
    for head in range(2):
        logits = every[head]
        close = logits[:, :near] + bias[head].astype(f32)
        away = logits[:, near:]
        top = jnp.maximum(
            jnp.max(close, axis=-1, keepdims=True), jnp.max(away, axis=-1, keepdims=True)
        )
        close = jnp.exp(close - top)
        away = jnp.exp(away - top)
        total = jnp.sum(close, axis=-1, keepdims=True) + jnp.sum(away, axis=-1, keepdims=True)
        mixed = nn(close.astype(bf16), vcat[:near, :]) + nn(away.astype(bf16), vcat[near:, :])
        halves.append(mixed * (1.0 / total))
        norm[...] = jnp.where(lane == 2 * pair + head, top + jnp.log(total), norm[...])
    out[...] = jnp.where(lane < HEAD_DIM, halves[0], halves[1]).astype(bf16)


def attend(rank, q, kv, side, bias, deps):
    seqs, queries, _ = q.shape
    keys = kv.shape[1]
    near = bias.shape[-1]
    blocks = keys // queries
    return pl.pallas_call(
        partial(attend_kernel, near=near, blocks=blocks),
        grid=(seqs, PAIRS),
        in_specs=[
            pl.BlockSpec(memory_space=pltpu.SMEM),
            pl.BlockSpec((None, queries, SIDE), lambda s, i: (s, 0, i)),
            pl.BlockSpec((None, keys, 2 * SIDE), lambda s, i: (s, 0, i)),
            pl.BlockSpec((None, keys, SIDE), lambda s, i: (s, 0, 0)),
            pl.BlockSpec((2, queries, near), lambda s, i: (i, 0, 0)),
        ]
        + [pl.BlockSpec(memory_space=pl.ANY)] * len(deps),
        out_specs=[
            pl.BlockSpec((None, queries, SIDE), lambda s, i: (s, 0, i)),
            pl.BlockSpec((None, queries, SIDE), lambda s, i: (s, 0, 0)),
        ],
        out_shape=[
            jax.ShapeDtypeStruct((seqs, queries, D), bf16),
            jax.ShapeDtypeStruct((seqs, queries, SIDE), f32),
        ],
        scratch_shapes=[pltpu.VMEM((keys, 2 * SIDE), bf16), pltpu.VMEM((keys, SIDE), bf16)],
        cost_estimate=pl.CostEstimate(flops=25_000_000_000, bytes_accessed=8_000_000, transcendentals=0),
        name="attend",
    )(rank, q, kv, side, bias, *deps)


def attend_back_kernel(
    rank_ref, q, kv, side, bias, norm, mixed, grad, dq, dkv, dnear, dfar, kcat, vcat, kturn, *,
    near, blocks, part,
):
    rank = rank_ref[0]
    pair = pl.program_id(1)
    queries = q.shape[0]
    keys = kv.shape[0]

    @pl.when(pair == 0)
    def _():
        kcat[:, SIDE:] = side[...]
        vcat[:, SIDE:] = side[...]
        kturn[SIDE:, :] = side[...].astype(f32).T[ONES : 2 * ONES, :].astype(bf16)

    for step in range(2 * blocks):
        source = pl.ds(row_offset(rank, step, blocks), HALF)
        kcat[step * HALF : (step + 1) * HALF, :SIDE] = kv[source, :SIDE]
        vcat[step * HALF : (step + 1) * HALF, :SIDE] = kv[source, SIDE:]
    kturn[:SIDE, :] = kcat[:, :SIDE].astype(f32).T.astype(bf16)

    lane = lax.broadcasted_iota(jnp.int32, (queries, SIDE), 1)
    queries_of, grads_of, wide_q, wide_g = [], [], [], []
    products = grad[...].astype(f32) * mixed[...].astype(f32)
    for head in range(2):
        index = 2 * pair + head
        level = jnp.sum(jnp.where(lane == index, norm[...], 0.0), axis=-1, keepdims=True)
        delta = jnp.sum(
            jnp.where((lane // HEAD_DIM) == head, products, 0.0), axis=-1, keepdims=True
        )
        la, lb, lc = three_parts(-level)
        da, db, dc = three_parts(-delta)
        queries_of.append(one_head(q[...], head))
        grads_of.append(one_head(grad[...], head))
        extra = [(0, 1.0), (1 + index, 1.0), (ONES, la), (ONES + 1, lb), (ONES + 2, lc)]
        wide_q.append(jnp.concatenate([queries_of[head], side_lanes(queries, extra)], axis=1))
        extra = [(ONES, da), (ONES + 1, db), (ONES + 2, dc)]
        wide_g.append(jnp.concatenate([grads_of[head], side_lanes(queries, extra)], axis=1))

    sums = [jnp.zeros((kturn.shape[0], queries), f32) for _ in range(2)]
    for base in range(0, keys, part):
        span = slice(base, base + part)
        value_part = jnp.zeros((part, SIDE), f32)
        key_part = jnp.zeros((part, SIDE), f32)
        for head in range(2):
            logits = nt(kcat[span, :], wide_q[head])
            if base < near:
                here = min(near, base + part) - base
                close = logits[:here] + bias[head, base : base + here, :].astype(f32)
                logits = close if here == part else jnp.concatenate([close, logits[here:]], axis=0)
            probs = jnp.exp(logits)
            pull = nt(vcat[span, :], wide_g[head])
            low = (probs * pull).astype(bf16)
            value_part += nn(probs.astype(bf16), grads_of[head])
            key_part += nn(low, queries_of[head])
            sums[head] += nn(kturn[:, span], low)
            if base < near:
                here = min(near, base + part) - base
                dnear[head, base : base + here, :] = low[:here]
        for step in range(base // HALF, (base + part) // HALF):
            target = pl.ds(row_offset(rank, step, blocks), HALF)
            inner = slice(step * HALF - base, (step + 1) * HALF - base)
            dkv[target, :SIDE] = key_part[inner].astype(bf16)
            dkv[target, SIDE:] = value_part[inner].astype(bf16)
    turned = jnp.concatenate([sums[0][:HEAD_DIM], sums[1][HEAD_DIM:SIDE]], axis=0)
    dq[...] = turned.T.astype(bf16)
    for head in range(2):
        dfar[head] = sums[head][SIDE:, :]


def attend_back(rank, q, kv, side, bias, norm, mixed, grad):
    seqs, queries, _ = q.shape
    keys = kv.shape[1]
    near = bias.shape[1]
    blocks = keys // queries
    own = pl.BlockSpec((None, queries, SIDE), lambda s, i: (s, 0, i))
    every = pl.BlockSpec((None, keys, 2 * SIDE), lambda s, i: (s, 0, i))
    return pl.pallas_call(
        partial(attend_back_kernel, near=near, blocks=blocks, part=KEY_PART),
        grid=(seqs, PAIRS),
        in_specs=[
            pl.BlockSpec(memory_space=pltpu.SMEM),
            own,
            every,
            pl.BlockSpec((None, keys, SIDE), lambda s, i: (s, 0, 0)),
            pl.BlockSpec((2, near, queries), lambda s, i: (i, 0, 0)),
            pl.BlockSpec((None, queries, SIDE), lambda s, i: (s, 0, 0)),
            own,
            own,
        ],
        out_specs=[
            own,
            every,
            pl.BlockSpec((None, 2, near, queries), lambda s, i: (s, i, 0, 0)),
            pl.BlockSpec((None, 2, ONES, queries), lambda s, i: (s, i, 0, 0)),
        ],
        out_shape=[
            jax.ShapeDtypeStruct((seqs, queries, D), bf16),
            jax.ShapeDtypeStruct((seqs, keys, 2 * D), bf16),
            jax.ShapeDtypeStruct((seqs, HEADS, near, queries), bf16),
            jax.ShapeDtypeStruct((seqs, HEADS, ONES, queries), f32),
        ],
        scratch_shapes=[
            pltpu.VMEM((keys, 2 * SIDE), bf16),
            pltpu.VMEM((keys, 2 * SIDE), bf16),
            pltpu.VMEM((SIDE + ONES, keys), bf16),
        ],
        cost_estimate=pl.CostEstimate(flops=40_000_000_000, bytes_accessed=12_000_000, transcendentals=0),
        name="attend_back",
    )(rank, q, kv, side, bias, norm, mixed, grad)


def bias_grad_kernel(rank_ref, near, far, *rest, parts):
    out, lines = rest[-2:]
    rank = rank_ref[0]
    head = pl.program_id(0)
    seqs = near.shape[0]
    steps = near.shape[1] // HALF - 2
    first_in, last_in = rank != 0, rank != parts - 1

    def block(n, q):
        rows, cols = slice(n * HALF, (n + 1) * HALF), slice(q * HALF, (q + 1) * HALF)
        return sum(near[s, rows, cols].astype(f32) for s in range(seqs))

    sums = [jnp.zeros((HALF, HALF), f32) for _ in range(3)]
    left = sum(far[s, LEFT - ONES : LEFT - ONES + 1, :] for s in range(seqs))
    right = sum(far[s, RIGHT - ONES : RIGHT - ONES + 1, :] for s in range(seqs))
    left = [left[:, q * HALF : (q + 1) * HALF] for q in range(steps)]
    right = [right[:, q * HALF : (q + 1) * HALF] for q in range(steps)]
    for n in range(steps + 2):
        inside = first_in if n == 0 else last_in if n == steps + 1 else None
        for q in range(steps):
            value = block(n, q)
            apart = n - 1 - q
            if inside is not None:
                column = jnp.sum(value, axis=0, keepdims=True)
                outer = jnp.where(inside, 0.0, column)
                if n == 0:
                    right[q] += outer
                else:
                    left[q] += outer
                kept = jnp.where(inside, column, 0.0)
                if apart < -1:
                    left[q] += kept
                elif apart > 1:
                    right[q] += kept
                value = jnp.where(inside, value, 0.0)
            if abs(apart) <= 1:
                sums[apart + 1] += value
    found = []
    for value in sums:
        wide = jnp.concatenate([value, jnp.zeros((HALF, HALF), f32)], axis=1)
        folded = wide[0:8, :]
        for a in range(8, HALF, 8):
            folded += pltpu.roll(wide[a : a + 8, :], 2 * HALF - a, 1)
        line = folded[0:1, :]
        for b in range(1, 8):
            line += pltpu.roll(folded[b : b + 1, :], 2 * HALF - b, 1)
        found.append(line)
    found += [jnp.concatenate(left, axis=1), jnp.concatenate(right, axis=1)]
    lines[pl.ds(head, 1), :] = jnp.concatenate(found, axis=1)

    @pl.when(head == pl.num_programs(0) - 1)
    def _():
        shape = (10 * HALF, 128)
        place = lax.broadcasted_iota(jnp.int32, shape, 0)
        lane = lax.broadcasted_iota(jnp.int32, shape, 1)
        segment, inner = place // (2 * HALF), lax.rem(place, 2 * HALF)
        behind = jnp.where(inner < HALF, inner, inner - 2 * HALF)
        relative = (segment - 1) * HALF - behind
        bucket = jnp.where(segment == 3, 15, jnp.where(segment == 4, 31, bucket_of(relative)))
        hot = (bucket == lane).astype(bf16)
        split = jnp.concatenate([part.astype(bf16) for part in three_parts(lines[...])], axis=0)
        total = nn(split, hot)
        rows = lines.shape[0]
        out[...] = total[:rows] + total[rows : 2 * rows] + total[2 * rows :]


def bias_sums(rank, near_parts, far_parts, parts, deps):
    seqs, heads, near, queries = near_parts.shape
    assert queries == 2 * HALF
    return pl.pallas_call(
        partial(bias_grad_kernel, parts=parts),
        grid=(heads,),
        in_specs=[
            pl.BlockSpec(memory_space=pltpu.SMEM),
            pl.BlockSpec((seqs, None, near, queries), lambda i: (0, i, 0, 0)),
            pl.BlockSpec((seqs, None, ONES, queries), lambda i: (0, i, 0, 0)),
        ]
        + [pl.BlockSpec(memory_space=pl.ANY)] * len(deps),
        out_specs=pl.BlockSpec((16, 128), lambda i: (0, 0)),
        out_shape=jax.ShapeDtypeStruct((16, 128), f32),
        scratch_shapes=[pltpu.VMEM((16, 10 * HALF), f32)],
        cost_estimate=pl.CostEstimate(flops=6_000_000_000, bytes_accessed=9_000_000, transcendentals=0),
        name="bias_sums",
    )(rank, near_parts, far_parts, *deps)


def gelu_parts(x):
    inner = 0.7978845608028654 * (x + 0.044715 * (x * x * x))
    t = jnp.tanh(inner)
    half = 0.5 * (1.0 + t)
    slope = half + 0.5 * x * (1.0 - t * t) * (
        0.7978845608028654 * (1.0 + 0.134145 * (x * x))
    )
    return x * half, slope


def feed_kernel(
    place_ref, count_ref, lengths_ref, att, resid, teacher, gain, wide_hbm, down_hbm,
    block_out, normed, hidden, branch, gate_low, up_low, after_grad, after_low, att_grad, stats,
    act, steep, gate_w, up_w, down_w, output_w, sems, *, chunk,
):
    step = pl.program_id(0)
    rows = att.shape[0]
    ffn_dim = gate_w.shape[1]
    copies = [
        pltpu.make_async_copy(wide_hbm.at[:, 3 * ffn_dim : 3 * ffn_dim + D], output_w, sems.at[0]),
        pltpu.make_async_copy(wide_hbm.at[:, 0:ffn_dim], gate_w, sems.at[1]),
        pltpu.make_async_copy(wide_hbm.at[:, ffn_dim : 2 * ffn_dim], up_w, sems.at[2]),
        pltpu.make_async_copy(down_hbm, down_w, sems.at[3]),
    ]

    @pl.when(step == 0)
    def _():
        for copy in copies:
            copy.start()

    def arrived(index):
        @pl.when(step == 0)
        def _():
            copies[index].wait()

    @pl.when(step == 0)
    def _():
        stats[...] = jnp.zeros_like(stats)

    arrived(0)
    after = resid[...] + nn(att[...], output_w[...])
    scale = lax.rsqrt(jnp.mean(after * after, axis=-1, keepdims=True) + epsilon)
    normed[...] = (after * scale * gain[...]).astype(bf16)
    arrived(1)
    arrived(2)
    arrived(3)
    out = after
    for base in range(0, ffn_dim, chunk):
        span = slice(base, base + chunk)
        gate = nn(normed[...], gate_w[:, span])
        up_part = nn(normed[...], up_w[:, span])
        value, slope = gelu_parts(gate)
        act[:, span] = value
        steep[:, span] = slope * up_part
        low = (value * up_part).astype(bf16)
        hidden[:, span] = low
        out = out + nn(low, down_w[span, :])
    block_out[...] = out
    token = place_ref[0] + lax.broadcasted_iota(jnp.int32, (rows, D), 0)
    live = (2 * token < lengths_ref[step]).astype(f32)
    error = live * (out - teacher[...])
    stats[1:2, :] += jnp.sum(error * error, axis=0, keepdims=True)
    out_grad = (2.0 / count_ref[0]) * error
    branch[...] = out_grad.astype(bf16)
    back = jnp.zeros((rows, D), f32)
    for base in range(0, ffn_dim, chunk):
        span = slice(base, base + chunk)
        pull = nt(branch[...], down_w[span, :])
        gate_part = (pull * steep[:, span]).astype(bf16)
        up_part = (pull * act[:, span]).astype(bf16)
        gate_low[:, span] = gate_part
        up_low[:, span] = up_part
        back = back + nt(gate_part, gate_w[:, span]) + nt(up_part, up_w[:, span])
    stats[0:1, :] += jnp.sum(back * after * scale, axis=0, keepdims=True)
    gained = back * gain[...]
    inner = jnp.mean(gained * after, axis=-1, keepdims=True)
    total = out_grad + scale * gained - after * (scale * scale * scale * inner)
    after_grad[...] = total
    low = total.astype(bf16)
    after_low[...] = low
    att_grad[...] = nt(low, output_w[...]).astype(bf16)


def feed(place, count, lengths, att, resid, teacher, gain, wide, down_w):
    tokens = att.shape[0]
    seqs = lengths.shape[0]
    rows = tokens // seqs
    ffn_dim = down_w.shape[0]
    own = pl.BlockSpec((rows, D), lambda i: (i, 0))
    broad = pl.BlockSpec((rows, ffn_dim), lambda i: (i, 0))
    smem = pl.BlockSpec(memory_space=pltpu.SMEM)
    return pl.pallas_call(
        partial(feed_kernel, chunk=512),
        grid=(seqs,),
        in_specs=[
            smem,
            smem,
            smem,
            own,
            pl.BlockSpec((None, rows, D), lambda i: (i, 0, 0)),
            own,
            pl.BlockSpec((1, D), lambda i: (0, 0)),
            pl.BlockSpec(memory_space=pl.ANY),
            pl.BlockSpec(memory_space=pl.ANY),
        ],
        out_specs=[own, own, broad, own, broad, broad, own, own, own, pl.BlockSpec((8, D), lambda i: (0, 0))],
        out_shape=[
            jax.ShapeDtypeStruct((tokens, D), f32),
            jax.ShapeDtypeStruct((tokens, D), bf16),
            jax.ShapeDtypeStruct((tokens, ffn_dim), bf16),
            jax.ShapeDtypeStruct((tokens, D), bf16),
            jax.ShapeDtypeStruct((tokens, ffn_dim), bf16),
            jax.ShapeDtypeStruct((tokens, ffn_dim), bf16),
            jax.ShapeDtypeStruct((tokens, D), f32),
            jax.ShapeDtypeStruct((tokens, D), bf16),
            jax.ShapeDtypeStruct((tokens, D), bf16),
            jax.ShapeDtypeStruct((8, D), f32),
        ],
        scratch_shapes=[
            pltpu.VMEM((rows, ffn_dim), f32),
            pltpu.VMEM((rows, ffn_dim), f32),
            pltpu.VMEM((D, ffn_dim), bf16),
            pltpu.VMEM((D, ffn_dim), bf16),
            pltpu.VMEM((ffn_dim, D), bf16),
            pltpu.VMEM((D, D), bf16),
            pltpu.SemaphoreType.DMA((4,)),
        ],
        cost_estimate=pl.CostEstimate(flops=17_000_000_000, bytes_accessed=30_000_000, transcendentals=0),
        name="feed",
    )(place, count, lengths, att, resid, teacher, gain, wide, down_w)


def dot(a, b):
    return jnp.dot(a, b, preferred_element_type=f32)


def per_device(
    byte_ids,
    lengths,
    teacher,
    embed_table,
    conv_weight,
    score_weight,
    attn_gain,
    rel_bias,
    query_weight,
    key_weight,
    value_weight,
    output_weight,
    ffn_gain,
    gate_weight,
    up_weight,
    down_weight,
):
    seqs, own_bytes = byte_ids.shape
    own = own_bytes // 2
    parts = lax.axis_size("seq")
    dp_size = lax.axis_size("dp")
    rank = lax.axis_index("seq")
    total_tokens, total_bytes = own * parts, own_bytes * parts
    shard = score_weight.shape[0]
    rank_ref = rank.reshape(1).astype(jnp.int32)

    tiled = down_weight.shape[0] % 64 == 0
    third = D // 3
    columns, *attn_halves, packed = (pack if tiled else pack_plain)(
        rank_ref, lengths, embed_table, conv_weight,
        (score_weight[None], attn_gain[None], ffn_gain[None]),
        (query_weight, key_weight, value_weight),
        (gate_weight, up_weight, down_weight, output_weight), total_tokens,
    )
    ids_low = jnp.stack([byte_ids // 16, byte_ids % 16]).astype(bf16)
    id_rows = ids_low.reshape(-1, TABLE)
    cut = attn_halves[0].shape[1]
    qkv_halves = [
        RowGather(attn_halves[0], gather_order("y")),
        RowGather(attn_halves[1], gather_order("x")),
    ]
    small = RowGather(columns, axis_bits("dp"))
    while small.order:
        small.start()
        for each in qkv_halves:
            each.finish()
            if len(each.order) > 3:
                each.start()
        small.finish()
    value = small.value.reshape(-1, TABLE)
    mine = jnp.concatenate([value, id_rows], axis=0)
    x_other = swap(mine, "seq", 2)
    pair = jnp.concatenate([mine, x_other], axis=0)
    c_other = swap(pair, "seq", 1)
    wide_rows = mine.shape[0]
    quarters = jnp.concatenate([pair, c_other], axis=0).reshape(parts, wide_rows, TABLE)
    apart = jnp.bitwise_xor(rank, jnp.arange(parts))
    slots = (apart % 2) * 2 + apart // 2
    ordered = jnp.take(quarters, slots, axis=0)
    table = (
        ordered[:, : dp_size * shard]
        .reshape(parts, dp_size, shard, TABLE)
        .transpose(1, 0, 2, 3)
        .reshape(D, TABLE)
    )
    all_ids = ordered[:, dp_size * shard :].reshape(parts, 2, seqs, own_bytes).astype(jnp.int32)
    all_ids = (all_ids[:, 0] * 16 + all_ids[:, 1]).transpose(1, 0, 2).reshape(seqs, total_bytes)
    counts = jnp.sum(table[:, VOCAB + 7 : VOCAB + 9].astype(f32), axis=0)
    live_count = counts[0] * 64.0 + counts[1]
    ffn_gain_full = table[:, VOCAB + 6].astype(f32)

    padded_ids = jnp.pad(all_ids, ((0, 0), (32, 32)), constant_values=-1)
    first_byte = (rank * own_bytes).astype(jnp.int32)
    first_other = (jnp.bitwise_xor(rank, 2) * own_bytes).astype(jnp.int32)

    def phases(start):
        window = lax.dynamic_slice_in_dim(padded_ids, start, own_bytes + 64, 1)
        return window.reshape(seqs, -1, 4).transpose(0, 2, 1).reshape(seqs, -1)

    phase_ids = phases(first_byte)
    other_ids = phases(first_other)

    ffn_dim = gate_weight.shape[1]
    ffn_dim = gate_weight.shape[1]
    wide_full = lax.all_gather(packed, both, axis=0, tiled=True)
    down_full = wide_full[:, 2 * ffn_dim : 3 * ffn_dim]
    if tiled:
        down_full = down_full.reshape(-1, 3, 8, 8, third).transpose(0, 3, 2, 1, 4)
    down_full = down_full.reshape(ffn_dim, D)

    for each in qkv_halves:
        each.start()
    tile, turned_tile, side = prepare(
        after(rank_ref, table), lengths, rel_bias, own, total_tokens, parts
    )
    for each in qkv_halves:
        each.finish(tile)
        each.start()
    residual, normed_own = pool(
        first_byte.reshape(1), phase_ids[:, :, None], table,
        [tile] + [each.value for each in qkv_halves], total_bytes,
    )
    own_other = swap(normed_own, "seq", 1)
    for each in qkv_halves:
        each.finish(normed_own)
        each.start()
    _, normed_x = pool(
        first_other.reshape(1), other_ids[:, :, None], table,
        [normed_own] + [each.value for each in qkv_halves], total_bytes,
    )
    x_side = swap(normed_x, "seq", 1)
    for each in qkv_halves:
        each.finish(normed_x)
    halves = [each.result().reshape(D, cut) for each in qkv_halves]
    qkv_full = jnp.concatenate(halves, axis=1)
    query_full, kv_full = qkv_full[:, :D], qkv_full[:, D:]
    normed = jnp.concatenate([normed_own, normed_x, own_other, x_side], axis=1)
    own_rows = normed_own.reshape(-1, D)
    queries = dot(own_rows, query_full).astype(bf16).reshape(seqs, own, D)
    pairs_kv = dot(normed.reshape(-1, D), kv_full).astype(bf16).reshape(seqs, total_tokens, 2 * D)
    attended, norms = attend(rank_ref, queries, pairs_kv, side, tile, [])

    token_rows = seqs * own
    att = attended.reshape(token_rows, D)
    (
        block_out, ffn_in, hidden, branch_grad, gate_low, up_low, after_grad, after_low,
        attended_grad, feed_stats,
    ) = feed(
        (rank * own).reshape(1), live_count.reshape(1), lengths, att,
        residual, teacher.reshape(token_rows, D), ffn_gain_full[None],
        wide_full, down_full,
    )
    down_grad = jnp.einsum("tf,td->fd", hidden, branch_grad, preferred_element_type=f32)
    gate_grad = jnp.einsum("td,tf->df", ffn_in, gate_low, preferred_element_type=f32)
    up_grad = jnp.einsum("td,tf->df", ffn_in, up_low, preferred_element_type=f32)
    output_grad = jnp.einsum("td,te->de", att, after_low, preferred_element_type=f32).astype(bf16)
    down_grad = down_grad.astype(bf16)
    if tiled:
        down_grad = down_grad.reshape(-1, 8, 8, 3, third).transpose(0, 3, 2, 1, 4)
    wide_grad = jnp.concatenate(
        [
            gate_grad.astype(bf16),
            up_grad.astype(bf16),
            down_grad.reshape(D, ffn_dim),
            output_grad,
        ],
        axis=1,
    )
    wide_sum = lax.psum_scatter(wide_grad, both, scatter_dimension=0, tiled=True)
    turn = after(attended_grad, wide_grad).reshape(seqs, own, D)
    dq, dkv, near_parts, far_parts = attend_back(
        rank_ref, queries, pairs_kv, side, turned_tile, norms, attended, turn
    )
    dq_rows, dkv_rows = dq.reshape(-1, D), dkv.reshape(-1, 2 * D)
    pulled = jnp.einsum("te,de->td", dkv_rows, kv_full, preferred_element_type=f32)
    pulled = pulled.astype(bf16).reshape(seqs, total_tokens, D)
    to_core = pulled[:, 2 * own :]
    from_core = swap(to_core, "seq", 1)
    query_grad = jnp.einsum(
        "td,te->de", own_rows, after(dq_rows, to_core), preferred_element_type=f32
    ).astype(bf16)
    from_core = after(from_core, query_grad)
    to_x = [
        (pulled[s, own : 2 * own].astype(f32) + from_core[s, own:].astype(f32)).astype(bf16)
        for s in range(seqs)
    ]
    from_x = [swap(rows, "seq", 2) for rows in to_x]
    normed_rows = normed.reshape(-1, D)
    kv_grad = jnp.einsum(
        "td,te->de", normed_rows, after(dkv_rows, *to_x), preferred_element_type=f32
    ).astype(bf16)
    attn_sum = RowSum(jnp.concatenate([query_grad, kv_grad], axis=1)[None], sum_order("y"))
    attn_sum.start()
    attn_sum.finish()
    attn_sum.start()
    bias_rows = bias_sums(rank_ref, near_parts, far_parts, parts, [attn_sum.sent])
    shared = SumEverywhere(
        jnp.where(
            (jnp.arange(16) < HEADS)[:, None],
            bias_rows,
            jnp.broadcast_to(jnp.sum(feed_stats[1]), (16, 128)),
        )
    )
    shared.start()
    sums, deps = (), [bias_rows]
    for s in range(seqs):
        sums = pool_back(
            s, first_byte.reshape(1), phase_ids[:, :, None], phase_ids[:, None, :], table,
            pulled, from_core, from_x[s], dq, halves[0], residual,
            after_grad.reshape(seqs, own, D), feed_stats, sums, deps, total_bytes,
        )
        if s < seqs - 1:
            shared.finish(sums[1])
            shared.start()
            deps = [shared.value]
        if s < seqs - 1:
            attn_sum.finish(sums[1])
            attn_sum.start()
            deps.append(attn_sum.sent)
    shared.finish(sums)
    shared.start()
    front_sum = RowSum(sums[None], sum_order("x"))
    while front_sum.order:
        front_sum.start()
        for each in (attn_sum, shared):
            each.finish()
            each.start()
        front_sum.finish()
    front_sum = front_sum.result().reshape(shard, TABLE).T
    every = shared.result()
    bias_grad = every[:HEADS, :BUCKETS].T
    attn_sum = attn_sum.result()[0]
    kv_sum = attn_sum[:, D : 3 * D].reshape(shard, PAIRS, 2, SIDE)
    if tiled:
        gate_sum, up_sum, down_sum, output_sum = unpack(wide_sum, ffn_dim, down_weight.shape[0])
    else:
        wide_sum = wide_sum.astype(f32)
        gate_sum, up_sum = wide_sum[:, :ffn_dim], wide_sum[:, ffn_dim : 2 * ffn_dim]
        down_sum = wide_sum[:, 2 * ffn_dim : 3 * ffn_dim].reshape(-1, D)
        output_sum = wide_sum[:, 3 * ffn_dim :]

    return (
        block_out.reshape(seqs, own, D),
        every[HEADS, 0] / live_count,
        front_sum[:VOCAB],
        front_sum[VOCAB : VOCAB + 4],
        front_sum[VOCAB + 4],
        front_sum[VOCAB + 5],
        bias_grad,
        attn_sum[:, :D],
        kv_sum[:, :, 0].reshape(shard, D),
        kv_sum[:, :, 1].reshape(shard, D),
        output_sum,
        front_sum[VOCAB + 6],
        gate_sum,
        up_sum,
        down_sum,
    )


def solution(mesh):
    tokens = P("dp", "seq", None)
    features = P(("dp", "seq"))
    columns = P(None, ("dp", "seq"))
    rows = P(("dp", "seq"), None)
    in_specs = (
        P("dp", "seq"), P("dp"), tokens, columns, columns, features, features, P(),
        rows, rows, rows, rows, features, rows, rows, rows,
    )
    out_specs = (
        tokens, P(), columns, columns, features, features, P(), rows, rows, rows, rows,
        features, rows, rows, rows,
    )
    return jax.shard_map(
        per_device, mesh=mesh, in_specs=in_specs, out_specs=out_specs, check_vma=False
    )
```

```python
from functools import partial

import jax
import jax.numpy as jnp
from jax import lax
from jax.experimental import pallas as pl
from jax.experimental.pallas import tpu as pltpu
from jax.sharding import PartitionSpec as P

D = 768
HEADS = 12
HEAD_DIM = 64
VOCAB = 259
BUCKETS = 32
TABLE = 384
PAIRS = HEADS // 2
SIDE = 128
ONES = 16
LEFT = 20
RIGHT = 21
HALF = 128
KEY_PART = 1024

epsilon = 1e-06
thresholds = (12, 16, 23, 32, 46, 64, 91)
masked_score = -1000000000.0
highest = lax.Precision.HIGHEST
bf16 = jnp.bfloat16
f32 = jnp.float32
both = ("dp", "seq")


def nt(a, b):
    return lax.dot_general(a, b, (((1,), (1,)), ((), ())), preferred_element_type=f32)


def nn(a, b):
    return lax.dot_general(a, b, (((1,), (0,)), ((), ())), preferred_element_type=f32)


def bucket_of(relative):
    distance = jnp.abs(relative)
    far_bucket = 8 + sum(((distance >= border).astype(jnp.int32) for border in thresholds))
    return jnp.where(relative > 0, 16, 0).astype(jnp.int32) + jnp.where(
        distance < 8, distance, far_bucket
    )


def hot_buckets(relative):
    return (bucket_of(relative)[..., None] == jnp.arange(BUCKETS, dtype=jnp.int32)).astype(f32)


def swap(value, axis, bit):
    peers = lax.axis_size(axis)
    return lax.ppermute(value, axis, [(i, i ^ bit) for i in range(peers)])


def axis_bits(axis):
    bits, bit = [], lax.axis_size(axis) // 2
    while bit:
        bits.append((axis, bit))
        bit //= 2
    return bits


def my_bit(axis, bit):
    return (lax.axis_index(axis) // bit) % 2


def gather_stage(value, axis, bit, position):
    other = swap(value, axis, bit)
    upper = my_bit(axis, bit) == 1
    return jnp.stack(
        [jnp.where(upper, other, value), jnp.where(upper, value, other)], axis=position
    )


class RowGather:
    def __init__(self, rows, order):
        self.value = rows
        self.order = list(order)
        self.places = axis_bits("dp") + axis_bits("seq")
        self.done = []
        self.got = None

    def start(self):
        if self.order:
            self.stage = self.order.pop(0)
            self.got = swap(self.value, *self.stage)

    def finish(self, *others):
        if self.got is None:
            return
        got = after(self.got, *others) if others else self.got
        self.got = None
        place = self.places.index(self.stage)
        position = sum(p < place for p in self.done)
        self.done.append(place)
        upper = my_bit(*self.stage) == 1
        self.value = jnp.stack(
            [jnp.where(upper, got, self.value), jnp.where(upper, self.value, got)],
            axis=position,
        )

    def result(self):
        self.finish()
        while self.order:
            self.start()
            self.finish()
        return self.value


def gather_order(first_axis):
    seq, dp = axis_bits("seq"), axis_bits("dp")
    if first_axis == "y":
        return dp + seq
    return dp[:-1] + seq[:-1] + dp[-1:] + seq[-1:]


def after(value, *others):
    return lax.optimization_barrier((value,) + others)[0]


def hold(value, other):
    return value + (other[(0,) * other.ndim] * 0).astype(value.dtype)


def sum_order(first):
    seq, dp = axis_bits("seq")[::-1], axis_bits("dp")[::-1]
    if first == "x":
        return seq + dp
    if first == "y":
        return seq[:1] + dp[:1] + seq[1:] + dp[1:]
    return seq[:1] + dp[1:] + dp[:1] + seq[1:]


class RowSum:
    def __init__(self, total, order):
        self.parts = [total]
        self.left = axis_bits("dp") + axis_bits("seq")
        self.order = list(order)
        self.sent = self.got = None

    def start(self):
        if not self.order:
            return
        axis, bit = self.order.pop(0)
        position = self.left.index((axis, bit))
        self.left.remove((axis, bit))
        mine = my_bit(axis, bit)

        def half(value, which):
            lead, rows, cols = value.shape
            outer = lead << position
            cut = value.reshape(outer, 2, lead * rows // (2 * outer), cols)
            picked = lax.dynamic_index_in_dim(cut, which, 1, keepdims=False)
            return picked.reshape(lead, rows // 2, cols)

        send = sum(half(value, 1 - mine).astype(f32) for value in self.parts)
        self.sent = send.astype(bf16)
        self.parts = [half(value, mine) for value in self.parts]
        self.got = swap(self.sent, axis, bit)

    def finish(self, other=None, hard=False):
        if self.got is not None:
            order = hold if hard else after
            self.parts.append(self.got if other is None else order(self.got, other))
            self.got = None

    def result(self):
        self.finish()
        while self.order:
            self.start()
            self.finish()
        return sum(value.astype(f32) for value in self.parts)


def after_sends(value, *sums):
    sends = [each.sent for each in sums if each.sent is not None]
    return after(value, *sends)


class SumEverywhere:
    def __init__(self, value):
        self.value = value
        self.order = axis_bits("seq")[::-1] + axis_bits("dp")[::-1]
        self.got = None

    def start(self):
        if self.order:
            self.got = swap(self.value, *self.order.pop(0))

    def finish(self, *others):
        if self.got is not None:
            self.value = self.value + (after(self.got, *others) if others else self.got)
            self.got = None

    def result(self):
        self.finish()
        while self.order:
            self.start()
            self.finish()
        return self.value


def pack_kernel(
    rank_ref, lengths_ref, table, taps, scorer, gain_a, gain_f, query, key, value, gate, up, down,
    output, columns, first_half, second_half, packed, rows, *, total_tokens,
):
    shard = table.shape[1]
    live = jnp.int32(0)
    for s in range(lengths_ref.shape[0]):
        live += jnp.minimum((lengths_ref[s] + 1) // 2, total_tokens)
    live = jnp.where(rank_ref[0] == 0, live, 0)
    first = lax.broadcasted_iota(jnp.int32, (1, shard), 1) == 0
    rows[...] = jnp.zeros_like(rows)
    rows[0:VOCAB, 0:shard] = table[...].astype(f32)
    rows[VOCAB : VOCAB + 4, 0:shard] = taps[...].astype(f32)
    for i, vector in enumerate((scorer, gain_a, gain_f)):
        rows[VOCAB + 4 + i : VOCAB + 5 + i, 0:shard] = vector[...].astype(f32)
    for i, part in enumerate((live // 64, live % 64)):
        at = VOCAB + 7 + i
        rows[at : at + 1, 0:shard] = jnp.where(first, part, 0).astype(f32)
    columns[...] = rows[...].T[0:shard, :].astype(bf16)

    pieces = [query[:, i * SIDE : (i + 1) * SIDE] for i in range(PAIRS)]
    for i in range(PAIRS):
        pieces += [key[:, i * SIDE : (i + 1) * SIDE], value[:, i * SIDE : (i + 1) * SIDE]]
    for half in (first_half, second_half):
        count = half.shape[1] // SIDE
        for i in range(count):
            half[:, i * SIDE : (i + 1) * SIDE] = pieces.pop(0)

    ffn_dim = gate.shape[1]
    packed[:, 0:ffn_dim] = gate[...]
    packed[:, ffn_dim : 2 * ffn_dim] = up[...]
    packed[:, 3 * ffn_dim :] = output[...]
    third = D // 3
    wide = down[...].astype(f32)
    for group in range(down.shape[0] // 64):
        for i in range(8):
            at = group * 64 + i * 8
            tiles = [wide[at : at + 8, j * third : (j + 1) * third] for j in range(3)]
            start = 2 * ffn_dim + i * third
            packed[group * 24 : (group + 1) * 24, start : start + third] = jnp.concatenate(
                tiles, axis=0
            ).astype(bf16)


def pack(rank, lengths, table, taps, vectors, attn, feed_weights, total_tokens):
    smem = pl.BlockSpec(memory_space=pltpu.SMEM)
    shard, ffn_dim = table.shape[1], feed_weights[0].shape[1]
    shapes = [(shard, TABLE), (shard, 3 * D // 2), (shard, 3 * D // 2), (shard, 3 * ffn_dim + D)]
    arrays = (table, taps, *vectors, *attn, *feed_weights)

    def whole(shape):
        return pl.BlockSpec(shape, lambda i: (0, 0))

    return pl.pallas_call(
        partial(pack_kernel, total_tokens=total_tokens),
        grid=(1,),
        in_specs=[smem, smem] + [whole(array.shape) for array in arrays],
        out_specs=[whole(shape) for shape in shapes],
        out_shape=[jax.ShapeDtypeStruct(shape, bf16) for shape in shapes],
        scratch_shapes=[pltpu.VMEM((TABLE, -(-shard // 128) * 128), f32)],
        cost_estimate=pl.CostEstimate(flops=100_000_000, bytes_accessed=1_000_000, transcendentals=0),
        name="pack",
    )(rank, lengths, *arrays)


def pack_plain(rank, lengths, table, taps, vectors, attn, feed_weights, total_tokens):
    shard = table.shape[1]
    live = jnp.sum(jnp.minimum((lengths + 1) // 2, total_tokens))
    live = jnp.where(rank[0] == 0, live, 0)
    counts = jnp.stack([live // 64, live % 64])
    at_count = (jnp.arange(shard) == 0).astype(jnp.int32)
    columns = jnp.concatenate(
        [table, taps, *vectors, (counts[:, None] * at_count[None]).astype(bf16)], axis=0
    )
    columns = jnp.pad(columns, ((0, TABLE - columns.shape[0]), (0, 0))).T
    query, key, value = attn
    pairs = jnp.stack([key.reshape(shard, PAIRS, SIDE), value.reshape(shard, PAIRS, SIDE)], axis=2)
    rows = jnp.concatenate([query, pairs.reshape(shard, 2 * D)], axis=1)
    gate, up, down, output = feed_weights
    packed = jnp.concatenate([gate, up, down.reshape(shard, gate.shape[1]), output], axis=1)
    return columns, rows[:, : 3 * D // 2], rows[:, 3 * D // 2 :], packed


def unpack_kernel(packed, gate, up, down, output):
    ffn_dim = gate.shape[1]
    third = D // 3
    value = packed[...].astype(f32)
    gate[...] = value[:, :ffn_dim]
    up[...] = value[:, ffn_dim : 2 * ffn_dim]
    output[...] = value[:, 3 * ffn_dim :]
    for group in range(down.shape[0] // 64):
        for i in range(8):
            at = group * 64 + i * 8
            start = 2 * ffn_dim + i * third
            for j in range(3):
                row = group * 24 + j * 8
                down[at : at + 8, j * third : (j + 1) * third] = value[
                    row : row + 8, start : start + third
                ]


def unpack(packed, ffn_dim, down_rows):
    shard = packed.shape[0]
    shapes = [(shard, ffn_dim), (shard, ffn_dim), (down_rows, D), (shard, D)]

    def whole(shape):
        return pl.BlockSpec(shape, lambda i: (0, 0))

    return pl.pallas_call(
        unpack_kernel,
        grid=(1,),
        in_specs=[whole(packed.shape)],
        out_specs=[whole(shape) for shape in shapes],
        out_shape=[jax.ShapeDtypeStruct(shape, f32) for shape in shapes],
        name="unpack",
    )(packed)


def up(x):
    return pltpu.roll(x, x.shape[0] - 1, 0)


def down(x):
    return pltpu.roll(x, 1, 0)


def ahead_lane(x):
    return pltpu.roll(x, x.shape[1] - 1, 1)


def behind_lane(x):
    return pltpu.roll(x, 1, 1)


def triples(c, m0, m1):
    c0, c1, c2, c3 = c
    p01, p23 = c0 + c1, c2 + c3
    t0, t1, t2, t3 = behind_lane(c3) + p01, p01 + c2, c1 + p23, p23 + ahead_lane(c0)
    before, after = (behind_lane(t3), t0, t1, t2), (t1, t2, t3, ahead_lane(t0))
    here = (t0, t1, t2, t3)
    return tuple(
        jnp.where(m0[k], after[k], jnp.where(m1[k], here[k], before[k])) for k in range(4)
    )


def live_rows(first, rows, total_bytes):
    row = lax.broadcasted_iota(jnp.int32, (rows, 128), 0)
    live = []
    for k in range(4):
        pos = first + 4 * (row - 8) + k
        live.append(((pos >= 0) & (pos < total_bytes)).astype(f32))
    return live


def lane_marks(first, wide, total_bytes):
    row = lax.broadcasted_iota(jnp.int32, (1, wide), 1)
    live, m0, m1 = [], [], []
    for k in range(4):
        pos = first + 4 * (row - 8) + k
        live.append(((pos >= 0) & (pos < total_bytes)).astype(f32))
        shifted = (pos + 48).astype(f32)
        third = jnp.floor((shifted + 0.5) * (1.0 / 3.0))
        rest = shifted - 3.0 * third
        m0.append(rest < 0.5)
        m1.append((rest > 0.5) & (rest < 1.5))
    return live, m0, m1


def to_lanes(accs, count, flat):
    rows = accs.shape[1]
    lane = lax.broadcasted_iota(jnp.int32, (rows, 128), 1)
    value = jnp.zeros((rows, 128), f32)
    for k in range(count):
        value = jnp.where(lane == k, jnp.sum(accs[k], axis=-1, keepdims=True), value)
    flat[0:rows, :] = value
    turned = flat[...].T
    return [turned[k : k + 1, :] for k in range(count)]


def to_rows(lines, lines_ref, accs):
    rows = accs.shape[1]
    for k, line in enumerate(lines):
        lines_ref[k : k + 1, :] = line
    turned = lines_ref[...].T
    for k in range(len(lines)):
        accs[k] = jnp.broadcast_to(turned[0:rows, k : k + 1], (rows, 128))


def lane_chunk(i):
    return pl.ds(pl.multiple_of(i * 128, 128), 128)


def embed_bytes(ids, table, emb):
    lane = lax.broadcasted_iota(jnp.int32, (ids.shape[0], TABLE), 1)
    emb[...] = nt((ids == lane).astype(bf16), table)


def small_rows(table, small):
    lane = lax.broadcasted_iota(jnp.int32, (8, TABLE), 1)
    row = lax.broadcasted_iota(jnp.int32, (8, TABLE), 0)
    small[...] = nt((lane == row + VOCAB).astype(bf16), table)


def block_probs(emb, small, conv, accs, flat, live, m0, m1, rows):
    accs[0:4] = jnp.zeros((4, rows, 128), f32)

    def step(i, _):
        chunk = lane_chunk(i)
        w0, w1, w2, w3 = [small[k : k + 1, chunk] for k in range(4)]
        scorer = small[4:5, chunk]
        e0, e1, e2, e3 = [emb[k * rows : (k + 1) * rows, chunk] for k in range(4)]
        e3d, e0u, e1u = down(e3), up(e0), up(e1)
        c = (
            w0 * e3d + w1 * e0 + w2 * e1 + w3 * e2,
            w0 * e0 + w1 * e1 + w2 * e2 + w3 * e3,
            w0 * e1 + w1 * e2 + w2 * e3 + w3 * e0u,
            w0 * e2 + w1 * e3 + w2 * e0u + w3 * e1u,
        )
        for k in range(4):
            value = c[k] * live[k]
            conv[k, :, chunk] = value
            accs[k] += value * scorer
        return 0

    lax.fori_loop(0, D // 128, step, 0)
    score = to_lanes(accs, 4, flat)
    three = triples(score, m0, m1)
    p01, p23 = score[0] + score[1], score[2] + score[3]
    quad = 0.25 * (p01 + p23)
    probs = []
    for k in range(4):
        scores = (score[k], 0.5 * (p01, p01, p23, p23)[k], three[k] * (1.0 / 3.0), quad)
        top = jnp.maximum(jnp.maximum(scores[0], scores[1]), jnp.maximum(scores[2], scores[3]))
        powers = [jnp.exp(value - top) for value in scores]
        norm = 1.0 / (powers[0] + powers[1] + powers[2] + powers[3])
        probs.append([power * norm for power in powers])
    return probs


def reach(m0, m1, k, ahead):
    one = jnp.ones(m0[k].shape, f32)
    zero = jnp.zeros_like(one)
    if ahead == 0:
        return one
    if ahead == 1:
        return jnp.where(m0[k] | m1[k], one, zero)
    if ahead == 2:
        return jnp.where(m0[k], one, zero)
    if ahead == -1:
        return jnp.where(m0[k], zero, one)
    return jnp.where(m0[k] | m1[k], zero, one)


def token_weights(probs, m0, m1):
    weights = []
    for half in range(2):
        first, second = probs[2 * half], probs[2 * half + 1]
        pair = 0.5 * (first[1] + second[1])
        quad = 0.25 * (first[3] + second[3])
        row = []
        for j in range(6):
            place = 2 * half - 2 + j
            value = jnp.zeros_like(pair)
            for k, p in ((2 * half, first), (2 * half + 1, second)):
                ahead = place - k
                if abs(ahead) <= 2:
                    value += p[2] * (1.0 / 3.0) * reach(m0, m1, k, ahead)
                if ahead == 0:
                    value += p[0]
            if 0 <= place < 4:
                value += quad
            if place // 2 == half:
                value += pair
            row.append(value)
        weights.append(row)
    return weights


def places(c):
    c0, c1, c2, c3 = c
    return ((down(c2), down(c3), c0, c1, c2, c3), (c0, c1, c2, c3, up(c0), up(c1)))


def pool_kernel(first_ref, ids, table, *rest, rows, total_bytes):
    resid, normed, emb, small, conv, accs, flat, lines, tokens = rest[-9:]
    first = first_ref[0]
    embed_bytes(ids[...], table[...], emb)
    small_rows(table[...], small)

    @pl.when(pl.program_id(0) == 0)
    def _():
        flat[...] = jnp.zeros_like(flat)
        lines[...] = jnp.zeros_like(lines)

    _, m0, m1 = lane_marks(first, flat.shape[0], total_bytes)
    live = live_rows(first, rows, total_bytes)
    probs = block_probs(emb, small, conv, accs, flat, live, m0, m1, rows)
    weights = token_weights(probs, m0, m1)
    to_rows([0.5 * weights[half][j] for half in range(2) for j in range(6)], lines, accs)
    own = rows - 16

    def step(i, square):
        chunk = lane_chunk(i)
        around = places([conv[k, :, chunk] for k in range(4)])
        for half in range(2):
            token = accs[6 * half] * around[half][0]
            for j in range(1, 6):
                token += accs[6 * half + j] * around[half][j]
            tokens[i, pl.ds(half, own, stride=2), :] = token[8 : 8 + own]
        values = tokens[i]
        resid[:, chunk] = values
        return square + values * values

    square = lax.fori_loop(0, D // 128, step, jnp.zeros((2 * own, 128), f32))
    scale = lax.rsqrt(jnp.sum(square, axis=-1, keepdims=True) * (1.0 / D) + epsilon)
    normed[...] = (resid[...] * scale * small[5:6, :]).astype(bf16)


def pool(first, ids, table, deps, total_bytes):
    count, wide, _ = ids.shape
    rows = wide // 4
    tokens = 2 * (rows - 16)
    return pl.pallas_call(
        partial(pool_kernel, rows=rows, total_bytes=total_bytes),
        grid=(count,),
        in_specs=[
            pl.BlockSpec(memory_space=pltpu.SMEM),
            pl.BlockSpec((None, wide, 1), lambda i: (i, 0, 0)),
            pl.BlockSpec((D, TABLE), lambda i: (0, 0)),
        ]
        + [pl.BlockSpec(memory_space=pl.ANY)] * len(deps),
        out_specs=[
            pl.BlockSpec((None, tokens, D), lambda i: (i, 0, 0)),
            pl.BlockSpec((None, tokens, D), lambda i: (i, 0, 0)),
        ],
        out_shape=[
            jax.ShapeDtypeStruct((count, tokens, D), f32),
            jax.ShapeDtypeStruct((count, tokens, D), bf16),
        ],
        scratch_shapes=[
            pltpu.VMEM((wide, D), f32),
            pltpu.VMEM((8, D), f32),
            pltpu.VMEM((4, rows, D), f32),
            pltpu.VMEM((12, rows, 128), f32),
            pltpu.VMEM((2 * 128, 128), f32),
            pltpu.VMEM((16, 2 * 128), f32),
            pltpu.VMEM((D // 128, tokens, 128), f32),
        ],
        cost_estimate=pl.CostEstimate(flops=count * 3_000_000_000, bytes_accessed=4_000_000, transcendentals=0),
        name="pool",
    )(first, ids, table, *deps)


def pool_back_kernel(
    first_ref, ids, ids_row, table, pulled_own, from_core, from_x, dq, query_w, resid, after,
    feed_stats, *rest, rows, total_bytes, given, last, deps,
):
    if given:
        embed_before, small_before = rest[:2]
        rest = rest[2:]
    rest = rest[deps:]
    if last:
        turned = rest[0]
        embed_grad, small_grad = rest[-2:]
        rest = rest[1:-2]
    else:
        embed_grad, small_grad = rest[:2]
        rest = rest[2:]
    emb, small, conv, accs, flat, lines, tokens, pulls, emb_grad = rest
    first = first_ref[0]
    own = rows - 16
    chunks = D // 128

    if given:
        small_grad[...] = small_before[...]
    else:
        small_grad[...] = jnp.zeros_like(small_grad)
    flat[...] = jnp.zeros_like(flat)
    lines[...] = jnp.zeros_like(lines)

    embed_bytes(ids[...], table[...], emb)
    small_rows(table[...], small)
    live_lane, m0, m1 = lane_marks(first, flat.shape[0], total_bytes)
    live = live_rows(first, rows, total_bytes)

    x = resid[...]
    gn = pulled_own[...].astype(f32) + from_core[...].astype(f32) + from_x[...].astype(f32)
    gn = gn + nt(dq[...], query_w[...])
    scale = lax.rsqrt(jnp.mean(x * x, axis=-1, keepdims=True) + epsilon)
    gain = small[5:6, :]
    small_grad[5:6, :] += jnp.sum(gn * x * scale, axis=0, keepdims=True)
    gg = gain * gn
    inner = jnp.mean(gg * x, axis=-1, keepdims=True)
    total = after[...] + scale * gg - x * (scale * scale * scale * inner)
    for i in range(chunks):
        tokens[i] = total[:, i * 128 : (i + 1) * 128]

    probs = block_probs(emb, small, conv, accs, flat, live, m0, m1, rows)
    accs[0:12] = jnp.zeros((12, rows, 128), f32)
    pulls[:, 0:8, :] = jnp.zeros((2, 8, D), f32)
    pulls[:, rows - 8 : rows, :] = jnp.zeros((2, 8, D), f32)

    def dots(i, _):
        chunk = lane_chunk(i)
        around = places([conv[k, :, chunk] for k in range(4)])
        for half in range(2):
            pulls[half, 8 : 8 + own, chunk] = 0.5 * tokens[i, pl.ds(half, own, stride=2), :]
            g = pulls[half, :, chunk]
            for j in range(6):
                accs[6 * half + j] += g * around[half][j]
        return 0

    lax.fori_loop(0, chunks, dots, 0)
    every = to_lanes(accs, 12, flat)
    pulled = []
    for half in range(2):
        at = every[6 * half : 6 * half + 6]
        pair = 0.5 * (at[2] + at[3])
        quad = 0.25 * (at[2] + at[3] + (at[4] + at[5] if half == 0 else at[0] + at[1]))
        for k in (2 * half, 2 * half + 1):
            middle = k - (2 * half - 2)
            three = sum(
                at[middle + ahead] * reach(m0, m1, k, ahead)
                for ahead in range(-2, 3)
                if 0 <= middle + ahead < 6
            ) * (1.0 / 3.0)
            gd = (at[middle], pair, three, quad)
            p = probs[k]
            mean = p[0] * gd[0] + p[1] * gd[1] + p[2] * gd[2] + p[3] * gd[3]
            pulled.append([p[b] * (gd[b] - mean) for b in range(4)])

    spread = triples([pulled[k][2] for k in range(4)], m0, m1)
    quad = 0.25 * (pulled[0][3] + pulled[1][3] + pulled[2][3] + pulled[3][3])
    weights = token_weights(probs, m0, m1)
    factors = []
    for k in range(4):
        half = k // 2
        pair = 0.5 * (pulled[2 * half][1] + pulled[2 * half + 1][1])
        factors.append((pulled[k][0] + pair + spread[k] * (1.0 / 3.0) + quad) * live_lane[k])
    at_row = lax.broadcasted_iota(jnp.int32, (1, flat.shape[0]), 1)
    inside = (at_row >= 8) & (at_row < 8 + own)
    even = [jnp.where(inside, weight, 0.0) for weight in weights[0]]
    odd = [jnp.where(inside, weight, 0.0) for weight in weights[1]]
    reached = (
        (behind_lane(odd[4]), even[2], odd[0]),
        (behind_lane(odd[5]), even[3], odd[1]),
        (even[4], odd[2], ahead_lane(even[0])),
        (even[5], odd[3], ahead_lane(even[1])),
    )
    for k in range(4):
        for j in range(3):
            factors.append(reached[k][j] * live_lane[k])
    to_rows(factors, lines, accs)

    def back(i, _):
        chunk = lane_chunk(i)
        w0, w1, w2, w3 = [small[k : k + 1, chunk] for k in range(4)]
        scorer = small[4:5, chunk]
        g0, g1 = pulls[0, :, chunk], pulls[1, :, chunk]
        g1d, g0u = down(g1), up(g0)
        e0, e1, e2, e3 = [emb[k * rows : (k + 1) * rows, chunk] for k in range(4)]
        near = ((g1d, g0, g1), (g1d, g0, g1), (g0, g1, g0u), (g0, g1, g0u))
        score = jnp.zeros((rows, 128), f32)
        gc = []
        for k in range(4):
            score += accs[k] * conv[k, :, chunk]
            value = accs[k] * scorer
            for j in range(3):
                value += accs[4 + 3 * k + j] * near[k][j]
            gc.append(value)
        small_grad[4:5, chunk] += jnp.sum(score, axis=0, keepdims=True)
        gc0, gc1, gc2, gc3 = gc
        e3d, e0u, e1u = down(e3), up(e0), up(e1)
        taps = (
            gc0 * e3d + gc1 * e0 + gc2 * e1 + gc3 * e2,
            gc0 * e0 + gc1 * e1 + gc2 * e2 + gc3 * e3,
            gc0 * e1 + gc1 * e2 + gc2 * e3 + gc3 * e0u,
            gc0 * e2 + gc1 * e3 + gc2 * e0u + gc3 * e1u,
        )
        for k in range(4):
            small_grad[k : k + 1, chunk] += jnp.sum(taps[k], axis=0, keepdims=True)
        gc3d, gc2d, gc0u = down(gc3), down(gc2), up(gc0)
        grads = (
            w0 * gc1 + w1 * gc0 + w2 * gc3d + w3 * gc2d,
            w0 * gc2 + w1 * gc1 + w2 * gc0 + w3 * gc3d,
            w0 * gc3 + w1 * gc2 + w2 * gc1 + w3 * gc0,
            w0 * gc0u + w1 * gc3 + w2 * gc2 + w3 * gc1,
        )
        for k in range(4):
            emb_grad[k * rows : (k + 1) * rows, chunk] = grads[k].astype(bf16)
        return 0

    lax.fori_loop(0, chunks, back, 0)
    row = lax.broadcasted_iota(jnp.int32, (TABLE, 4 * rows), 0)
    total = nn((ids_row[...] == row).astype(bf16), emb_grad[...])
    if given:
        total = total + embed_before[...]
    embed_grad[...] = total
    if last:
        small_grad[6:7, :] = feed_stats[0:1, :]
        embed_grad[VOCAB : VOCAB + 7, :] = small_grad[0:7, :]
        turned[...] = embed_grad[...].T.astype(bf16)


def pool_back(
    seq, first, ids, ids_row, table, pulled, from_core, from_x, dq, qkv, resid, after_grad,
    feed_stats, before, deps, total_bytes,
):
    count, wide, _ = ids.shape
    rows = wide // 4
    tokens = 2 * (rows - 16)
    last = seq == count - 1
    token_spec = pl.BlockSpec((None, tokens, D), lambda i: (seq, 0, 0))
    table_sum = pl.BlockSpec((TABLE, D), lambda i: (0, 0))
    small_sum = pl.BlockSpec((8, D), lambda i: (0, 0))
    sums = [pltpu.VMEM((TABLE, D), f32), pltpu.VMEM((8, D), f32)]
    return pl.pallas_call(
        partial(
            pool_back_kernel, rows=rows, total_bytes=total_bytes, given=bool(before), last=last,
            deps=len(deps),
        ),
        grid=(1,),
        in_specs=[
            pl.BlockSpec(memory_space=pltpu.SMEM),
            pl.BlockSpec((None, wide, 1), lambda i: (seq, 0, 0)),
            pl.BlockSpec((None, 1, wide), lambda i: (seq, 0, 0)),
            pl.BlockSpec((D, TABLE), lambda i: (0, 0)),
            token_spec,
            token_spec,
            pl.BlockSpec((tokens, D), lambda i: (0, 0)),
            token_spec,
            pl.BlockSpec((D, D), lambda i: (0, 0)),
            token_spec,
            token_spec,
            small_sum,
        ]
        + ([table_sum, small_sum] if before else [])
        + [pl.BlockSpec(memory_space=pl.ANY)] * len(deps),
        out_specs=pl.BlockSpec((D, TABLE), lambda i: (0, 0)) if last else [table_sum, small_sum],
        out_shape=jax.ShapeDtypeStruct((D, TABLE), bf16)
        if last
        else [jax.ShapeDtypeStruct((TABLE, D), f32), jax.ShapeDtypeStruct((8, D), f32)],
        scratch_shapes=[
            pltpu.VMEM((wide, D), f32),
            pltpu.VMEM((8, D), f32),
            pltpu.VMEM((4, rows, D), f32),
            pltpu.VMEM((16, rows, 128), f32),
            pltpu.VMEM((2 * 128, 128), f32),
            pltpu.VMEM((16, 2 * 128), f32),
            pltpu.VMEM((D // 128, tokens, 128), f32),
            pltpu.VMEM((2, rows, D), f32),
            pltpu.VMEM((wide, D), bf16),
        ]
        + (sums if last else []),
        cost_estimate=pl.CostEstimate(flops=9_000_000_000, bytes_accessed=8_000_000, transcendentals=0),
        name="pool_back",
    )(
        first, ids, ids_row, table, pulled, from_core, from_x, dq, qkv, resid, after_grad,
        feed_stats, *before, *deps,
    )


def prepare_kernel(
    rank_ref, lengths_ref, bias_ref, lanes_bias, tile, turned, side, diag, *, queries, keys, parts
):
    head = pl.program_id(0)
    rank = rank_ref[0]

    @pl.when(head == 0)
    def _():
        place = lax.broadcasted_iota(jnp.int32, (BUCKETS, 6 * HALF), 1)
        inside = lax.rem(place, 2 * HALF)
        offset = jnp.where(inside < HALF, inside, inside - 2 * HALF)
        relative = (place // (2 * HALF) - 1) * HALF + offset
        bucket = lax.broadcasted_iota(jnp.int32, (BUCKETS, 6 * HALF), 0)
        hot = (bucket_of(relative) == bucket).astype(bf16)
        diag[...] = lax.dot_general(
            lanes_bias[...], hot, (((0,), (0,)), ((), ())), preferred_element_type=f32
        )
        row = lax.broadcasted_iota(jnp.int32, (keys, SIDE), 0)
        lane = lax.broadcasted_iota(jnp.int32, (keys, SIDE), 1)
        at = lax.rem(rank * queries - HALF + row + keys, keys)
        far = row >= queries + 2 * HALF
        right = far & (at > rank * queries)
        left = far & (at <= rank * queries)
        fixed = jnp.where(
            right,
            lanes_bias[31:32, :].astype(f32),
            jnp.where(left, lanes_bias[15:16, :].astype(f32), 0.0),
        )
        fixed = jnp.where((lane >= ONES) & (lane < ONES + 3), 1.0, fixed)
        fixed = jnp.where((lane == LEFT) & left | (lane == RIGHT) & right, 1.0, fixed)
        for s in range(side.shape[0]):
            masked = jnp.where(2 * at < lengths_ref[s], 0.0, masked_score)
            side[s] = jnp.where(lane == 0, masked, fixed).astype(bf16)

    blocks = []
    for index in range(3):
        line = diag[pl.ds(head + 1, 1), index * 2 * HALF : (index + 1) * 2 * HALF]
        full = jnp.broadcast_to(line, (HALF, 2 * HALF))
        blocks.append(pltpu.roll(full, 0, 1, stride=1, stride_axis=0)[:, :HALF])
    turned_blocks = [block.T.astype(bf16) for block in blocks]
    blocks = [block.astype(bf16) for block in blocks]
    behind = jnp.full((HALF, HALF), bias_ref[15, head], f32).astype(bf16)
    ahead = jnp.full((HALF, HALF), bias_ref[31, head], f32).astype(bf16)
    steps = queries // HALF
    for q in range(steps):
        for n in range(steps + 2):
            apart = n - 1 - q
            wrapped = ((n == 0) & (rank == 0), (n == steps + 1) & (rank == parts - 1))
            plain = behind if apart < -1 else ahead if apart > 1 else blocks[apart + 1]
            flipped = behind if apart < -1 else ahead if apart > 1 else turned_blocks[apart + 1]
            if n == 0:
                plain = jnp.where(wrapped[0], ahead, plain)
                flipped = jnp.where(wrapped[0], ahead, flipped)
            if n == steps + 1:
                plain = jnp.where(wrapped[1], behind, plain)
                flipped = jnp.where(wrapped[1], behind, flipped)
            tile[q * HALF : (q + 1) * HALF, n * HALF : (n + 1) * HALF] = plain
            turned[n * HALF : (n + 1) * HALF, q * HALF : (q + 1) * HALF] = flipped


def prepare(rank, lengths, bias, queries, keys, parts):
    near = queries + 2 * HALF
    seqs = lengths.shape[0]
    lanes_bias = jnp.pad(bias, ((0, 0), (1, SIDE - 1 - HEADS)))
    smem = pl.BlockSpec(memory_space=pltpu.SMEM)
    return pl.pallas_call(
        partial(prepare_kernel, queries=queries, keys=keys, parts=parts),
        grid=(HEADS,),
        in_specs=[smem, smem, smem, pl.BlockSpec((BUCKETS, SIDE), lambda i: (0, 0))],
        out_specs=[
            pl.BlockSpec((None, queries, near), lambda i: (i, 0, 0)),
            pl.BlockSpec((None, near, queries), lambda i: (i, 0, 0)),
            pl.BlockSpec((seqs, keys, SIDE), lambda i: (0, 0, 0)),
        ],
        out_shape=[
            jax.ShapeDtypeStruct((HEADS, queries, near), bf16),
            jax.ShapeDtypeStruct((HEADS, near, queries), bf16),
            jax.ShapeDtypeStruct((seqs, keys, SIDE), bf16),
        ],
        scratch_shapes=[pltpu.VMEM((SIDE, 6 * HALF), f32)],
        cost_estimate=pl.CostEstimate(flops=6_000_000_000, bytes_accessed=7_000_000, transcendentals=0),
        name="prepare",
    )(rank, lengths, bias.astype(f32), lanes_bias)


def row_offset(rank, step, blocks):
    half = lax.rem(2 * rank - 1 + step + 2 * blocks, 2 * blocks)
    apart = jnp.bitwise_xor(rank, half // 2)
    slot = (apart % 2) * 2 + apart // 2
    return pl.multiple_of(slot * (2 * HALF) + (half % 2) * HALF, HALF)


def side_lanes(rows, picks):
    lane = lax.broadcasted_iota(jnp.int32, (rows, SIDE), 1)
    value = jnp.zeros((rows, SIDE), f32)
    for index, entry in picks:
        value = jnp.where(lane == index, entry, value)
    return value.astype(bf16)


def three_parts(value):
    high = value.astype(bf16).astype(f32)
    rest = value - high
    middle = rest.astype(bf16).astype(f32)
    return high, middle, rest - middle


def one_head(values, head):
    lane = lax.broadcasted_iota(jnp.int32, values.shape, 1)
    return jnp.where((lane // HEAD_DIM) == head, values, jnp.zeros_like(values))


def attend_kernel(rank_ref, q, kv, side, bias, *rest, near, blocks):
    out, norm, kcat, vcat = rest[-4:]
    rank = rank_ref[0]
    pair = pl.program_id(1)
    queries = q.shape[0]

    @pl.when(pair == 0)
    def _():
        kcat[:, SIDE:] = side[...]
        norm[...] = jnp.zeros_like(norm)

    for step in range(2 * blocks):
        source = pl.ds(row_offset(rank, step, blocks), HALF)
        kcat[step * HALF : (step + 1) * HALF, :SIDE] = kv[source, :SIDE]
        vcat[step * HALF : (step + 1) * HALF, :] = kv[source, SIDE:]

    lane = lax.broadcasted_iota(jnp.int32, (queries, SIDE), 1)
    halves, every = [], []
    for head in range(2):
        extra = side_lanes(queries, [(0, 1.0), (1 + 2 * pair + head, 1.0)])
        wide = jnp.concatenate([one_head(q[...], head), extra], axis=1)
        every.append(nt(wide, kcat[...]))
    for head in range(2):
        logits = every[head]
        close = logits[:, :near] + bias[head].astype(f32)
        away = logits[:, near:]
        top = jnp.maximum(
            jnp.max(close, axis=-1, keepdims=True), jnp.max(away, axis=-1, keepdims=True)
        )
        close = jnp.exp(close - top)
        away = jnp.exp(away - top)
        total = jnp.sum(close, axis=-1, keepdims=True) + jnp.sum(away, axis=-1, keepdims=True)
        mixed = nn(close.astype(bf16), vcat[:near, :]) + nn(away.astype(bf16), vcat[near:, :])
        halves.append(mixed * (1.0 / total))
        norm[...] = jnp.where(lane == 2 * pair + head, top + jnp.log(total), norm[...])
    out[...] = jnp.where(lane < HEAD_DIM, halves[0], halves[1]).astype(bf16)


def attend(rank, q, kv, side, bias, deps):
    seqs, queries, _ = q.shape
    keys = kv.shape[1]
    near = bias.shape[-1]
    blocks = keys // queries
    return pl.pallas_call(
        partial(attend_kernel, near=near, blocks=blocks),
        grid=(seqs, PAIRS),
        in_specs=[
            pl.BlockSpec(memory_space=pltpu.SMEM),
            pl.BlockSpec((None, queries, SIDE), lambda s, i: (s, 0, i)),
            pl.BlockSpec((None, keys, 2 * SIDE), lambda s, i: (s, 0, i)),
            pl.BlockSpec((None, keys, SIDE), lambda s, i: (s, 0, 0)),
            pl.BlockSpec((2, queries, near), lambda s, i: (i, 0, 0)),
        ]
        + [pl.BlockSpec(memory_space=pl.ANY)] * len(deps),
        out_specs=[
            pl.BlockSpec((None, queries, SIDE), lambda s, i: (s, 0, i)),
            pl.BlockSpec((None, queries, SIDE), lambda s, i: (s, 0, 0)),
        ],
        out_shape=[
            jax.ShapeDtypeStruct((seqs, queries, D), bf16),
            jax.ShapeDtypeStruct((seqs, queries, SIDE), f32),
        ],
        scratch_shapes=[pltpu.VMEM((keys, 2 * SIDE), bf16), pltpu.VMEM((keys, SIDE), bf16)],
        cost_estimate=pl.CostEstimate(flops=25_000_000_000, bytes_accessed=8_000_000, transcendentals=0),
        name="attend",
    )(rank, q, kv, side, bias, *deps)


def attend_back_kernel(
    rank_ref, q, kv, side, bias, norm, mixed, grad, dq, dkv, dnear, dfar, kcat, vcat, kturn, *,
    near, blocks, part,
):
    rank = rank_ref[0]
    pair = pl.program_id(1)
    queries = q.shape[0]
    keys = kv.shape[0]

    @pl.when(pair == 0)
    def _():
        kcat[:, SIDE:] = side[...]
        vcat[:, SIDE:] = side[...]
        kturn[SIDE:, :] = side[...].astype(f32).T[ONES : 2 * ONES, :].astype(bf16)

    for step in range(2 * blocks):
        source = pl.ds(row_offset(rank, step, blocks), HALF)
        kcat[step * HALF : (step + 1) * HALF, :SIDE] = kv[source, :SIDE]
        vcat[step * HALF : (step + 1) * HALF, :SIDE] = kv[source, SIDE:]
    kturn[:SIDE, :] = kcat[:, :SIDE].astype(f32).T.astype(bf16)

    lane = lax.broadcasted_iota(jnp.int32, (queries, SIDE), 1)
    queries_of, grads_of, wide_q, wide_g = [], [], [], []
    products = grad[...].astype(f32) * mixed[...].astype(f32)
    for head in range(2):
        index = 2 * pair + head
        level = jnp.sum(jnp.where(lane == index, norm[...], 0.0), axis=-1, keepdims=True)
        delta = jnp.sum(
            jnp.where((lane // HEAD_DIM) == head, products, 0.0), axis=-1, keepdims=True
        )
        la, lb, lc = three_parts(-level)
        da, db, dc = three_parts(-delta)
        queries_of.append(one_head(q[...], head))
        grads_of.append(one_head(grad[...], head))
        extra = [(0, 1.0), (1 + index, 1.0), (ONES, la), (ONES + 1, lb), (ONES + 2, lc)]
        wide_q.append(jnp.concatenate([queries_of[head], side_lanes(queries, extra)], axis=1))
        extra = [(ONES, da), (ONES + 1, db), (ONES + 2, dc)]
        wide_g.append(jnp.concatenate([grads_of[head], side_lanes(queries, extra)], axis=1))

    sums = [jnp.zeros((kturn.shape[0], queries), f32) for _ in range(2)]
    for base in range(0, keys, part):
        span = slice(base, base + part)
        value_part = jnp.zeros((part, SIDE), f32)
        key_part = jnp.zeros((part, SIDE), f32)
        for head in range(2):
            logits = nt(kcat[span, :], wide_q[head])
            if base < near:
                here = min(near, base + part) - base
                close = logits[:here] + bias[head, base : base + here, :].astype(f32)
                logits = close if here == part else jnp.concatenate([close, logits[here:]], axis=0)
            probs = jnp.exp(logits)
            pull = nt(vcat[span, :], wide_g[head])
            low = (probs * pull).astype(bf16)
            value_part += nn(probs.astype(bf16), grads_of[head])
            key_part += nn(low, queries_of[head])
            sums[head] += nn(kturn[:, span], low)
            if base < near:
                here = min(near, base + part) - base
                dnear[head, base : base + here, :] = low[:here]
        for step in range(base // HALF, (base + part) // HALF):
            target = pl.ds(row_offset(rank, step, blocks), HALF)
            inner = slice(step * HALF - base, (step + 1) * HALF - base)
            dkv[target, :SIDE] = key_part[inner].astype(bf16)
            dkv[target, SIDE:] = value_part[inner].astype(bf16)
    turned = jnp.concatenate([sums[0][:HEAD_DIM], sums[1][HEAD_DIM:SIDE]], axis=0)
    dq[...] = turned.T.astype(bf16)
    for head in range(2):
        dfar[head] = sums[head][SIDE:, :]


def attend_back(rank, q, kv, side, bias, norm, mixed, grad):
    seqs, queries, _ = q.shape
    keys = kv.shape[1]
    near = bias.shape[1]
    blocks = keys // queries
    own = pl.BlockSpec((None, queries, SIDE), lambda s, i: (s, 0, i))
    every = pl.BlockSpec((None, keys, 2 * SIDE), lambda s, i: (s, 0, i))
    return pl.pallas_call(
        partial(attend_back_kernel, near=near, blocks=blocks, part=KEY_PART),
        grid=(seqs, PAIRS),
        in_specs=[
            pl.BlockSpec(memory_space=pltpu.SMEM),
            own,
            every,
            pl.BlockSpec((None, keys, SIDE), lambda s, i: (s, 0, 0)),
            pl.BlockSpec((2, near, queries), lambda s, i: (i, 0, 0)),
            pl.BlockSpec((None, queries, SIDE), lambda s, i: (s, 0, 0)),
            own,
            own,
        ],
        out_specs=[
            own,
            every,
            pl.BlockSpec((None, 2, near, queries), lambda s, i: (s, i, 0, 0)),
            pl.BlockSpec((None, 2, ONES, queries), lambda s, i: (s, i, 0, 0)),
        ],
        out_shape=[
            jax.ShapeDtypeStruct((seqs, queries, D), bf16),
            jax.ShapeDtypeStruct((seqs, keys, 2 * D), bf16),
            jax.ShapeDtypeStruct((seqs, HEADS, near, queries), bf16),
            jax.ShapeDtypeStruct((seqs, HEADS, ONES, queries), f32),
        ],
        scratch_shapes=[
            pltpu.VMEM((keys, 2 * SIDE), bf16),
            pltpu.VMEM((keys, 2 * SIDE), bf16),
            pltpu.VMEM((SIDE + ONES, keys), bf16),
        ],
        cost_estimate=pl.CostEstimate(flops=40_000_000_000, bytes_accessed=12_000_000, transcendentals=0),
        name="attend_back",
    )(rank, q, kv, side, bias, norm, mixed, grad)


def bias_grad_kernel(rank_ref, near, far, *rest, parts):
    out, lines = rest[-2:]
    rank = rank_ref[0]
    head = pl.program_id(0)
    seqs = near.shape[0]
    steps = near.shape[1] // HALF - 2
    first_in, last_in = rank != 0, rank != parts - 1

    def block(n, q):
        rows, cols = slice(n * HALF, (n + 1) * HALF), slice(q * HALF, (q + 1) * HALF)
        return sum(near[s, rows, cols].astype(f32) for s in range(seqs))

    sums = [jnp.zeros((HALF, HALF), f32) for _ in range(3)]
    left = sum(far[s, LEFT - ONES : LEFT - ONES + 1, :] for s in range(seqs))
    right = sum(far[s, RIGHT - ONES : RIGHT - ONES + 1, :] for s in range(seqs))
    left = [left[:, q * HALF : (q + 1) * HALF] for q in range(steps)]
    right = [right[:, q * HALF : (q + 1) * HALF] for q in range(steps)]
    for n in range(steps + 2):
        inside = first_in if n == 0 else last_in if n == steps + 1 else None
        for q in range(steps):
            value = block(n, q)
            apart = n - 1 - q
            if inside is not None:
                column = jnp.sum(value, axis=0, keepdims=True)
                outer = jnp.where(inside, 0.0, column)
                if n == 0:
                    right[q] += outer
                else:
                    left[q] += outer
                kept = jnp.where(inside, column, 0.0)
                if apart < -1:
                    left[q] += kept
                elif apart > 1:
                    right[q] += kept
                value = jnp.where(inside, value, 0.0)
            if abs(apart) <= 1:
                sums[apart + 1] += value
    found = []
    for value in sums:
        wide = jnp.concatenate([value, jnp.zeros((HALF, HALF), f32)], axis=1)
        folded = wide[0:8, :]
        for a in range(8, HALF, 8):
            folded += pltpu.roll(wide[a : a + 8, :], 2 * HALF - a, 1)
        line = folded[0:1, :]
        for b in range(1, 8):
            line += pltpu.roll(folded[b : b + 1, :], 2 * HALF - b, 1)
        found.append(line)
    found += [jnp.concatenate(left, axis=1), jnp.concatenate(right, axis=1)]
    lines[pl.ds(head, 1), :] = jnp.concatenate(found, axis=1)

    @pl.when(head == pl.num_programs(0) - 1)
    def _():
        shape = (10 * HALF, 128)
        place = lax.broadcasted_iota(jnp.int32, shape, 0)
        lane = lax.broadcasted_iota(jnp.int32, shape, 1)
        segment, inner = place // (2 * HALF), lax.rem(place, 2 * HALF)
        behind = jnp.where(inner < HALF, inner, inner - 2 * HALF)
        relative = (segment - 1) * HALF - behind
        bucket = jnp.where(segment == 3, 15, jnp.where(segment == 4, 31, bucket_of(relative)))
        hot = (bucket == lane).astype(bf16)
        split = jnp.concatenate([part.astype(bf16) for part in three_parts(lines[...])], axis=0)
        total = nn(split, hot)
        rows = lines.shape[0]
        out[...] = total[:rows] + total[rows : 2 * rows] + total[2 * rows :]


def bias_sums(rank, near_parts, far_parts, parts, deps):
    seqs, heads, near, queries = near_parts.shape
    assert queries == 2 * HALF
    return pl.pallas_call(
        partial(bias_grad_kernel, parts=parts),
        grid=(heads,),
        in_specs=[
            pl.BlockSpec(memory_space=pltpu.SMEM),
            pl.BlockSpec((seqs, None, near, queries), lambda i: (0, i, 0, 0)),
            pl.BlockSpec((seqs, None, ONES, queries), lambda i: (0, i, 0, 0)),
        ]
        + [pl.BlockSpec(memory_space=pl.ANY)] * len(deps),
        out_specs=pl.BlockSpec((16, 128), lambda i: (0, 0)),
        out_shape=jax.ShapeDtypeStruct((16, 128), f32),
        scratch_shapes=[pltpu.VMEM((16, 10 * HALF), f32)],
        cost_estimate=pl.CostEstimate(flops=6_000_000_000, bytes_accessed=9_000_000, transcendentals=0),
        name="bias_sums",
    )(rank, near_parts, far_parts, *deps)


def gelu_parts(x):
    inner = 0.7978845608028654 * (x + 0.044715 * (x * x * x))
    t = jnp.tanh(inner)
    half = 0.5 * (1.0 + t)
    slope = half + 0.5 * x * (1.0 - t * t) * (
        0.7978845608028654 * (1.0 + 0.134145 * (x * x))
    )
    return x * half, slope


def feed_kernel(
    place_ref, count_ref, lengths_ref, att, resid, teacher, gain, wide_hbm, down_hbm,
    block_out, normed, hidden, branch, gate_low, up_low, after_grad, after_low, att_grad, stats,
    act, steep, gate_w, up_w, down_w, output_w, sems, *, chunk,
):
    step = pl.program_id(0)
    rows = att.shape[0]
    ffn_dim = gate_w.shape[1]
    copies = [
        pltpu.make_async_copy(wide_hbm.at[:, 3 * ffn_dim : 3 * ffn_dim + D], output_w, sems.at[0]),
        pltpu.make_async_copy(wide_hbm.at[:, 0:ffn_dim], gate_w, sems.at[1]),
        pltpu.make_async_copy(wide_hbm.at[:, ffn_dim : 2 * ffn_dim], up_w, sems.at[2]),
        pltpu.make_async_copy(down_hbm, down_w, sems.at[3]),
    ]

    @pl.when(step == 0)
    def _():
        for copy in copies:
            copy.start()

    def arrived(index):
        @pl.when(step == 0)
        def _():
            copies[index].wait()

    @pl.when(step == 0)
    def _():
        stats[...] = jnp.zeros_like(stats)

    arrived(0)
    after = resid[...] + nn(att[...], output_w[...])
    scale = lax.rsqrt(jnp.mean(after * after, axis=-1, keepdims=True) + epsilon)
    normed[...] = (after * scale * gain[...]).astype(bf16)
    arrived(1)
    arrived(2)
    arrived(3)
    out = after
    for base in range(0, ffn_dim, chunk):
        span = slice(base, base + chunk)
        gate = nn(normed[...], gate_w[:, span])
        up_part = nn(normed[...], up_w[:, span])
        value, slope = gelu_parts(gate)
        act[:, span] = value
        steep[:, span] = slope * up_part
        low = (value * up_part).astype(bf16)
        hidden[:, span] = low
        out = out + nn(low, down_w[span, :])
    block_out[...] = out
    token = place_ref[0] + lax.broadcasted_iota(jnp.int32, (rows, D), 0)
    live = (2 * token < lengths_ref[step]).astype(f32)
    error = live * (out - teacher[...])
    stats[1:2, :] += jnp.sum(error * error, axis=0, keepdims=True)
    out_grad = (2.0 / count_ref[0]) * error
    branch[...] = out_grad.astype(bf16)
    back = jnp.zeros((rows, D), f32)
    for base in range(0, ffn_dim, chunk):
        span = slice(base, base + chunk)
        pull = nt(branch[...], down_w[span, :])
        gate_part = (pull * steep[:, span]).astype(bf16)
        up_part = (pull * act[:, span]).astype(bf16)
        gate_low[:, span] = gate_part
        up_low[:, span] = up_part
        back = back + nt(gate_part, gate_w[:, span]) + nt(up_part, up_w[:, span])
    stats[0:1, :] += jnp.sum(back * after * scale, axis=0, keepdims=True)
    gained = back * gain[...]
    inner = jnp.mean(gained * after, axis=-1, keepdims=True)
    total = out_grad + scale * gained - after * (scale * scale * scale * inner)
    after_grad[...] = total
    low = total.astype(bf16)
    after_low[...] = low
    att_grad[...] = nt(low, output_w[...]).astype(bf16)


def feed(place, count, lengths, att, resid, teacher, gain, wide, down_w):
    tokens = att.shape[0]
    seqs = lengths.shape[0]
    rows = tokens // seqs
    ffn_dim = down_w.shape[0]
    own = pl.BlockSpec((rows, D), lambda i: (i, 0))
    broad = pl.BlockSpec((rows, ffn_dim), lambda i: (i, 0))
    smem = pl.BlockSpec(memory_space=pltpu.SMEM)
    return pl.pallas_call(
        partial(feed_kernel, chunk=512),
        grid=(seqs,),
        in_specs=[
            smem,
            smem,
            smem,
            own,
            pl.BlockSpec((None, rows, D), lambda i: (i, 0, 0)),
            own,
            pl.BlockSpec((1, D), lambda i: (0, 0)),
            pl.BlockSpec(memory_space=pl.ANY),
            pl.BlockSpec(memory_space=pl.ANY),
        ],
        out_specs=[own, own, broad, own, broad, broad, own, own, own, pl.BlockSpec((8, D), lambda i: (0, 0))],
        out_shape=[
            jax.ShapeDtypeStruct((tokens, D), f32),
            jax.ShapeDtypeStruct((tokens, D), bf16),
            jax.ShapeDtypeStruct((tokens, ffn_dim), bf16),
            jax.ShapeDtypeStruct((tokens, D), bf16),
            jax.ShapeDtypeStruct((tokens, ffn_dim), bf16),
            jax.ShapeDtypeStruct((tokens, ffn_dim), bf16),
            jax.ShapeDtypeStruct((tokens, D), f32),
            jax.ShapeDtypeStruct((tokens, D), bf16),
            jax.ShapeDtypeStruct((tokens, D), bf16),
            jax.ShapeDtypeStruct((8, D), f32),
        ],
        scratch_shapes=[
            pltpu.VMEM((rows, ffn_dim), f32),
            pltpu.VMEM((rows, ffn_dim), f32),
            pltpu.VMEM((D, ffn_dim), bf16),
            pltpu.VMEM((D, ffn_dim), bf16),
            pltpu.VMEM((ffn_dim, D), bf16),
            pltpu.VMEM((D, D), bf16),
            pltpu.SemaphoreType.DMA((4,)),
        ],
        cost_estimate=pl.CostEstimate(flops=17_000_000_000, bytes_accessed=30_000_000, transcendentals=0),
        name="feed",
    )(place, count, lengths, att, resid, teacher, gain, wide, down_w)


def dot(a, b):
    return jnp.dot(a, b, preferred_element_type=f32)


def per_device(
    byte_ids,
    lengths,
    teacher,
    embed_table,
    conv_weight,
    score_weight,
    attn_gain,
    rel_bias,
    query_weight,
    key_weight,
    value_weight,
    output_weight,
    ffn_gain,
    gate_weight,
    up_weight,
    down_weight,
):
    seqs, own_bytes = byte_ids.shape
    own = own_bytes // 2
    parts = lax.axis_size("seq")
    dp_size = lax.axis_size("dp")
    rank = lax.axis_index("seq")
    total_tokens, total_bytes = own * parts, own_bytes * parts
    shard = score_weight.shape[0]
    rank_ref = rank.reshape(1).astype(jnp.int32)

    tiled = down_weight.shape[0] % 64 == 0
    third = D // 3
    columns, *attn_halves, packed = (pack if tiled else pack_plain)(
        rank_ref, lengths, embed_table, conv_weight,
        (score_weight[None], attn_gain[None], ffn_gain[None]),
        (query_weight, key_weight, value_weight),
        (gate_weight, up_weight, down_weight, output_weight), total_tokens,
    )
    ids_low = jnp.stack([byte_ids // 16, byte_ids % 16]).astype(bf16)
    id_rows = ids_low.reshape(-1, TABLE)
    cut = attn_halves[0].shape[1]
    qkv_halves = [
        RowGather(attn_halves[0], gather_order("y")),
        RowGather(attn_halves[1], gather_order("x")),
    ]
    small = RowGather(columns, axis_bits("dp"))
    while small.order:
        small.start()
        for each in qkv_halves:
            each.finish()
            if len(each.order) > 3:
                each.start()
        small.finish()
    value = small.value.reshape(-1, TABLE)
    mine = jnp.concatenate([value, id_rows], axis=0)
    x_other = swap(mine, "seq", 2)
    pair = jnp.concatenate([mine, x_other], axis=0)
    c_other = swap(pair, "seq", 1)
    wide_rows = mine.shape[0]
    quarters = jnp.concatenate([pair, c_other], axis=0).reshape(parts, wide_rows, TABLE)
    apart = jnp.bitwise_xor(rank, jnp.arange(parts))
    slots = (apart % 2) * 2 + apart // 2
    ordered = jnp.take(quarters, slots, axis=0)
    table = (
        ordered[:, : dp_size * shard]
        .reshape(parts, dp_size, shard, TABLE)
        .transpose(1, 0, 2, 3)
        .reshape(D, TABLE)
    )
    all_ids = ordered[:, dp_size * shard :].reshape(parts, 2, seqs, own_bytes).astype(jnp.int32)
    all_ids = (all_ids[:, 0] * 16 + all_ids[:, 1]).transpose(1, 0, 2).reshape(seqs, total_bytes)
    counts = jnp.sum(table[:, VOCAB + 7 : VOCAB + 9].astype(f32), axis=0)
    live_count = counts[0] * 64.0 + counts[1]
    ffn_gain_full = table[:, VOCAB + 6].astype(f32)

    padded_ids = jnp.pad(all_ids, ((0, 0), (32, 32)), constant_values=-1)
    first_byte = (rank * own_bytes).astype(jnp.int32)
    first_other = (jnp.bitwise_xor(rank, 2) * own_bytes).astype(jnp.int32)

    def phases(start):
        window = lax.dynamic_slice_in_dim(padded_ids, start, own_bytes + 64, 1)
        return window.reshape(seqs, -1, 4).transpose(0, 2, 1).reshape(seqs, -1)

    phase_ids = phases(first_byte)
    other_ids = phases(first_other)

    ffn_dim = gate_weight.shape[1]
    ffn_dim = gate_weight.shape[1]
    wide_full = lax.all_gather(packed, both, axis=0, tiled=True)
    down_full = wide_full[:, 2 * ffn_dim : 3 * ffn_dim]
    if tiled:
        down_full = down_full.reshape(-1, 3, 8, 8, third).transpose(0, 3, 2, 1, 4)
    down_full = down_full.reshape(ffn_dim, D)

    for each in qkv_halves:
        each.start()
    tile, turned_tile, side = prepare(
        after(rank_ref, table), lengths, rel_bias, own, total_tokens, parts
    )
    for each in qkv_halves:
        each.finish(tile)
        each.start()
    residual, normed_own = pool(
        first_byte.reshape(1), phase_ids[:, :, None], table,
        [tile] + [each.value for each in qkv_halves], total_bytes,
    )
    own_other = swap(normed_own, "seq", 1)
    for each in qkv_halves:
        each.finish(normed_own)
        each.start()
    _, normed_x = pool(
        first_other.reshape(1), other_ids[:, :, None], table,
        [normed_own] + [each.value for each in qkv_halves], total_bytes,
    )
    x_side = swap(normed_x, "seq", 1)
    for each in qkv_halves:
        each.finish(normed_x)
    halves = [each.result().reshape(D, cut) for each in qkv_halves]
    qkv_full = jnp.concatenate(halves, axis=1)
    query_full, kv_full = qkv_full[:, :D], qkv_full[:, D:]
    normed = jnp.concatenate([normed_own, normed_x, own_other, x_side], axis=1)
    own_rows = normed_own.reshape(-1, D)
    queries = dot(own_rows, query_full).astype(bf16).reshape(seqs, own, D)
    pairs_kv = dot(normed.reshape(-1, D), kv_full).astype(bf16).reshape(seqs, total_tokens, 2 * D)
    attended, norms = attend(rank_ref, queries, pairs_kv, side, tile, [])

    token_rows = seqs * own
    att = attended.reshape(token_rows, D)
    (
        block_out, ffn_in, hidden, branch_grad, gate_low, up_low, after_grad, after_low,
        attended_grad, feed_stats,
    ) = feed(
        (rank * own).reshape(1), live_count.reshape(1), lengths, att,
        residual, teacher.reshape(token_rows, D), ffn_gain_full[None],
        wide_full, down_full,
    )
    down_grad = jnp.einsum("tf,td->fd", hidden, branch_grad, preferred_element_type=f32)
    gate_grad = jnp.einsum("td,tf->df", ffn_in, gate_low, preferred_element_type=f32)
    up_grad = jnp.einsum("td,tf->df", ffn_in, up_low, preferred_element_type=f32)
    output_grad = jnp.einsum("td,te->de", att, after_low, preferred_element_type=f32).astype(bf16)
    down_grad = down_grad.astype(bf16)
    if tiled:
        down_grad = down_grad.reshape(-1, 8, 8, 3, third).transpose(0, 3, 2, 1, 4)
    wide_grad = jnp.concatenate(
        [
            gate_grad.astype(bf16),
            up_grad.astype(bf16),
            down_grad.reshape(D, ffn_dim),
            output_grad,
        ],
        axis=1,
    )
    wide_sum = lax.psum_scatter(wide_grad, both, scatter_dimension=0, tiled=True)
    turn = after(attended_grad, wide_grad).reshape(seqs, own, D)
    dq, dkv, near_parts, far_parts = attend_back(
        rank_ref, queries, pairs_kv, side, turned_tile, norms, attended, turn
    )
    dq_rows, dkv_rows = dq.reshape(-1, D), dkv.reshape(-1, 2 * D)
    pulled = jnp.einsum("te,de->td", dkv_rows, kv_full, preferred_element_type=f32)
    pulled = pulled.astype(bf16).reshape(seqs, total_tokens, D)
    to_core = pulled[:, 2 * own :]
    from_core = swap(to_core, "seq", 1)
    to_x = [
        (pulled[s, own : 2 * own].astype(f32) + from_core[s, own:].astype(f32)).astype(bf16)
        for s in range(seqs)
    ]
    from_x = [swap(rows, "seq", 2) for rows in to_x]
    normed_rows = normed.reshape(-1, D)
    kv_grad = jnp.einsum(
        "td,te->de", normed_rows, after(dkv_rows, *to_x), preferred_element_type=f32
    ).astype(bf16)
    query_grad = jnp.einsum(
        "td,te->de", own_rows, dq_rows, preferred_element_type=f32
    ).astype(bf16)
    attn_sum = RowSum(jnp.concatenate([query_grad, kv_grad], axis=1)[None], sum_order("y"))
    attn_sum.start()
    attn_sum.finish()
    attn_sum.start()
    bias_rows = bias_sums(rank_ref, near_parts, far_parts, parts, [attn_sum.sent])
    shared = SumEverywhere(
        jnp.where(
            (jnp.arange(16) < HEADS)[:, None],
            bias_rows,
            jnp.broadcast_to(jnp.sum(feed_stats[1]), (16, 128)),
        )
    )
    shared.start()
    sums, deps = (), [bias_rows]
    for s in range(seqs):
        sums = pool_back(
            s, first_byte.reshape(1), phase_ids[:, :, None], phase_ids[:, None, :], table,
            pulled, from_core, from_x[s], dq, halves[0], residual,
            after_grad.reshape(seqs, own, D), feed_stats, sums, deps, total_bytes,
        )
        if s < seqs - 1:
            shared.finish(sums[1])
            shared.start()
            deps = [shared.value]
        if s < seqs - 1:
            attn_sum.finish(sums[1])
            attn_sum.start()
            deps.append(attn_sum.sent)
    shared.finish(sums)
    shared.start()
    front_sum = RowSum(sums[None], sum_order("x"))
    while front_sum.order:
        front_sum.start()
        for each in (attn_sum, shared):
            each.finish()
            each.start()
        front_sum.finish()
    front_sum = front_sum.result().reshape(shard, TABLE).T
    every = shared.result()
    bias_grad = every[:HEADS, :BUCKETS].T
    attn_sum = attn_sum.result()[0]
    kv_sum = attn_sum[:, D : 3 * D].reshape(shard, PAIRS, 2, SIDE)
    if tiled:
        gate_sum, up_sum, down_sum, output_sum = unpack(wide_sum, ffn_dim, down_weight.shape[0])
    else:
        wide_sum = wide_sum.astype(f32)
        gate_sum, up_sum = wide_sum[:, :ffn_dim], wide_sum[:, ffn_dim : 2 * ffn_dim]
        down_sum = wide_sum[:, 2 * ffn_dim : 3 * ffn_dim].reshape(-1, D)
        output_sum = wide_sum[:, 3 * ffn_dim :]

    return (
        block_out.reshape(seqs, own, D),
        every[HEADS, 0] / live_count,
        front_sum[:VOCAB],
        front_sum[VOCAB : VOCAB + 4],
        front_sum[VOCAB + 4],
        front_sum[VOCAB + 5],
        bias_grad,
        attn_sum[:, :D],
        kv_sum[:, :, 0].reshape(shard, D),
        kv_sum[:, :, 1].reshape(shard, D),
        output_sum,
        front_sum[VOCAB + 6],
        gate_sum,
        up_sum,
        down_sum,
    )


def solution(mesh):
    tokens = P("dp", "seq", None)
    features = P(("dp", "seq"))
    columns = P(None, ("dp", "seq"))
    rows = P(("dp", "seq"), None)
    in_specs = (
        P("dp", "seq"), P("dp"), tokens, columns, columns, features, features, P(),
        rows, rows, rows, rows, features, rows, rows, rows,
    )
    out_specs = (
        tokens, P(), columns, columns, features, features, P(), rows, rows, rows, rows,
        features, rows, rows, rows,
    )
    return jax.shard_map(
        per_device, mesh=mesh, in_specs=in_specs, out_specs=out_specs, check_vma=False
    )
```
